32 devices in a mesh: row: 8 (over z, x), col: 4 (over y, core).
Axes of the slice: x: 2, y: 2, z: 4, core: 2. Of those that a mesh axis runs over, the one named last changes fastest.
Arguments:
- tokens: bfloat16 [1024, 87040], P('col', 'row'), may hold values from -6 to 6
- condition: bfloat16 [128, 1024], P('row', 'col'), may hold values from -6 to 6
- scale_ids: int32 [128, 680], P('row'), may hold values from 0 to 9, never falling along the last dimension, each value on 1 to 256 neighbouring positions
- attention_triple_matrix: bfloat16 [1024, 3, 1024], P('row', None, 'col'), may hold values from -0.1875 to 0.1875
- attention_triple_offset: bfloat16 [3, 1024], P(None, 'col'), may hold values from -1.75 to 1.75
- qk_gain: float32 [16], P('col'), may hold values from 8 to 20
- w_proj: bfloat16 [1024, 1024], P('row', 'col'), may hold values from -0.75 to 0.75
- b_proj: bfloat16 [1024], P('col'), may hold values from -1.75 to 1.75
- w_fc1: bfloat16 [1024, 4096], P('row', 'col'), may hold values from -0.1875 to 0.1875
- b_fc1: bfloat16 [4096], P('col'), may hold values from -1.75 to 1.75
- w_fc2: bfloat16 [4096, 1024], P('col', 'row'), may hold values from -0.09375 to 0.09375
- b_fc2: bfloat16 [1024], P('col'), may hold values from -1.75 to 1.75
- w_ada: bfloat16 [6, 1024, 1024], P(None, 'row', 'col'), may hold values from -0.1875 to 0.1875
- b_ada: bfloat16 [6, 1024], P(None, 'col'), may hold values from -3 to 3
- out_grad: bfloat16 [1024, 87040], P('col', 'row'), may hold values from -6 to 6
Outputs:
- layer_out: bfloat16 [1024, 87040], P('col', 'row')
- grad_tokens: bfloat16 [1024, 87040], P('col', 'row')
- grad_condition: bfloat16 [128, 1024], P('row', 'col')
- grad_w_qkv: float32 [1024, 3, 1024], P('row', None, 'col')
- grad_b_qkv: float32 [3, 1024], P(None, 'col')
- grad_qk_gain: float32 [16], P('col')
- grad_w_proj: float32 [1024, 1024], P('row', 'col')
- grad_b_proj: float32 [1024], P('col')
- grad_w_fc1: float32 [1024, 4096], P('row', 'col')
- grad_b_fc1: float32 [4096], P('col')
- grad_w_fc2: float32 [4096, 1024], P('col', 'row')
- grad_b_fc2: float32 [1024], P('col')
- grad_w_ada: float32 [6, 1024, 1024], P(None, 'row', 'col')
- grad_b_ada: float32 [6, 1024], P(None, 'col')
The draws below stay inside these ranges and needn't reach their ends.
Inputs may be any that keep to these rules, and one draw needn't show every extreme that they name: Along each image's 680 tokens scale_ids never falls and takes every value from 0 to 9; one scale of each image has exactly 256 tokens and none has more.
All inputs are finite; a program needn't handle non-finite values.
Results may differ from the reference program's by a relative error of at most 0.018.
The reference program's roundings to bfloat16 on the way count: a program that leaves them out, or rounds other values in their place, can miss the bound.
Values may be sent and summed in bfloat16 or wider, within the bound.
A program may use at most 768 MiB of HBM per device.

```python
import math
import jax
import jax.numpy as jnp
import numpy as np
from jax import lax

D = 1024
HEADS = 16
HEAD_DIM = 64
FF = 4096
COND = 1024
LENGTH = 680
SCALES = 10
MOST = 256
IMG_MB = 4
IMAGES = 128
TOKENS = 87040


def steps_of(rng, shape, cuts, low, high):
    def one(position, parts):
        heights = jax.random.uniform(jax.random.fold_in(jax.random.fold_in(rng, 6), position), (parts,), jnp.float32, low / len(cuts), high / len(cuts))
        return jnp.repeat(jnp.exp(heights), shape[position] // parts).reshape((-1,) + (1,) * (len(shape) - position - 1))

    factor_of = one(*cuts[0])
    for cut in cuts[1:]:
        factor_of = factor_of * one(*cut)
    return factor_of


def split_up(amount, total, most, lean):
    loads = [(1 << 20) // math.isqrt(standing ** lean) + 1 for standing in range(2, amount + 1)]
    spare, counts = total - most - (amount - 1), [1] * (amount - 1)
    while spare > 0:
        candidates = [i for i in range(amount - 1) if counts[i] < most]
        mass, remaining = sum([loads[i] for i in candidates]), spare
        for i in candidates:
            extra = min(most - counts[i], max(1, remaining * loads[i] // mass), spare)
            counts[i] = counts[i] + extra
            spare = spare - extra
    return np.array([most] + counts)


def ragged_sizes(own_key, number_of, total, most, lean):
    if number_of == 2:
        one = jax.random.randint(own_key, (), max(1, total - most), min(most, total - 1) + 1)
        return jnp.stack([one, total - one])
    sizes = jnp.asarray(split_up(number_of, total, most, lean), jnp.int32)
    pairs = (number_of - 1) // 2
    donor, sink = sizes[1:1 + 2 * pairs:2], sizes[2:2 + 2 * pairs:2]
    slack = jnp.minimum(donor - 1, most - sink)
    passed = jax.random.randint(jax.random.fold_in(own_key, 1), (pairs,), 0, 1 << 20) % (slack + 1)
    sizes = sizes.at[1:1 + 2 * pairs:2].set(donor - passed).at[2:2 + 2 * pairs:2].set(sink + passed)
    return sizes[jax.random.permutation(jax.random.fold_in(own_key, 2), number_of)]


def normal_values(key, shape, scale, reach, pieces=(), held_as=jnp.bfloat16):
    values = scale * jax.random.normal(key, shape, jnp.float32)
    if pieces:
        values = values * steps_of(key, shape, pieces, -0.22, 0.18)
    return jnp.clip(values, -reach, reach).astype(held_as)


def setup_inputs(seed: int = 0) -> dict:
    arg_keys = jax.random.split(jax.random.key(seed), 16)
    return {
        "tokens": normal_values(arg_keys[0], (D, TOKENS), 1.0, 6.0, ((0, 4), (1, 8))),
        "condition": normal_values(arg_keys[1], (IMAGES, COND), 1.0, 6.0, ((0, 8), (1, 4))),
        "scale_ids": jax.vmap(lambda own: jnp.searchsorted(jnp.cumsum(ragged_sizes(own, SCALES, LENGTH, MOST, 1)), jnp.arange(LENGTH), side="right"))(jax.random.split(arg_keys[2], IMAGES)).reshape((IMAGES, LENGTH)).astype(jnp.int32),
        "attention_triple_matrix": normal_values(arg_keys[3], (D, 3, D), D ** -0.5, 0.1875, ((0, 8), (2, 4))),
        "attention_triple_offset": normal_values(arg_keys[4], (3, D), 0.3, 1.75, ((1, 4),)),
        "qk_gain": jnp.clip(8.0 + 12.0 * jax.random.uniform(arg_keys[5], (HEADS,), jnp.float32) ** steps_of(arg_keys[5], (HEADS,), ((0, 4),), -0.2, 0.2), 8.0, 20.0),
        "w_proj": normal_values(arg_keys[6], (D, D), (D // 16) ** -0.5, 0.75, ((0, 8), (1, 4))),
        "b_proj": normal_values(arg_keys[7], (D,), 0.3, 1.75, ((0, 4),)),
        "w_fc1": normal_values(arg_keys[8], (D, FF), D ** -0.5, 0.1875, ((0, 8), (1, 4))),
        "b_fc1": normal_values(arg_keys[9], (FF,), 0.3, 1.75, ((0, 4),)),
        "w_fc2": normal_values(arg_keys[10], (FF, D), FF ** -0.5, 0.09375, ((0, 4), (1, 8))),
        "b_fc2": normal_values(arg_keys[11], (D,), 0.3, 1.75, ((0, 4),)),
        "w_ada": normal_values(arg_keys[12], (6, COND, D), COND ** -0.5, 0.1875, ((1, 8), (2, 4))),
        "b_ada": normal_values(arg_keys[13], (6, D), 0.5, 3.0, ((1, 4),)),
        "out_grad": normal_values(arg_keys[14], (D, TOKENS), 1.0, 6.0, ((0, 4), (1, 8))),
    }


exact_arithmetic_mode = lax.Precision.HIGHEST

@jax.custom_vjp
def low(v):
    return lax.optimization_barrier(v.astype(jnp.bfloat16)).astype(jnp.float32)

@jax.custom_vjp
def reduced_reverse_pass(v):
    return v

def low_keep(v):
    return (low(v), None)

def low_pass(kept, grad):
    return (grad,)

def back_keep(v):
    return (v, None)

def back_low(kept, grad):
    return (low(grad),)
low.defvjp(low_keep, low_pass)
reduced_reverse_pass.defvjp(back_keep, back_low)

def layer_norm(vector):
    centered = vector - lax.optimization_barrier(jnp.mean(vector, axis=-1, keepdims=True))
    return centered * lax.rsqrt(lax.optimization_barrier(jnp.mean(centered * centered, axis=-1, keepdims=True)) + 1e-06)

def layer(tokens, condition, scale_rows, attention_triple_matrix, attention_triple_offset, qk_gain, w_proj, b_proj, w_fc1, b_fc1, w_fc2, b_fc2, w_ada, b_ada):
    images = condition.shape[0]
    soft_cond = low(jax.nn.silu(condition))
    modulation = reduced_reverse_pass(jnp.einsum('ic,scd->isd', soft_cond, w_ada, precision=exact_arithmetic_mode) + b_ada[None])
    per_token = jnp.repeat(modulation, LENGTH, axis=0)
    shift_attn = per_token[:, 0]
    scale_attn = per_token[:, 1]
    gate_attn = per_token[:, 2]
    shift_ffn = per_token[:, 3]
    scale_ffn = per_token[:, 4]
    gate_ffn = per_token[:, 5]
    initial_standardize = low(layer_norm(tokens) * (1.0 + scale_attn) + shift_attn)
    attention_triple = reduced_reverse_pass(jnp.einsum('zp,pxh->zxh', initial_standardize, attention_triple_matrix, precision=exact_arithmetic_mode) + attention_triple_offset[None])
    head_shape = (images, LENGTH, HEADS, HEAD_DIM)
    queries = attention_triple[:, 0].reshape(head_shape)
    keys_raw = attention_triple[:, 1].reshape(head_shape)
    values_raw = attention_triple[:, 2].reshape(head_shape)
    queries_unit = queries * lax.rsqrt(lax.optimization_barrier(jnp.sum(queries * queries, axis=-1, keepdims=True)) + 1e-06)
    keys_unit = keys_raw * lax.rsqrt(lax.optimization_barrier(jnp.sum(keys_raw * keys_raw, axis=-1, keepdims=True)) + 1e-06)
    queries_low = low(queries_unit * qk_gain[None, None, :, None])
    keys_low = low(keys_unit)
    values_low = low(values_raw)
    scores = reduced_reverse_pass(jnp.einsum('bqhd,bkhd->bhqk', queries_low, keys_low, precision=exact_arithmetic_mode))
    allowed = scale_rows[:, None, :] <= scale_rows[:, :, None]
    attn_prob = jax.nn.softmax(jnp.where(allowed[:, None], scores, -1e+30), axis=-1)
    attended = jnp.einsum('bhqk,bkhd->bqhd', low(attn_prob), values_low, precision=exact_arithmetic_mode).reshape(tokens.shape)
    attended = reduced_reverse_pass(low(attended))
    branch_one = reduced_reverse_pass(jnp.dot(attended, w_proj, precision=exact_arithmetic_mode) + b_proj)
    residual = tokens + gate_attn * branch_one
    ln_two = low(layer_norm(residual) * (1.0 + scale_ffn) + shift_ffn)
    pre_act = reduced_reverse_pass(jnp.dot(ln_two, w_fc1, precision=exact_arithmetic_mode) + b_fc1)
    hidden = low(jax.nn.gelu(pre_act, approximate=True))
    branch_two = reduced_reverse_pass(jnp.dot(hidden, w_fc2, precision=exact_arithmetic_mode) + b_fc2)
    return residual + gate_ffn * branch_two

def reference(tokens, condition, scale_ids, attention_triple_matrix, attention_triple_offset, qk_gain, w_proj, b_proj, w_fc1, b_fc1, w_fc2, b_fc2, w_ada, b_ada, out_grad):
    parameters = (attention_triple_matrix.astype(jnp.float32), attention_triple_offset.astype(jnp.float32), qk_gain.astype(jnp.float32), w_proj.astype(jnp.float32), b_proj.astype(jnp.float32), w_fc1.astype(jnp.float32), b_fc1.astype(jnp.float32), w_fc2.astype(jnp.float32), b_fc2.astype(jnp.float32), w_ada.astype(jnp.float32), b_ada.astype(jnp.float32))
    groups = IMAGES // IMG_MB
    block_rows = IMG_MB * LENGTH
    inputs = (tokens.astype(jnp.float32).T.reshape(groups, block_rows, D), condition.astype(jnp.float32).reshape(groups, IMG_MB, COND), scale_ids.reshape(groups, IMG_MB, LENGTH), out_grad.astype(jnp.float32).T.reshape(groups, block_rows, D))

    def group_step(running, block_item):
        tok_block, cond_block, scale_block, grad_block = block_item

        def local_layer(tok_in, cond_in, *weights):
            return layer(tok_in, cond_in, scale_block, *weights)
        result, pullback = jax.vjp(local_layer, tok_block, cond_block, *parameters)
        gradients = pullback(grad_block)
        running = tuple((earlier + addend for earlier, addend in zip(running, gradients[2:])))
        return (running, (result.astype(jnp.bfloat16), gradients[0].astype(jnp.bfloat16), gradients[1].astype(jnp.bfloat16)))
    starting = tuple((jnp.zeros_like(weight) for weight in parameters))
    totals, (outputs, d_tokens, d_cond) = lax.scan(group_step, starting, inputs)
    return (outputs.reshape(TOKENS, D).T, d_tokens.reshape(TOKENS, D).T, d_cond.reshape(IMAGES, COND), totals[0], totals[1], totals[2], totals[3], totals[4], totals[5], totals[6], totals[7], totals[8], totals[9], totals[10])
```

```python
import functools
import jax
import jax.numpy as jnp
from jax import lax
from jax.sharding import PartitionSpec as P
from jax.experimental import pallas as pl
from jax.experimental.pallas import tpu as pltpu

HEAD_DIM = 64
PAIR = 2 * HEAD_DIM
NEG = -1024.0
FIRST_EXTRA = 16


def head_sums(values, left):
    first = jnp.sum(jnp.where(left, values, 0.0), axis=-1, keepdims=True)
    second = jnp.sum(jnp.where(left, 0.0, values), axis=-1, keepdims=True)
    return first, second


def unit_of(raw, left):
    first, second = head_sums(raw * raw, left)
    inverse = jnp.where(left, lax.rsqrt(first + 1e-06), lax.rsqrt(second + 1e-06))
    return raw * inverse, inverse


def nt(left_rows, right_rows):
    return lax.dot_general(
        left_rows, right_rows, (((1,), (1,)), ((), ())), preferred_element_type=jnp.float32
    )


def nn(left_rows, right_rows):
    return jnp.dot(left_rows, right_rows, preferred_element_type=jnp.float32)


def split_three(value):
    high = value.astype(jnp.bfloat16)
    rest = value - high.astype(jnp.float32)
    middle = rest.astype(jnp.bfloat16)
    lowest = (rest - middle.astype(jnp.float32)).astype(jnp.bfloat16)
    return high, middle, lowest


def forward_kernel(q_ref, k_ref, v_ref, gain_ref, qm_ref, km_ref, o_ref, lse_ref):
    lane = lax.broadcasted_iota(jnp.int32, q_ref.shape[-2:], 1)
    left = lane < HEAD_DIM
    q_unit, _ = unit_of(q_ref[0, 0], left)
    k_unit, _ = unit_of(k_ref[0, 0], left)
    q_low = (q_unit * gain_ref[...]).astype(jnp.bfloat16)
    k_low = k_unit.astype(jnp.bfloat16)
    v_low = v_ref[0, 0].astype(jnp.bfloat16)
    qm = qm_ref[0]
    km = km_ref[0]
    one = jnp.ones_like(v_low)
    results = []
    for head in range(2):
        mine = left if head == 0 else ~left
        scores = nt(jnp.where(mine, q_low, qm), jnp.where(mine, k_low, km))
        weights = jnp.exp(scores).astype(jnp.bfloat16)
        results.append(nn(weights, jnp.where(mine, v_low, one)))
    totals = jnp.where(left, results[1], results[0])
    lse_ref[0] = jnp.log(totals)
    swapped = pltpu.roll(totals, HEAD_DIM, 1)
    o_ref[0] = (jnp.where(left, results[0], results[1]) / swapped).astype(jnp.bfloat16)


def backward_kernel(
    q_ref, k_ref, v_ref, gain_ref, qm_ref, km_ref, o_ref, lse_ref, do_ref, d_ref, sums_ref
):
    shape = q_ref.shape[-2:]
    lane = lax.broadcasted_iota(jnp.int32, shape, 1)
    left = lane < HEAD_DIM
    spot = lane % HEAD_DIM
    gain = gain_ref[...]
    q_unit, q_inv = unit_of(q_ref[0, 0], left)
    k_unit, k_inv = unit_of(k_ref[0, 0], left)
    q_low = (q_unit * gain).astype(jnp.bfloat16)
    k_low = k_unit.astype(jnp.bfloat16)
    v_low = v_ref[0, 0].astype(jnp.bfloat16)
    d_out = do_ref[0]
    km = km_ref[0]

    def place(base, value):
        high, middle, lowest = split_three(value)
        base = jnp.where(spot == FIRST_EXTRA, high, base)
        base = jnp.where(spot == FIRST_EXTRA + 1, middle, base)
        return jnp.where(spot == FIRST_EXTRA + 2, lowest, base)

    qm = place(qm_ref[0], -lse_ref[0])
    product = d_out.astype(jnp.float32) * o_ref[0].astype(jnp.float32)
    first, second = head_sums(product, left)
    dm = place(jnp.zeros_like(d_out), -jnp.where(left, second, first))
    k_turned = k_low.astype(jnp.float32).T.astype(jnp.bfloat16)
    d_v, d_k, d_q = [], [], []
    for head in range(2):
        mine = left if head == 0 else ~left
        probs = jnp.exp(nt(jnp.where(mine, k_low, km), jnp.where(mine, q_low, qm)))
        d_v.append(nn(probs.astype(jnp.bfloat16), d_out))
        shifted = nt(jnp.where(mine, v_low, km), jnp.where(mine, d_out, dm))
        d_scores = (probs * shifted).astype(jnp.bfloat16)
        d_k.append(nn(d_scores, q_low))
        d_q.append(nn(k_turned[head * HEAD_DIM : (head + 1) * HEAD_DIM], d_scores))
    d_q_low = jnp.concatenate(d_q, axis=0).T
    d_k_low = jnp.where(left, d_k[0], d_k[1])
    d_values = jnp.where(left, d_v[0], d_v[1])
    turned = d_q_low * gain
    first, second = head_sums(turned * q_unit, left)
    d_queries = q_inv * (turned - q_unit * jnp.where(left, first, second))
    first, second = head_sums(d_k_low * k_unit, left)
    d_keys = k_inv * (d_k_low - k_unit * jnp.where(left, first, second))
    parts = []
    for index, value in enumerate((d_queries, d_keys, d_values)):
        rounded = value.astype(jnp.bfloat16)
        d_ref[index, 0] = rounded
        parts.append(jnp.sum(rounded.astype(jnp.float32), axis=0, keepdims=True))
    parts.append(jnp.sum(d_q_low * q_unit, axis=0, keepdims=True))
    parts.append(jnp.zeros((4, PAIR), jnp.float32))
    sums_ref[0] = jnp.concatenate(parts, axis=0)


def mask_lanes(ids):
    spot = jnp.arange(PAIR, dtype=jnp.int32) % HEAD_DIM
    rows = ids[:, :, None]
    queries = (rows == spot).astype(jnp.bfloat16)
    keys = jnp.where((rows > spot) & (spot < FIRST_EXTRA), NEG, 0.0)
    extra = (spot >= FIRST_EXTRA) & (spot < FIRST_EXTRA + 3)
    return queries, jnp.where(extra, 1.0, keys).astype(jnp.bfloat16)


def specs(length):
    def raw(which):
        return pl.BlockSpec((1, 1, length, PAIR), lambda b, h: (which, b, 0, h))

    gain = pl.BlockSpec((1, PAIR), lambda b, h: (0, h))
    lanes = pl.BlockSpec((1, length, PAIR), lambda b, h: (b, 0, 0))
    tokens = pl.BlockSpec((1, length, PAIR), lambda b, h: (b, 0, h))
    return [raw(0), raw(1), raw(2), gain, lanes, lanes], tokens


def attention_forward(qkv, gain_row, qm, km):
    _, images, length, width = qkv.shape
    ins, tokens = specs(length)
    return pl.pallas_call(
        forward_kernel,
        grid=(images, width // PAIR),
        in_specs=ins,
        out_specs=[tokens, tokens],
        out_shape=[
            jax.ShapeDtypeStruct((images, length, width), jnp.bfloat16),
            jax.ShapeDtypeStruct((images, length, width), jnp.float32),
        ],
        compiler_params=pltpu.CompilerParams(vmem_limit_bytes=48 << 20),
        cost_estimate=pl.CostEstimate(
            flops=4 * images * length * length * width * 2, bytes_accessed=images * length * width * 18, transcendentals=images * length * length * 16
        ),
        name="attention_forward",
    )(qkv, qkv, qkv, gain_row, qm, km)


def attention_backward(qkv, gain_row, qm, km, out, lse, d_out):
    _, images, length, width = qkv.shape
    ins, tokens = specs(length)
    return pl.pallas_call(
        backward_kernel,
        grid=(images, width // PAIR),
        in_specs=ins + [tokens, tokens, tokens],
        out_specs=[
            pl.BlockSpec((3, 1, length, PAIR), lambda b, h: (0, b, 0, h)),
            pl.BlockSpec((1, 8, PAIR), lambda b, h: (b, 0, h)),
        ],
        out_shape=[
            jax.ShapeDtypeStruct((3, images, length, width), jnp.bfloat16),
            jax.ShapeDtypeStruct((images, 8, width), jnp.float32),
        ],
        compiler_params=pltpu.CompilerParams(vmem_limit_bytes=56 << 20),
        cost_estimate=pl.CostEstimate(
            flops=10 * images * length * length * width * 2, bytes_accessed=images * length * width * 30, transcendentals=images * length * length * 16
        ),
        name="attention_backward",
    )(qkv, qkv, qkv, gain_row, qm, km, out, lse, d_out)


GELU_RATE = 0.7978845608
GELU_CUBE = 0.7978845608 * 0.044715
FFN_CHUNK = 512


def tile_of(count, want):
    best = 8
    for size in range(8, want + 1, 8):
        if count % size == 0:
            best = size
    return best


def side_by_side(ref):
    return jnp.concatenate([ref[index] for index in range(ref.shape[0])], axis=1)


class Images:
    def __init__(self, rows, length, images):
        start = pl.program_id(0) * rows
        self.first = start // length
        self.second = jnp.minimum((start + rows - 1) // length, images - 1)
        index = lax.broadcasted_iota(jnp.int32, (rows, 1), 0) + start
        self.early = index < (self.first + 1) * length

    def pick(self, table, which):
        return jnp.where(
            self.early,
            table[self.first, which : which + 1],
            table[self.second, which : which + 1],
        )

    def add(self, sums, which, value):
        early = jnp.sum(jnp.where(self.early, value, 0.0), axis=0, keepdims=True)
        late = jnp.sum(jnp.where(self.early, 0.0, value), axis=0, keepdims=True)
        sums[self.first, which : which + 1] += early
        sums[self.second, which : which + 1] += late


def standard_rows(value):
    centered = value - jnp.mean(value, axis=-1, keepdims=True)
    inv_std = lax.rsqrt(jnp.mean(centered * centered, axis=-1, keepdims=True) + 1e-06)
    return centered * inv_std, inv_std


def norm_back(incoming, normed, inv_std):
    average = jnp.mean(incoming, axis=-1, keepdims=True)
    cross = jnp.mean(incoming * normed, axis=-1, keepdims=True)
    return inv_std * (incoming - average - normed * cross)


def block_copies(parts, start, target, sem, row_blocks, col_blocks):
    height = target.shape[0] // row_blocks
    span = target.shape[1] // col_blocks
    for r in range(row_blocks):
        for c in range(col_blocks):
            pltpu.make_async_copy(
                parts.at[r * col_blocks + c, :, pl.ds(start, span)],
                target.at[pl.ds(r * height, height), pl.ds(c * span, span)],
                sem,
            ).start()


def wait_all(target, sem):
    pltpu.make_async_copy(target, target, sem).wait()


def ffn_kernel(
    blocks, length, images,
    x_ref, att_ref, g_ref, mod_ref, bias_proj_ref, bias_one_ref, bias_two_ref, parts_ref,
    out_ref, ln_ref, hidden_ref, d_two_ref, d_pre_ref, d_one_ref, d_res_ref, d_att_ref,
    sums_ref, sum_proj_ref, sum_one_ref, sum_two_ref,
    w_proj, w_one, w_two, slope, sems,
):
    rows = att_ref.shape[0]
    ff = w_one.shape[1]
    first_step = pl.program_id(0) == 0

    @pl.when(first_step)
    def _():
        part = w_proj.shape[1] // blocks[1]
        ff_part = ff // blocks[1]
        block_copies(parts_ref, 0, w_proj, sems.at[0], *blocks)
        block_copies(parts_ref, part, w_one, sems.at[1], *blocks)
        block_copies(parts_ref, part + ff_part, w_two, sems.at[2], *blocks)
        sums_ref[...] = jnp.zeros_like(sums_ref)
        sum_proj_ref[...] = jnp.zeros_like(sum_proj_ref)
        sum_one_ref[...] = jnp.zeros_like(sum_one_ref)
        sum_two_ref[...] = jnp.zeros_like(sum_two_ref)
        wait_all(w_proj, sems.at[0])
        wait_all(w_one, sems.at[1])
        wait_all(w_two, sems.at[2])

    here = Images(rows, length, images)
    gate_attn = here.pick(mod_ref, 2)
    branch_one = nn(att_ref[...], w_proj[...]) + bias_proj_ref[...]
    residual = side_by_side(x_ref).astype(jnp.float32) + gate_attn * branch_one
    normed, inv_std = standard_rows(residual)
    scale = 1.0 + here.pick(mod_ref, 4)
    ln_two = (normed * scale + here.pick(mod_ref, 3)).astype(jnp.bfloat16)
    ln_ref[...] = ln_two
    branch_two = jnp.broadcast_to(bias_two_ref[...], residual.shape)
    for start in range(0, ff, FFN_CHUNK):
        span = slice(start, start + FFN_CHUNK)
        pre = nn(ln_two, w_one[:, span]) + bias_one_ref[:, span]
        square = pre * pre
        turn = jnp.tanh(pre * (GELU_RATE + GELU_CUBE * square))
        half = 0.5 + 0.5 * turn
        value = pre * half
        slope[:, span] = half + value * (1.0 - turn) * (GELU_RATE + 3.0 * GELU_CUBE * square)
        low = value.astype(jnp.bfloat16)
        hidden_ref[:, span] = low
        branch_two += nt(low, w_two[:, span])
    gate_ffn = here.pick(mod_ref, 5)
    result = (residual + gate_ffn * branch_two).astype(jnp.bfloat16)
    part = out_ref.shape[2]
    for index in range(out_ref.shape[0]):
        out_ref[index] = result[:, index * part : (index + 1) * part]
    incoming = side_by_side(g_ref).astype(jnp.float32)
    here.add(sums_ref, 3, incoming * branch_two)
    d_two = (gate_ffn * incoming).astype(jnp.bfloat16)
    d_two_ref[...] = d_two
    sum_two_ref[...] += jnp.sum(d_two.astype(jnp.float32), axis=0, keepdims=True)
    d_back = jnp.zeros_like(residual)
    for start in range(0, ff, FFN_CHUNK):
        span = slice(start, start + FFN_CHUNK)
        d_pre = (nn(d_two, w_two[:, span]) * slope[:, span]).astype(jnp.bfloat16)
        d_pre_ref[:, span] = d_pre
        sum_one_ref[:, span] += jnp.sum(d_pre.astype(jnp.float32), axis=0, keepdims=True)
        d_back += nt(d_pre, w_one[:, span])
    here.add(sums_ref, 1, d_back)
    here.add(sums_ref, 2, d_back * normed)
    d_res = incoming + norm_back(d_back * scale, normed, inv_std)
    d_res_ref[...] = d_res
    here.add(sums_ref, 0, d_res * branch_one)
    d_one = (gate_attn * d_res).astype(jnp.bfloat16)
    d_one_ref[...] = d_one
    sum_proj_ref[...] += jnp.sum(d_one.astype(jnp.float32), axis=0, keepdims=True)
    d_att_ref[...] = nt(d_one, w_proj[...]).astype(jnp.bfloat16)


def ffn(x, attended, g, modulation, bias_proj, bias_one, bias_two, parts, blocks, length):
    groups, count, part = x.shape
    width = groups * part
    ff = bias_one.shape[1]
    images = modulation.shape[0]
    rows = tile_of(count, 272)
    f32, bf16 = jnp.float32, jnp.bfloat16
    pieces = pl.BlockSpec((groups, rows, part), lambda i: (0, i, 0))
    wide = pl.BlockSpec((rows, width), lambda i: (i, 0))
    tall = pl.BlockSpec((rows, ff), lambda i: (i, 0))

    def fixed(*shape):
        return pl.BlockSpec(shape, lambda i: (0,) * len(shape))

    def made(shape, dtype):
        return jax.ShapeDtypeStruct(shape, dtype)

    return pl.pallas_call(
        functools.partial(ffn_kernel, blocks, length, images),
        grid=(count // rows,),
        in_specs=[
            pieces, wide, pieces, fixed(images, 6, width), fixed(1, width), fixed(1, ff),
            fixed(1, width), pl.BlockSpec(memory_space=pl.ANY),
        ],
        out_specs=[
            pieces, wide, tall, wide, tall, wide, wide, wide,
            fixed(images, 4, width), fixed(1, width), fixed(1, ff), fixed(1, width),
        ],
        out_shape=[
            made((groups, count, part), bf16), made((count, width), bf16),
            made((count, ff), bf16), made((count, width), bf16), made((count, ff), bf16),
            made((count, width), bf16), made((count, width), f32), made((count, width), bf16),
            made((images, 4, width), f32), made((1, width), f32), made((1, ff), f32),
            made((1, width), f32),
        ],
        scratch_shapes=[
            pltpu.VMEM((width, width), bf16), pltpu.VMEM((width, ff), bf16),
            pltpu.VMEM((width, ff), bf16), pltpu.VMEM((rows, ff), f32),
            pltpu.SemaphoreType.DMA((3,)),
        ],
        compiler_params=pltpu.CompilerParams(vmem_limit_bytes=62 << 20),
        cost_estimate=pl.CostEstimate(
            flops=4 * count * width * (2 * ff + width),
            bytes_accessed=count * width * 20 + count * ff * 4 + width * (2 * ff + width) * 2,
            transcendentals=count * ff,
        ),
        name="ffn_both",
    )(x, attended, g, modulation, bias_proj, bias_one, bias_two, parts)


def cube_copies(parts, target, sem, row_blocks, col_blocks):
    height = target.shape[1] // row_blocks
    span = target.shape[2] // col_blocks
    for r in range(row_blocks):
        for c in range(col_blocks):
            pltpu.make_async_copy(
                parts.at[r * col_blocks + c],
                target.at[:, pl.ds(r * height, height), pl.ds(c * span, span)],
                sem,
            ).start()


def qkv_kernel(blocks, length, images, x_ref, mod_ref, bias_ref, parts_ref, ln_ref, qkv_ref, weights, sem):
    @pl.when(pl.program_id(0) == 0)
    def _():
        cube_copies(parts_ref, weights, sem.at[0], *blocks)
        wait_all(weights, sem.at[0])

    here = Images(ln_ref.shape[0], length, images)
    normed, _ = standard_rows(side_by_side(x_ref).astype(jnp.float32))
    ln_one = (normed * (1.0 + here.pick(mod_ref, 1)) + here.pick(mod_ref, 0)).astype(jnp.bfloat16)
    ln_ref[...] = ln_one
    for index in range(3):
        qkv_ref[index] = nn(ln_one, weights[index]) + bias_ref[index]


def qkv_forward(x, modulation, bias, parts, blocks, length):
    groups, count, part = x.shape
    width = groups * part
    images = modulation.shape[0]
    rows = tile_of(count, 544)
    return pl.pallas_call(
        functools.partial(qkv_kernel, blocks, length, images),
        grid=(count // rows,),
        in_specs=[
            pl.BlockSpec((groups, rows, part), lambda i: (0, i, 0)),
            pl.BlockSpec((images, 6, width), lambda i: (0, 0, 0)),
            pl.BlockSpec((3, 1, width), lambda i: (0, 0, 0)),
            pl.BlockSpec(memory_space=pl.ANY),
        ],
        out_specs=[
            pl.BlockSpec((rows, width), lambda i: (i, 0)),
            pl.BlockSpec((3, rows, width), lambda i: (0, i, 0)),
        ],
        out_shape=[
            jax.ShapeDtypeStruct((count, width), jnp.bfloat16),
            jax.ShapeDtypeStruct((3, count, width), jnp.float32),
        ],
        scratch_shapes=[
            pltpu.VMEM((3, width, width), jnp.bfloat16),
            pltpu.SemaphoreType.DMA((1,)),
        ],
        compiler_params=pltpu.CompilerParams(vmem_limit_bytes=48 << 20),
        cost_estimate=pl.CostEstimate(
            flops=6 * count * width * width,
            bytes_accessed=count * width * 16 + 6 * width * width,
            transcendentals=count,
        ),
        name="qkv_forward",
    )(x, modulation, bias, parts)


def input_kernel(
    blocks, length, images, d_ref, x_ref, res_ref, mod_ref, parts_ref, out_ref, sums_ref, weights, sem
):
    @pl.when(pl.program_id(0) == 0)
    def _():
        cube_copies(parts_ref, weights, sem.at[0], *blocks)
        sums_ref[...] = jnp.zeros_like(sums_ref)
        wait_all(weights, sem.at[0])

    here = Images(res_ref.shape[0], length, images)
    normed, inv_std = standard_rows(side_by_side(x_ref).astype(jnp.float32))
    d_ln = nt(d_ref[0], weights[0]) + nt(d_ref[1], weights[1]) + nt(d_ref[2], weights[2])
    here.add(sums_ref, 0, d_ln)
    here.add(sums_ref, 1, d_ln * normed)
    scale = 1.0 + here.pick(mod_ref, 1)
    result = (res_ref[...] + norm_back(d_ln * scale, normed, inv_std)).astype(jnp.bfloat16)
    part = out_ref.shape[2]
    for index in range(out_ref.shape[0]):
        out_ref[index] = result[:, index * part : (index + 1) * part]


def input_backward(d_qkv, x, d_res, modulation, parts, blocks, length):
    groups, count, part = x.shape
    width = groups * part
    images = modulation.shape[0]
    rows = tile_of(count, 544)
    pieces = pl.BlockSpec((groups, rows, part), lambda i: (0, i, 0))
    return pl.pallas_call(
        functools.partial(input_kernel, blocks, length, images),
        grid=(count // rows,),
        in_specs=[
            pl.BlockSpec((3, rows, width), lambda i: (0, i, 0)),
            pieces,
            pl.BlockSpec((rows, width), lambda i: (i, 0)),
            pl.BlockSpec((images, 6, width), lambda i: (0, 0, 0)),
            pl.BlockSpec(memory_space=pl.ANY),
        ],
        out_specs=[pieces, pl.BlockSpec((images, 2, width), lambda i: (0, 0, 0))],
        out_shape=[
            jax.ShapeDtypeStruct((groups, count, part), jnp.bfloat16),
            jax.ShapeDtypeStruct((images, 2, width), jnp.float32),
        ],
        scratch_shapes=[
            pltpu.VMEM((3, width, width), jnp.bfloat16),
            pltpu.SemaphoreType.DMA((1,)),
        ],
        compiler_params=pltpu.CompilerParams(vmem_limit_bytes=48 << 20),
        cost_estimate=pl.CostEstimate(
            flops=6 * count * width * width,
            bytes_accessed=count * width * 14 + 6 * width * width,
            transcendentals=count,
        ),
        name="input_backward",
    )(d_qkv, x, d_res, modulation, parts)


def turn_rows(source, target):
    total = source.shape[0]
    step = 640
    for start in range(0, total, step):
        size = min(step, total - start)
        target[:, start : start + size] = source[start : start + size, :].T


def ffn_grad_kernel(left_a, left_b, right_a, right_b, out_ref, turned):
    pair, tile = pl.program_id(0), pl.program_id(1)

    def write(value):
        value = value.astype(jnp.bfloat16)
        out_ref[...] = value.reshape(out_ref.shape)

    @pl.when((pair == 0) & (tile == 0))
    def _():
        turn_rows(left_a, turned)

    @pl.when((pair == 1) & (tile == 0))
    def _():
        turn_rows(left_b, turned)

    @pl.when(pair == 0)
    def _():
        write(nn(turned[...], right_a[...]))

    @pl.when(pair == 1)
    def _():
        write(nn(turned[...], right_b[...]))


def ffn_grads(left_a, right_a, left_b, right_b, blocks):
    row_blocks, col_blocks = blocks
    count, width = left_a.shape
    ff = right_a.shape[1]
    ff_part = ff // col_blocks
    span = min(512, ff_part)
    inner = ff_part // span
    tiles = ff // span
    height = width // row_blocks
    left = pl.BlockSpec((count, width), lambda p, j: (0, 0))
    return pl.pallas_call(
        ffn_grad_kernel,
        grid=(2, tiles),
        in_specs=[
            left,
            left,
            pl.BlockSpec((count, span), lambda p, j: (0, j * (1 - p) + (tiles - 1) * p)),
            pl.BlockSpec((count, span), lambda p, j: (0, j * p)),
        ],
        out_specs=pl.BlockSpec(
            (row_blocks, 1, height, span), lambda p, j: (0, j // inner, 0, p * inner + j % inner)
        ),
        out_shape=jax.ShapeDtypeStruct((row_blocks, col_blocks, height, 2 * ff_part), jnp.bfloat16),
        scratch_shapes=[pltpu.VMEM((width, count), jnp.bfloat16)],
        compiler_params=pltpu.CompilerParams(vmem_limit_bytes=56 << 20),
        cost_estimate=pl.CostEstimate(
            flops=4 * count * width * ff,
            bytes_accessed=count * width * 4 + count * ff * 4 + width * ff * 4,
            transcendentals=0,
        ),
        name="ffn_grads",
    )(left_a, left_b, right_a, right_b)


def attn_grad_kernel(left_a, left_b, right_a, right_b, out_ref, turned):
    which = pl.program_id(0)

    def write(value):
        height, part = out_ref.shape[2:]
        value = value.astype(jnp.bfloat16)
        for c in range(out_ref.shape[1]):
            piece = value[:, c * part : (c + 1) * part]
            out_ref[:, c] = piece.reshape(out_ref.shape[0], height, part)

    @pl.when(which == 0)
    def _():
        turn_rows(left_a, turned)
        write(nn(turned[...], right_a[...]))

    @pl.when(which == 1)
    def _():
        turn_rows(left_b, turned)

    @pl.when(which > 0)
    def _():
        write(nn(turned[...], right_b[0]))


def attn_grads(attended, d_one, ln_one, d_qkv, blocks):
    row_blocks, col_blocks = blocks
    count, width = attended.shape
    part = width // col_blocks
    height = width // row_blocks
    fixed = pl.BlockSpec((count, width), lambda p: (0, 0), pipeline_mode=pl.Buffered(1))
    return pl.pallas_call(
        attn_grad_kernel,
        grid=(4,),
        in_specs=[
            fixed,
            fixed,
            fixed,
            pl.BlockSpec((1, count, width), lambda p: (jnp.maximum(p - 1, 0), 0, 0)),
        ],
        out_specs=pl.BlockSpec((row_blocks, col_blocks, height, part), lambda p: (0, 0, 0, p)),
        out_shape=jax.ShapeDtypeStruct((row_blocks, col_blocks, height, 4 * part), jnp.bfloat16),
        scratch_shapes=[pltpu.VMEM((width, count), jnp.bfloat16)],
        compiler_params=pltpu.CompilerParams(vmem_limit_bytes=60 << 20),
        cost_estimate=pl.CostEstimate(
            flops=8 * count * width * width,
            bytes_accessed=count * width * 12 + width * width * 8,
            transcendentals=0,
        ),
        name="attn_grads",
    )(attended, ln_one, d_one, d_qkv)


def swap(pieces, axes):
    return lax.all_to_all(pieces, axes, split_axis=0, concat_axis=0, tiled=False)


def share(value, axes, count):
    return swap(jnp.broadcast_to(value[None], (count,) + value.shape), axes)


BOTH = ("row", "col")


def shards(
    tokens,
    condition,
    scale_ids,
    attention_triple_matrix,
    attention_triple_offset,
    qk_gain,
    w_proj,
    b_proj,
    w_fc1,
    b_fc1,
    w_fc2,
    b_fc2,
    w_ada,
    b_ada,
    out_grad,
):
    rows = lax.axis_size("row")
    groups = lax.axis_size("col")
    row = lax.axis_index("row")
    place = lax.axis_index("col")
    everyone = rows * groups
    part = tokens.shape[0]
    width = part * groups
    images_row, length = scale_ids.shape
    images = images_row // groups
    count = images * length
    block = w_proj.shape[0]
    ff_part = b_fc1.shape[0]
    hidden_width = ff_part * groups
    aligned = part % 128 == 0
    blocks = (rows, groups) if aligned else (1, 1)
    f32, bf16 = jnp.float32, jnp.bfloat16

    qkv_parts = lax.all_gather(attention_triple_matrix.transpose(1, 0, 2), BOTH)
    rest_parts = lax.all_gather(jnp.concatenate([w_proj, w_fc1, w_fc2.T], axis=1), BOTH)

    def whole(parts):
        parts = parts.reshape((rows, groups) + parts.shape[1:])
        return parts.transpose(0, 2, 1, 3).reshape(width, groups * parts.shape[-1])

    def spread(wide):
        cols = wide.shape[1] // groups
        pieces = wide.reshape(rows, block, groups, cols).transpose(0, 2, 1, 3)
        return pieces.reshape(everyone, block, cols)

    if not aligned:
        qkv_parts = jnp.stack([whole(qkv_parts[:, index]) for index in range(3)])[None]
        cut = part + ff_part
        rest_parts = jnp.concatenate(
            [
                whole(rest_parts[:, :, :part]),
                whole(rest_parts[:, :, part:cut]),
                whole(rest_parts[:, :, cut:]),
            ],
            axis=1,
        )[None]

    offsets = attention_triple_offset.astype(f32).reshape(-1)
    small = share(
        jnp.concatenate(
            [offsets, b_proj.astype(f32), b_fc1.astype(f32), b_fc2.astype(f32), qk_gain]
        ),
        "col",
        groups,
    )
    cuts = [3 * part, 4 * part, 4 * part + ff_part, 5 * part + ff_part]
    bias_qkv = small[:, : cuts[0]].reshape(groups, 3, part).transpose(1, 0, 2).reshape(3, 1, width)
    bias_proj = small[:, cuts[0] : cuts[1]].reshape(1, width)
    bias_one = small[:, cuts[1] : cuts[2]].reshape(1, hidden_width)
    bias_two = small[:, cuts[2] : cuts[3]].reshape(1, width)
    gain_row = jnp.repeat(small[:, cuts[3] :].reshape(-1), HEAD_DIM)[None]

    cond_float = condition.astype(f32)
    soft = jax.nn.silu(cond_float).astype(bf16)
    soft_all = (
        share(soft, BOTH, everyone)
        .reshape(rows, groups, images_row, part)
        .transpose(0, 2, 1, 3)
        .reshape(rows * images_row, width)
    )
    ada_block = w_ada.shape[1]
    soft_mine = lax.dynamic_slice(
        soft_all, (0, row * ada_block), (rows * images_row, ada_block)
    )
    mod_part = jnp.einsum("ic,scd->isd", soft_mine, w_ada, preferred_element_type=f32)
    mod_part = mod_part + jnp.where(row == 0, b_ada.astype(f32), 0.0)[None]
    modulation = swap(mod_part.reshape(everyone, images, 6, part), BOTH)
    modulation = (
        modulation.reshape(rows, groups, images, 6, part)
        .sum(axis=0)
        .transpose(1, 2, 0, 3)
        .reshape(images, 6, width)
    )

    def to_tokens(features):
        pieces = swap(features.T.reshape(groups, count, part), "col")
        return pieces if aligned else pieces.transpose(1, 0, 2).reshape(1, count, width)

    def to_features(pieces):
        if not aligned:
            pieces = pieces[0].reshape(count, groups, part).transpose(1, 0, 2)
        return swap(pieces, "col").reshape(groups * count, part).T

    tok_in = to_tokens(tokens)
    grad_in = to_tokens(out_grad)
    scale_rows = lax.dynamic_slice(scale_ids, (place * images, 0), (images, length))
    query_lanes, key_lanes = mask_lanes(scale_rows)

    ln_one, qkv = qkv_forward(tok_in, modulation, bias_qkv, qkv_parts, blocks, length)
    qkv = qkv.reshape(3, images, length, width)
    attended, log_sums = attention_forward(qkv, gain_row, query_lanes, key_lanes)
    attn_rows = attended.reshape(count, width)
    (
        layer_pieces,
        ln_two,
        hidden,
        d_two,
        d_pre,
        d_one,
        d_res,
        d_attended,
        mod_sums,
        sum_bproj,
        sum_b1,
        sum_b2,
    ) = ffn(
        tok_in,
        attn_rows,
        grad_in,
        modulation,
        bias_proj,
        bias_one,
        bias_two,
        rest_parts,
        blocks,
        length,
    )
    layer_out = to_features(layer_pieces)
    wide_ffn = ffn_grads(ln_two, d_pre, d_two, hidden, blocks)
    if aligned:
        wide_ffn = wide_ffn.reshape(everyone, block, 2 * ff_part)
    else:
        wide_ffn = wide_ffn[0, 0]
        wide_ffn = jnp.concatenate(
            [spread(wide_ffn[:, :hidden_width]), spread(wide_ffn[:, hidden_width:])], axis=2
        )
    wide_ffn = lax.psum_scatter(wide_ffn, BOTH, scatter_dimension=0, tiled=False).astype(f32)
    grad_fc1 = wide_ffn[:, :ff_part]
    grad_fc2 = wide_ffn[:, ff_part:].T

    d_qkv, head_totals = attention_backward(
        qkv,
        gain_row,
        query_lanes,
        key_lanes,
        attended,
        log_sums,
        d_attended.reshape(images, length, width),
    )
    d_qkv = d_qkv.reshape(3, count, width)
    wide_attn = attn_grads(attn_rows, d_one, ln_one, d_qkv, blocks)
    if aligned:
        wide_attn = wide_attn.reshape(everyone, block, 4 * part)
    else:
        wide_attn = wide_attn[0, 0]
        wide_attn = jnp.concatenate(
            [spread(wide_attn[:, index * width : (index + 1) * width]) for index in range(4)],
            axis=2,
        )
    wide_attn = lax.psum_scatter(wide_attn, BOTH, scatter_dimension=0, tiled=False).astype(f32)
    grad_proj = wide_attn[:, :part]
    grad_qkv = wide_attn[:, part:].reshape(block, 3, part)
    token_pieces, first_sums = input_backward(
        d_qkv, tok_in, d_res, modulation, qkv_parts, blocks, length
    )
    grad_tokens = to_features(token_pieces)

    head_totals = head_totals.sum(axis=0)
    totals = jnp.concatenate(
        [
            head_totals[:3].reshape(3, groups, part).transpose(1, 0, 2).reshape(groups, 3 * part),
            sum_bproj.reshape(groups, part),
            sum_b1.reshape(groups, ff_part),
            sum_b2.reshape(groups, part),
            head_totals[3].reshape(-1, HEAD_DIM).sum(axis=1).reshape(groups, -1),
        ],
        axis=1,
    )
    totals = jnp.broadcast_to(totals[None], (rows,) + totals.shape)
    totals = swap(totals.reshape(everyone, -1), BOTH).sum(axis=0)
    d_mod = jnp.concatenate([first_sums, mod_sums], axis=1).astype(bf16)
    d_mod = d_mod.reshape(images, 6, groups, part).transpose(2, 0, 1, 3)
    d_mod = jnp.broadcast_to(d_mod[None], (rows,) + d_mod.shape)
    d_mod = swap(d_mod.reshape((everyone,) + d_mod.shape[2:]), BOTH)
    d_mod = d_mod.reshape(everyone * images, 6, part)
    grad_ada = jnp.einsum("ic,isd->scd", soft_mine, d_mod, preferred_element_type=f32)
    grad_bada = jnp.sum(d_mod.astype(f32), axis=0)
    d_soft = jnp.einsum("isd,scd->ic", d_mod, w_ada, preferred_element_type=f32)
    d_soft = d_soft.reshape(rows, 1, images_row, ada_block)
    d_soft = jnp.broadcast_to(d_soft, (rows, groups, images_row, ada_block))
    d_soft = swap(d_soft.reshape(everyone, images_row, ada_block), BOTH)
    d_soft = d_soft.reshape(rows, groups, images_row, ada_block).sum(axis=1)
    d_soft = d_soft.transpose(1, 0, 2).reshape(images_row, width)
    d_soft = lax.dynamic_slice(d_soft, (0, place * part), (images_row, part))
    _, silu_pull = jax.vjp(jax.nn.silu, cond_float)
    grad_condition = silu_pull(d_soft)[0].astype(bf16)
    return (
        layer_out,
        grad_tokens,
        grad_condition,
        grad_qkv,
        totals[: cuts[0]].reshape(3, part),
        totals[cuts[3] :],
        grad_proj,
        totals[cuts[0] : cuts[1]],
        grad_fc1,
        totals[cuts[1] : cuts[2]],
        grad_fc2,
        totals[cuts[2] : cuts[3]],
        grad_ada,
        grad_bada,
    )


def solution(mesh):
    placed = (
        P("col", "row"),
        P("row", "col"),
        P("row", None),
        P("row", None, "col"),
        P(None, "col"),
        P("col"),
        P("row", "col"),
        P("col"),
        P("row", "col"),
        P("col"),
        P("col", "row"),
        P("col"),
        P(None, "row", "col"),
        P(None, "col"),
        P("col", "row"),
    )
    return jax.shard_map(
        shards,
        mesh=mesh,
        in_specs=placed,
        out_specs=(
            P("col", "row"),
            P("col", "row"),
            P("row", "col"),
            P("row", None, "col"),
            P(None, "col"),
            P("col"),
            P("row", "col"),
            P("col"),
            P("row", "col"),
            P("col"),
            P("col", "row"),
            P("col"),
            P(None, "row", "col"),
            P(None, "col"),
        ),
        check_vma=False,
    )
```

```python
import functools
import jax
import jax.numpy as jnp
from jax import lax
from jax.sharding import PartitionSpec as P
from jax.experimental import pallas as pl
from jax.experimental.layout import Layout, with_layout_constraint
from jax.experimental.pallas import tpu as pltpu

HEAD_DIM = 64
PAIR = 2 * HEAD_DIM
NEG = -1024.0
FIRST_EXTRA = 16


def head_sums(values, left):
    first = jnp.sum(jnp.where(left, values, 0.0), axis=-1, keepdims=True)
    second = jnp.sum(jnp.where(left, 0.0, values), axis=-1, keepdims=True)
    return first, second


def unit_of(raw, left):
    first, second = head_sums(raw * raw, left)
    inverse = jnp.where(left, lax.rsqrt(first + 1e-06), lax.rsqrt(second + 1e-06))
    return raw * inverse, inverse


def nt(left_rows, right_rows):
    return lax.dot_general(
        left_rows, right_rows, (((1,), (1,)), ((), ())), preferred_element_type=jnp.float32
    )


def nn(left_rows, right_rows):
    return jnp.dot(left_rows, right_rows, preferred_element_type=jnp.float32)


def split_three(value):
    high = value.astype(jnp.bfloat16)
    rest = value - high.astype(jnp.float32)
    middle = rest.astype(jnp.bfloat16)
    lowest = (rest - middle.astype(jnp.float32)).astype(jnp.bfloat16)
    return high, middle, lowest


def forward_kernel(q_ref, k_ref, v_ref, gain_ref, qm_ref, km_ref, o_ref, lse_ref):
    lane = lax.broadcasted_iota(jnp.int32, q_ref.shape[-2:], 1)
    left = lane < HEAD_DIM
    q_unit, _ = unit_of(q_ref[0, 0], left)
    k_unit, _ = unit_of(k_ref[0, 0], left)
    q_low = (q_unit * gain_ref[...]).astype(jnp.bfloat16)
    k_low = k_unit.astype(jnp.bfloat16)
    v_low = v_ref[0, 0].astype(jnp.bfloat16)
    qm = qm_ref[0]
    km = km_ref[0]
    one = jnp.ones_like(v_low)
    results = []
    for head in range(2):
        mine = left if head == 0 else ~left
        scores = nt(jnp.where(mine, q_low, qm), jnp.where(mine, k_low, km))
        weights = jnp.exp(scores).astype(jnp.bfloat16)
        results.append(nn(weights, jnp.where(mine, v_low, one)))
    totals = jnp.where(left, results[1], results[0])
    lse_ref[0] = jnp.log(totals)
    swapped = pltpu.roll(totals, HEAD_DIM, 1)
    o_ref[0] = (jnp.where(left, results[0], results[1]) / swapped).astype(jnp.bfloat16)


def backward_kernel(
    q_ref, k_ref, v_ref, gain_ref, qm_ref, km_ref, o_ref, lse_ref, do_ref, d_ref, sums_ref
):
    shape = q_ref.shape[-2:]
    lane = lax.broadcasted_iota(jnp.int32, shape, 1)
    left = lane < HEAD_DIM
    spot = lane % HEAD_DIM
    gain = gain_ref[...]
    q_unit, q_inv = unit_of(q_ref[0, 0], left)
    k_unit, k_inv = unit_of(k_ref[0, 0], left)
    q_low = (q_unit * gain).astype(jnp.bfloat16)
    k_low = k_unit.astype(jnp.bfloat16)
    v_low = v_ref[0, 0].astype(jnp.bfloat16)
    d_out = do_ref[0]
    km = km_ref[0]

    def place(base, value):
        high, middle, lowest = split_three(value)
        base = jnp.where(spot == FIRST_EXTRA, high, base)
        base = jnp.where(spot == FIRST_EXTRA + 1, middle, base)
        return jnp.where(spot == FIRST_EXTRA + 2, lowest, base)

    qm = place(qm_ref[0], -lse_ref[0])
    product = d_out.astype(jnp.float32) * o_ref[0].astype(jnp.float32)
    first, second = head_sums(product, left)
    dm = place(jnp.zeros_like(d_out), -jnp.where(left, second, first))
    k_turned = k_low.astype(jnp.float32).T.astype(jnp.bfloat16)
    d_v, d_k, d_q = [], [], []
    for head in range(2):
        mine = left if head == 0 else ~left
        probs = jnp.exp(nt(jnp.where(mine, k_low, km), jnp.where(mine, q_low, qm)))
        d_v.append(nn(probs.astype(jnp.bfloat16), d_out))
        shifted = nt(jnp.where(mine, v_low, km), jnp.where(mine, d_out, dm))
        d_scores = (probs * shifted).astype(jnp.bfloat16)
        d_k.append(nn(d_scores, q_low))
        d_q.append(nn(k_turned[head * HEAD_DIM : (head + 1) * HEAD_DIM], d_scores))
    d_q_low = jnp.concatenate(d_q, axis=0).T
    d_k_low = jnp.where(left, d_k[0], d_k[1])
    d_values = jnp.where(left, d_v[0], d_v[1])
    turned = d_q_low * gain
    first, second = head_sums(turned * q_unit, left)
    d_queries = q_inv * (turned - q_unit * jnp.where(left, first, second))
    first, second = head_sums(d_k_low * k_unit, left)
    d_keys = k_inv * (d_k_low - k_unit * jnp.where(left, first, second))
    parts = []
    for index, value in enumerate((d_queries, d_keys, d_values)):
        rounded = value.astype(jnp.bfloat16)
        d_ref[index, 0] = rounded
        parts.append(jnp.sum(rounded.astype(jnp.float32), axis=0, keepdims=True))
    parts.append(jnp.sum(d_q_low * q_unit, axis=0, keepdims=True))
    parts.append(jnp.zeros((4, PAIR), jnp.float32))
    sums_ref[0] = jnp.concatenate(parts, axis=0)


def mask_lanes(ids):
    spot = jnp.arange(PAIR, dtype=jnp.int32) % HEAD_DIM
    rows = ids[:, :, None]
    queries = (rows == spot).astype(jnp.bfloat16)
    keys = jnp.where((rows > spot) & (spot < FIRST_EXTRA), NEG, 0.0)
    extra = (spot >= FIRST_EXTRA) & (spot < FIRST_EXTRA + 3)
    return queries, jnp.where(extra, 1.0, keys).astype(jnp.bfloat16)


def specs(length):
    def raw(which):
        return pl.BlockSpec((1, 1, length, PAIR), lambda b, h: (which, b, 0, h))

    gain = pl.BlockSpec((1, PAIR), lambda b, h: (0, h))
    lanes = pl.BlockSpec((1, length, PAIR), lambda b, h: (b, 0, 0))
    tokens = pl.BlockSpec((1, length, PAIR), lambda b, h: (b, 0, h))
    return [raw(0), raw(1), raw(2), gain, lanes, lanes], tokens


def attention_forward(qkv, gain_row, qm, km):
    _, images, length, width = qkv.shape
    ins, tokens = specs(length)
    return pl.pallas_call(
        forward_kernel,
        grid=(images, width // PAIR),
        in_specs=ins,
        out_specs=[tokens, tokens],
        out_shape=[
            jax.ShapeDtypeStruct((images, length, width), jnp.bfloat16),
            jax.ShapeDtypeStruct((images, length, width), jnp.float32),
        ],
        compiler_params=pltpu.CompilerParams(vmem_limit_bytes=48 << 20),
        cost_estimate=pl.CostEstimate(
            flops=4 * images * length * length * width * 2, bytes_accessed=images * length * width * 18, transcendentals=images * length * length * 16
        ),
        name="attention_forward",
    )(qkv, qkv, qkv, gain_row, qm, km)


def attention_backward(qkv, gain_row, qm, km, out, lse, d_out):
    _, images, length, width = qkv.shape
    ins, tokens = specs(length)
    return pl.pallas_call(
        backward_kernel,
        grid=(images, width // PAIR),
        in_specs=ins + [tokens, tokens, tokens],
        out_specs=[
            pl.BlockSpec((3, 1, length, PAIR), lambda b, h: (0, b, 0, h)),
            pl.BlockSpec((1, 8, PAIR), lambda b, h: (b, 0, h)),
        ],
        out_shape=[
            jax.ShapeDtypeStruct((3, images, length, width), jnp.bfloat16),
            jax.ShapeDtypeStruct((images, 8, width), jnp.float32),
        ],
        compiler_params=pltpu.CompilerParams(vmem_limit_bytes=56 << 20),
        cost_estimate=pl.CostEstimate(
            flops=10 * images * length * length * width * 2, bytes_accessed=images * length * width * 30, transcendentals=images * length * length * 16
        ),
        name="attention_backward",
    )(qkv, qkv, qkv, gain_row, qm, km, out, lse, d_out)


GELU_RATE = 0.7978845608
GELU_CUBE = 0.7978845608 * 0.044715
FFN_CHUNK = 512


def tile_of(count, want):
    best = 8
    for size in range(8, want + 1, 8):
        if count % size == 0:
            best = size
    return best


def side_by_side(ref):
    return jnp.concatenate([ref[index] for index in range(ref.shape[0])], axis=1)


class Images:
    def __init__(self, rows, length, images):
        start = pl.program_id(0) * rows
        self.first = start // length
        self.second = jnp.minimum((start + rows - 1) // length, images - 1)
        index = lax.broadcasted_iota(jnp.int32, (rows, 1), 0) + start
        self.early = index < (self.first + 1) * length

    def pick(self, table, which):
        return jnp.where(
            self.early,
            table[self.first, which : which + 1],
            table[self.second, which : which + 1],
        )

    def add(self, sums, which, value):
        early = jnp.sum(jnp.where(self.early, value, 0.0), axis=0, keepdims=True)
        late = jnp.sum(jnp.where(self.early, 0.0, value), axis=0, keepdims=True)
        sums[self.first, which : which + 1] += early
        sums[self.second, which : which + 1] += late


def standard_rows(value):
    centered = value - jnp.mean(value, axis=-1, keepdims=True)
    inv_std = lax.rsqrt(jnp.mean(centered * centered, axis=-1, keepdims=True) + 1e-06)
    return centered * inv_std, inv_std


def norm_back(incoming, normed, inv_std):
    average = jnp.mean(incoming, axis=-1, keepdims=True)
    cross = jnp.mean(incoming * normed, axis=-1, keepdims=True)
    return inv_std * (incoming - average - normed * cross)


def block_copies(parts, start, target, sem, row_blocks, col_blocks):
    height = target.shape[0] // row_blocks
    span = target.shape[1] // col_blocks
    for r in range(row_blocks):
        for c in range(col_blocks):
            pltpu.make_async_copy(
                parts.at[r * col_blocks + c, :, pl.ds(start, span)],
                target.at[pl.ds(r * height, height), pl.ds(c * span, span)],
                sem,
            ).start()


def wait_all(target, sem):
    pltpu.make_async_copy(target, target, sem).wait()


def ffn_kernel(
    blocks, length, images,
    x_ref, att_ref, g_ref, mod_ref, bias_proj_ref, bias_one_ref, bias_two_ref, parts_ref,
    out_ref, ln_ref, hidden_ref, d_two_ref, d_pre_ref, d_one_ref, d_res_ref, d_att_ref,
    sums_ref, sum_proj_ref, sum_one_ref, sum_two_ref,
    w_proj, w_one, w_two, slope, sems,
):
    rows = att_ref.shape[0]
    ff = w_one.shape[1]
    first_step = pl.program_id(0) == 0

    @pl.when(first_step)
    def _():
        part = w_proj.shape[1] // blocks[1]
        ff_part = ff // blocks[1]
        block_copies(parts_ref, 0, w_proj, sems.at[0], *blocks)
        block_copies(parts_ref, part, w_one, sems.at[1], *blocks)
        block_copies(parts_ref, part + ff_part, w_two, sems.at[2], *blocks)
        sums_ref[...] = jnp.zeros_like(sums_ref)
        sum_proj_ref[...] = jnp.zeros_like(sum_proj_ref)
        sum_one_ref[...] = jnp.zeros_like(sum_one_ref)
        sum_two_ref[...] = jnp.zeros_like(sum_two_ref)
        wait_all(w_proj, sems.at[0])
        wait_all(w_one, sems.at[1])
        wait_all(w_two, sems.at[2])

    here = Images(rows, length, images)
    gate_attn = here.pick(mod_ref, 2)
    branch_one = nn(att_ref[...], w_proj[...]) + bias_proj_ref[...]
    residual = side_by_side(x_ref).astype(jnp.float32) + gate_attn * branch_one
    normed, inv_std = standard_rows(residual)
    scale = 1.0 + here.pick(mod_ref, 4)
    ln_two = (normed * scale + here.pick(mod_ref, 3)).astype(jnp.bfloat16)
    ln_ref[...] = ln_two
    branch_two = jnp.broadcast_to(bias_two_ref[...], residual.shape)
    for start in range(0, ff, FFN_CHUNK):
        span = slice(start, start + FFN_CHUNK)
        pre = nn(ln_two, w_one[:, span]) + bias_one_ref[:, span]
        square = pre * pre
        turn = jnp.tanh(pre * (GELU_RATE + GELU_CUBE * square))
        half = 0.5 + 0.5 * turn
        value = pre * half
        slope[:, span] = half + value * (1.0 - turn) * (GELU_RATE + 3.0 * GELU_CUBE * square)
        low = value.astype(jnp.bfloat16)
        hidden_ref[:, span] = low
        branch_two += nt(low, w_two[:, span])
    gate_ffn = here.pick(mod_ref, 5)
    result = (residual + gate_ffn * branch_two).astype(jnp.bfloat16)
    part = out_ref.shape[2]
    for index in range(out_ref.shape[0]):
        out_ref[index] = result[:, index * part : (index + 1) * part]
    incoming = side_by_side(g_ref).astype(jnp.float32)
    here.add(sums_ref, 3, incoming * branch_two)
    d_two = (gate_ffn * incoming).astype(jnp.bfloat16)
    d_two_ref[...] = d_two
    sum_two_ref[...] += jnp.sum(d_two.astype(jnp.float32), axis=0, keepdims=True)
    d_back = jnp.zeros_like(residual)
    for start in range(0, ff, FFN_CHUNK):
        span = slice(start, start + FFN_CHUNK)
        d_pre = (nn(d_two, w_two[:, span]) * slope[:, span]).astype(jnp.bfloat16)
        d_pre_ref[:, span] = d_pre
        sum_one_ref[:, span] += jnp.sum(d_pre.astype(jnp.float32), axis=0, keepdims=True)
        d_back += nt(d_pre, w_one[:, span])
    here.add(sums_ref, 1, d_back)
    here.add(sums_ref, 2, d_back * normed)
    d_res = incoming + norm_back(d_back * scale, normed, inv_std)
    d_res_ref[...] = d_res
    here.add(sums_ref, 0, d_res * branch_one)
    d_one = (gate_attn * d_res).astype(jnp.bfloat16)
    d_one_ref[...] = d_one
    sum_proj_ref[...] += jnp.sum(d_one.astype(jnp.float32), axis=0, keepdims=True)
    d_att_ref[...] = nt(d_one, w_proj[...]).astype(jnp.bfloat16)


def ffn(x, attended, g, modulation, bias_proj, bias_one, bias_two, parts, blocks, length):
    groups, count, part = x.shape
    width = groups * part
    ff = bias_one.shape[1]
    images = modulation.shape[0]
    rows = tile_of(count, 272)
    f32, bf16 = jnp.float32, jnp.bfloat16
    pieces = pl.BlockSpec((groups, rows, part), lambda i: (0, i, 0))
    wide = pl.BlockSpec((rows, width), lambda i: (i, 0))
    tall = pl.BlockSpec((rows, ff), lambda i: (i, 0))

    def fixed(*shape):
        return pl.BlockSpec(shape, lambda i: (0,) * len(shape))

    def made(shape, dtype):
        return jax.ShapeDtypeStruct(shape, dtype)

    return pl.pallas_call(
        functools.partial(ffn_kernel, blocks, length, images),
        grid=(count // rows,),
        in_specs=[
            pieces, wide, pieces, fixed(images, 6, width), fixed(1, width), fixed(1, ff),
            fixed(1, width), pl.BlockSpec(memory_space=pl.ANY),
        ],
        out_specs=[
            pieces, wide, tall, wide, tall, wide, wide, wide,
            fixed(images, 4, width), fixed(1, width), fixed(1, ff), fixed(1, width),
        ],
        out_shape=[
            made((groups, count, part), bf16), made((count, width), bf16),
            made((count, ff), bf16), made((count, width), bf16), made((count, ff), bf16),
            made((count, width), bf16), made((count, width), f32), made((count, width), bf16),
            made((images, 4, width), f32), made((1, width), f32), made((1, ff), f32),
            made((1, width), f32),
        ],
        scratch_shapes=[
            pltpu.VMEM((width, width), bf16), pltpu.VMEM((width, ff), bf16),
            pltpu.VMEM((width, ff), bf16), pltpu.VMEM((rows, ff), f32),
            pltpu.SemaphoreType.DMA((3,)),
        ],
        compiler_params=pltpu.CompilerParams(vmem_limit_bytes=62 << 20),
        cost_estimate=pl.CostEstimate(
            flops=4 * count * width * (2 * ff + width),
            bytes_accessed=count * width * 20 + count * ff * 4 + width * (2 * ff + width) * 2,
            transcendentals=count * ff,
        ),
        name="ffn_both",
    )(x, attended, g, modulation, bias_proj, bias_one, bias_two, parts)


def cube_copies(parts, target, sem, row_blocks, col_blocks):
    height = target.shape[1] // row_blocks
    span = target.shape[2] // col_blocks
    for r in range(row_blocks):
        for c in range(col_blocks):
            pltpu.make_async_copy(
                parts.at[r * col_blocks + c],
                target.at[:, pl.ds(r * height, height), pl.ds(c * span, span)],
                sem,
            ).start()


def qkv_kernel(blocks, length, images, x_ref, mod_ref, bias_ref, parts_ref, ln_ref, qkv_ref, weights, sem):
    @pl.when(pl.program_id(0) == 0)
    def _():
        cube_copies(parts_ref, weights, sem.at[0], *blocks)
        wait_all(weights, sem.at[0])

    here = Images(ln_ref.shape[0], length, images)
    normed, _ = standard_rows(side_by_side(x_ref).astype(jnp.float32))
    ln_one = (normed * (1.0 + here.pick(mod_ref, 1)) + here.pick(mod_ref, 0)).astype(jnp.bfloat16)
    ln_ref[...] = ln_one
    for index in range(3):
        qkv_ref[index] = nn(ln_one, weights[index]) + bias_ref[index]


def qkv_forward(x, modulation, bias, parts, blocks, length):
    groups, count, part = x.shape
    width = groups * part
    images = modulation.shape[0]
    rows = tile_of(count, 544)
    return pl.pallas_call(
        functools.partial(qkv_kernel, blocks, length, images),
        grid=(count // rows,),
        in_specs=[
            pl.BlockSpec((groups, rows, part), lambda i: (0, i, 0)),
            pl.BlockSpec((images, 6, width), lambda i: (0, 0, 0)),
            pl.BlockSpec((3, 1, width), lambda i: (0, 0, 0)),
            pl.BlockSpec(memory_space=pl.ANY),
        ],
        out_specs=[
            pl.BlockSpec((rows, width), lambda i: (i, 0)),
            pl.BlockSpec((3, rows, width), lambda i: (0, i, 0)),
        ],
        out_shape=[
            jax.ShapeDtypeStruct((count, width), jnp.bfloat16),
            jax.ShapeDtypeStruct((3, count, width), jnp.float32),
        ],
        scratch_shapes=[
            pltpu.VMEM((3, width, width), jnp.bfloat16),
            pltpu.SemaphoreType.DMA((1,)),
        ],
        compiler_params=pltpu.CompilerParams(vmem_limit_bytes=48 << 20),
        cost_estimate=pl.CostEstimate(
            flops=6 * count * width * width,
            bytes_accessed=count * width * 16 + 6 * width * width,
            transcendentals=count,
        ),
        name="qkv_forward",
    )(x, modulation, bias, parts)


def input_kernel(
    blocks, length, images, d_ref, x_ref, res_ref, mod_ref, parts_ref, out_ref, sums_ref, weights, sem
):
    @pl.when(pl.program_id(0) == 0)
    def _():
        cube_copies(parts_ref, weights, sem.at[0], *blocks)
        sums_ref[...] = jnp.zeros_like(sums_ref)
        wait_all(weights, sem.at[0])

    here = Images(res_ref.shape[0], length, images)
    normed, inv_std = standard_rows(side_by_side(x_ref).astype(jnp.float32))
    d_ln = nt(d_ref[0], weights[0]) + nt(d_ref[1], weights[1]) + nt(d_ref[2], weights[2])
    here.add(sums_ref, 0, d_ln)
    here.add(sums_ref, 1, d_ln * normed)
    scale = 1.0 + here.pick(mod_ref, 1)
    result = (res_ref[...] + norm_back(d_ln * scale, normed, inv_std)).astype(jnp.bfloat16)
    part = out_ref.shape[2]
    for index in range(out_ref.shape[0]):
        out_ref[index] = result[:, index * part : (index + 1) * part]


def input_backward(d_qkv, x, d_res, modulation, parts, blocks, length):
    groups, count, part = x.shape
    width = groups * part
    images = modulation.shape[0]
    rows = tile_of(count, 544)
    pieces = pl.BlockSpec((groups, rows, part), lambda i: (0, i, 0))
    return pl.pallas_call(
        functools.partial(input_kernel, blocks, length, images),
        grid=(count // rows,),
        in_specs=[
            pl.BlockSpec((3, rows, width), lambda i: (0, i, 0)),
            pieces,
            pl.BlockSpec((rows, width), lambda i: (i, 0)),
            pl.BlockSpec((images, 6, width), lambda i: (0, 0, 0)),
            pl.BlockSpec(memory_space=pl.ANY),
        ],
        out_specs=[pieces, pl.BlockSpec((images, 2, width), lambda i: (0, 0, 0))],
        out_shape=[
            jax.ShapeDtypeStruct((groups, count, part), jnp.bfloat16),
            jax.ShapeDtypeStruct((images, 2, width), jnp.float32),
        ],
        scratch_shapes=[
            pltpu.VMEM((3, width, width), jnp.bfloat16),
            pltpu.SemaphoreType.DMA((1,)),
        ],
        compiler_params=pltpu.CompilerParams(vmem_limit_bytes=48 << 20),
        cost_estimate=pl.CostEstimate(
            flops=6 * count * width * width,
            bytes_accessed=count * width * 14 + 6 * width * width,
            transcendentals=count,
        ),
        name="input_backward",
    )(d_qkv, x, d_res, modulation, parts)


def turn_rows(source, target):
    total = source.shape[0]
    step = 640
    for start in range(0, total, step):
        size = min(step, total - start)
        target[:, start : start + size] = source[start : start + size, :].T


def ffn_grad_kernel(left_a, left_b, right_a, right_b, out_ref, turned):
    pair, tile = pl.program_id(0), pl.program_id(1)

    def write(value):
        value = value.astype(jnp.bfloat16)
        out_ref[...] = value.reshape(out_ref.shape)

    @pl.when((pair == 0) & (tile == 0))
    def _():
        turn_rows(left_a, turned)

    @pl.when((pair == 1) & (tile == 0))
    def _():
        turn_rows(left_b, turned)

    @pl.when(pair == 0)
    def _():
        write(nn(turned[...], right_a[...]))

    @pl.when(pair == 1)
    def _():
        write(nn(turned[...], right_b[...]))


def ffn_grads(left_a, right_a, left_b, right_b, blocks):
    row_blocks, col_blocks = blocks
    count, width = left_a.shape
    ff = right_a.shape[1]
    ff_part = ff // col_blocks
    span = min(512, ff_part)
    inner = ff_part // span
    tiles = ff // span
    height = width // row_blocks
    left = pl.BlockSpec((count, width), lambda p, j: (0, 0))
    return pl.pallas_call(
        ffn_grad_kernel,
        grid=(2, tiles),
        in_specs=[
            left,
            left,
            pl.BlockSpec((count, span), lambda p, j: (0, j * (1 - p) + (tiles - 1) * p)),
            pl.BlockSpec((count, span), lambda p, j: (0, j * p)),
        ],
        out_specs=pl.BlockSpec(
            (row_blocks, 1, height, span), lambda p, j: (0, j // inner, 0, p * inner + j % inner)
        ),
        out_shape=jax.ShapeDtypeStruct((row_blocks, col_blocks, height, 2 * ff_part), jnp.bfloat16),
        scratch_shapes=[pltpu.VMEM((width, count), jnp.bfloat16)],
        compiler_params=pltpu.CompilerParams(vmem_limit_bytes=56 << 20),
        cost_estimate=pl.CostEstimate(
            flops=4 * count * width * ff,
            bytes_accessed=count * width * 4 + count * ff * 4 + width * ff * 4,
            transcendentals=0,
        ),
        name="ffn_grads",
    )(left_a, left_b, right_a, right_b)


MESH = pl.DeviceIdType.MESH


class Place:
    def __init__(self):
        row = lax.axis_index("row")
        col = lax.axis_index("col")
        self.z, self.x, self.y, self.k = row // 2, row % 2, col // 2, col % 2

    def other(self, z=None, x=None, y=None, k=None):
        z = self.z if z is None else z
        x = self.x if x is None else x
        y = self.y if y is None else y
        k = self.k if k is None else k
        return (z * 2 + x, y * 2 + k)

    def partners(self):
        near = [self.other(k=1 - self.k), self.other(x=1 - self.x), self.other(y=1 - self.y)]
        return near + [self.other(z=(self.z + step) % 4) for step in (1, 2, 3)]

    def meet(self):
        barrier = pltpu.get_barrier_semaphore()
        partners = self.partners()
        for partner in partners:
            pl.semaphore_signal(barrier, inc=1, device_id=partner, device_id_type=MESH)
        pl.semaphore_wait(barrier, len(partners))


def add_into(target, first, second):
    for index in range(first.shape[0]):
        value = first[index].astype(jnp.float32) + second[index].astype(jnp.float32)
        target[index] = value.astype(target.dtype)


def attn_grad_kernel(
    att_ref, one_ref, ln_ref, d_ref, totals_ref, mod_ref,
    out_ref, totals_out, mod_out,
    left, turned, right, mine, core_in, after_core, x_in, after_x, z_in, summed, y_send, y_in,
    t_core, t_x, t_z, t_y, t_sum, e_core, e_y, e_x,
    load_sems, send_sems, recv_sems,
):
    at = Place()
    loads = [
        pltpu.make_async_copy(att_ref, left, load_sems.at[0]),
        pltpu.make_async_copy(ln_ref, left, load_sems.at[1]),
        pltpu.make_async_copy(one_ref, right.at[0], load_sems.at[2]),
        pltpu.make_async_copy(d_ref.at[0], right.at[1], load_sems.at[3]),
        pltpu.make_async_copy(d_ref.at[1], right.at[0], load_sems.at[4]),
        pltpu.make_async_copy(d_ref.at[2], right.at[1], load_sems.at[5]),
    ]
    loads[0].start()
    loads[2].start()
    loads[3].start()
    at.meet()
    across = at.other(k=1 - at.k)
    beside = at.other(x=1 - at.x)
    over = at.other(y=1 - at.y)
    ahead = [(at.z + step) % 4 for step in (1, 2, 3)]
    sent = []

    def send(flow, which, source, target, device):
        copy = pltpu.make_async_remote_copy(
            src_ref=source,
            dst_ref=target,
            send_sem=send_sems.at[flow, which],
            recv_sem=recv_sems.at[flow, which],
            device_id=device,
            device_id_type=MESH,
        )
        copy.start()
        sent.append(copy)
        return copy

    flights = {}

    flights[4, 0] = send(4, 0, totals_ref.at[1 - at.k], t_core, across)
    flights[5, 0] = send(5, 0, mod_ref.at[1 - at.k], e_core.at[at.k], across)

    def small_one():
        flights[4, 0].wait_recv()
        for y in range(2):
            t_core[y] = t_core[y] + totals_ref[at.k, y]
        flights[4, 1] = send(4, 1, t_core, t_x, beside)
        flights[5, 0].wait_recv()
        for y in range(2):
            e_core[at.k, y] = mod_ref[at.k, y]
        flights[5, 1] = send(5, 1, e_core.at[:, 1 - at.y], e_y.at[at.y], over)

    def small_two():
        flights[4, 1].wait_recv()
        for y in range(2):
            t_z[at.z, y] = t_x[y] + t_core[y]
        flights[4, 2] = [
            send(4, 2 + index, t_z.at[at.z], t_z.at[at.z], at.other(z=z))
            for index, z in enumerate(ahead)
        ]
        flights[5, 1].wait_recv()
        for k in range(2):
            e_y[at.y, k] = e_core[k, at.y]
        flights[5, 2] = send(5, 2, e_y, e_x.at[at.x], beside)

    def small_three():
        for copy in flights[4, 2]:
            copy.wait_recv()
        for y in range(2):
            t_sum[y] = (t_z[0, y] + t_z[1, y]) + (t_z[2, y] + t_z[3, y])
        flights[4, 3] = send(4, 5, t_sum.at[1 - at.y], t_y, over)
        flights[5, 2].wait_recv()
        for y in range(2):
            for k in range(2):
                e_x[at.x, y, k] = e_y[y, k]
        mod_out[at.z] = e_x[...]
        flights[5, 3] = [
            send(5, 3 + index, e_x, mod_out.at[at.z], at.other(z=z))
            for index, z in enumerate(ahead)
        ]

    def small_four():
        flights[4, 3].wait_recv()
        totals_out[...] = t_sum[at.y] + t_y[...]
        for copy in flights[5, 3]:
            copy.wait_recv()

    def compute(p):
        for c in range(4):
            span = slice(c * 256, (c + 1) * 256)
            value = nn(turned[...], right[p % 2, :, span]).astype(jnp.bfloat16)
            for r in range(8):
                mine[p, c % 2, r % 2, r // 2, c // 2] = value[r * 128 : (r + 1) * 128]
        flights[p, 0] = send(p, 0, mine.at[p, 1 - at.k], core_in.at[p], across)

    def core_done(p):
        flights[p, 0].wait_recv()
        for x in range(2):
            for z in range(4):
                add_into(after_core.at[p, x, z], mine.at[p, at.k, x, z], core_in.at[p, x, z])
        flights[p, 1] = send(p, 1, after_core.at[p, 1 - at.x], x_in.at[p], beside)

    def x_done(p):
        flights[p, 1].wait_recv()
        for z in range(4):
            add_into(after_x.at[p, z], after_core.at[p, at.x, z], x_in.at[p, z])
        flights[p, 2] = [
            send(p, 2 + index, after_x.at[p, z], z_in.at[p, index], at.other(z=z))
            for index, z in enumerate(ahead)
        ]

    def z_done(p):
        for copy in flights[p, 2]:
            copy.wait_recv()
        for y in range(2):
            value = after_x[p, at.z, y].astype(jnp.float32)
            for index in range(3):
                value = value + z_in[p, index, y].astype(jnp.float32)
            summed[p, y] = value
        y_send[p] = summed[p, 1 - at.y].astype(jnp.bfloat16)
        flights[p, 3] = send(p, 5, y_send.at[p], y_in.at[p], over)

    def y_done(p):
        flights[p, 3].wait_recv()
        out_ref[p] = summed[p, at.y] + y_in[p].astype(jnp.float32)

    loads[0].wait()
    turn_rows(left, turned)
    loads[1].start()
    loads[2].wait()
    compute(0)
    loads[4].start()
    small_one()
    core_done(0)
    loads[1].wait()
    turn_rows(left, turned)
    loads[3].wait()
    compute(1)
    loads[5].start()
    core_done(1)
    small_two()
    x_done(0)
    loads[4].wait()
    compute(2)
    core_done(2)
    small_three()
    loads[5].wait()
    compute(3)
    core_done(3)
    x_done(1)
    z_done(0)
    small_four()
    x_done(2)
    z_done(1)
    y_done(0)
    x_done(3)
    z_done(2)
    y_done(1)
    z_done(3)
    y_done(2)
    y_done(3)
    for copy in sent:
        copy.wait_send()


def attn_grads_everywhere(attended, d_one, ln_one, d_qkv, totals, d_mod):
    count, width = attended.shape
    f32, bf16 = jnp.float32, jnp.bfloat16
    anywhere = pl.BlockSpec(memory_space=pl.ANY)
    inside = pl.BlockSpec(memory_space=pltpu.VMEM)
    images = d_mod.shape[2]
    vec = totals.shape[2:]
    tile = (128, 256)
    return pl.pallas_call(
        attn_grad_kernel,
        in_specs=[anywhere] * 4 + [inside] * 2,
        out_specs=[inside] * 3,
        out_shape=[
            jax.ShapeDtypeStruct((4,) + tile, f32),
            jax.ShapeDtypeStruct(vec, f32),
            jax.ShapeDtypeStruct((4, 2, 2, 2) + d_mod.shape[2:], bf16),
        ],
        scratch_shapes=[
            pltpu.VMEM((count, width), bf16),
            pltpu.VMEM((width, count), bf16),
            pltpu.VMEM((2, count, width), bf16),
            pltpu.VMEM((4, 2, 2, 4, 2) + tile, bf16),
            pltpu.VMEM((4, 2, 4, 2) + tile, bf16),
            pltpu.VMEM((4, 2, 4, 2) + tile, bf16),
            pltpu.VMEM((4, 4, 2) + tile, bf16),
            pltpu.VMEM((4, 4, 2) + tile, bf16),
            pltpu.VMEM((4, 3, 2) + tile, bf16),
            pltpu.VMEM((4, 2) + tile, f32),
            pltpu.VMEM((4,) + tile, bf16),
            pltpu.VMEM((4,) + tile, bf16),
            pltpu.VMEM((2,) + vec, f32),
            pltpu.VMEM((2,) + vec, f32),
            pltpu.VMEM((4, 2) + vec, f32),
            pltpu.VMEM(vec, f32),
            pltpu.VMEM((2,) + vec, f32),
            pltpu.VMEM((2, 2) + d_mod.shape[2:], bf16),
            pltpu.VMEM((2, 2) + d_mod.shape[2:], bf16),
            pltpu.VMEM((2, 2, 2) + d_mod.shape[2:], bf16),
            pltpu.SemaphoreType.DMA((6,)),
            pltpu.SemaphoreType.DMA((6, 6)),
            pltpu.SemaphoreType.DMA((6, 6)),
        ],
        compiler_params=pltpu.CompilerParams(
            vmem_limit_bytes=62 << 20, collective_id=1, has_side_effects=True
        ),
        cost_estimate=pl.CostEstimate(
            flops=8 * count * width * width * 2,
            bytes_accessed=count * width * 12 + width * width * 8,
            transcendentals=0,
        ),
        name="attn_grads",
    )(attended, d_one, ln_one, d_qkv, totals, d_mod)


def swap(pieces, axes):
    return lax.all_to_all(pieces, axes, split_axis=0, concat_axis=0, tiled=False)


def share(value, axes, count):
    return swap(jnp.broadcast_to(value[None], (count,) + value.shape), axes)


BOTH = ("row", "col")


def row_major(value):
    return with_layout_constraint(value, Layout(tuple(range(value.ndim))))


def after(value, *others):
    return lax.optimization_barrier((value,) + others)[0]


def shards(
    tokens,
    condition,
    scale_ids,
    attention_triple_matrix,
    attention_triple_offset,
    qk_gain,
    w_proj,
    b_proj,
    w_fc1,
    b_fc1,
    w_fc2,
    b_fc2,
    w_ada,
    b_ada,
    out_grad,
):
    rows = lax.axis_size("row")
    groups = lax.axis_size("col")
    row = lax.axis_index("row")
    place = lax.axis_index("col")
    everyone = rows * groups
    part = tokens.shape[0]
    width = part * groups
    images_row, length = scale_ids.shape
    images = images_row // groups
    count = images * length
    block = w_proj.shape[0]
    ff_part = b_fc1.shape[0]
    hidden_width = ff_part * groups
    aligned = part % 128 == 0
    blocks = (rows, groups) if aligned else (1, 1)
    f32, bf16 = jnp.float32, jnp.bfloat16

    qkv_parts = lax.all_gather(attention_triple_matrix.transpose(1, 0, 2), BOTH)
    rest_parts = lax.all_gather(
        row_major(jnp.concatenate([w_proj, w_fc1, w_fc2.T], axis=1)), BOTH
    )

    def whole(parts):
        parts = parts.reshape((rows, groups) + parts.shape[1:])
        return parts.transpose(0, 2, 1, 3).reshape(width, groups * parts.shape[-1])

    def spread(wide):
        cols = wide.shape[1] // groups
        pieces = wide.reshape(rows, block, groups, cols).transpose(0, 2, 1, 3)
        return pieces.reshape(everyone, block, cols)

    if not aligned:
        qkv_parts = jnp.stack([whole(qkv_parts[:, index]) for index in range(3)])[None]
        cut = part + ff_part
        rest_parts = jnp.concatenate(
            [
                whole(rest_parts[:, :, :part]),
                whole(rest_parts[:, :, part:cut]),
                whole(rest_parts[:, :, cut:]),
            ],
            axis=1,
        )[None]

    offsets = attention_triple_offset.astype(f32).reshape(-1)
    small = share(
        jnp.concatenate(
            [offsets, b_proj.astype(f32), b_fc1.astype(f32), b_fc2.astype(f32), qk_gain]
        ),
        "col",
        groups,
    )
    cuts = [3 * part, 4 * part, 4 * part + ff_part, 5 * part + ff_part]
    bias_qkv = small[:, : cuts[0]].reshape(groups, 3, part).transpose(1, 0, 2).reshape(3, 1, width)
    bias_proj = small[:, cuts[0] : cuts[1]].reshape(1, width)
    bias_one = small[:, cuts[1] : cuts[2]].reshape(1, hidden_width)
    bias_two = small[:, cuts[2] : cuts[3]].reshape(1, width)
    gain_row = jnp.repeat(small[:, cuts[3] :].reshape(-1), HEAD_DIM)[None]

    cond_float = condition.astype(f32)
    soft = jax.nn.silu(cond_float).astype(bf16)
    soft_all = (
        share(soft, BOTH, everyone)
        .reshape(rows, groups, images_row, part)
        .transpose(0, 2, 1, 3)
        .reshape(rows * images_row, width)
    )
    ada_block = w_ada.shape[1]
    soft_mine = lax.dynamic_slice(
        soft_all, (0, row * ada_block), (rows * images_row, ada_block)
    )
    mod_part = jnp.einsum("ic,scd->isd", soft_mine, w_ada, preferred_element_type=f32)
    mod_part = mod_part + jnp.where(row == 0, b_ada.astype(f32), 0.0)[None]
    modulation = swap(mod_part.reshape(everyone, images, 6, part), BOTH)
    modulation = (
        modulation.reshape(rows, groups, images, 6, part)
        .sum(axis=0)
        .transpose(1, 2, 0, 3)
        .reshape(images, 6, width)
    )

    def to_tokens(features):
        pieces = swap(features.T.reshape(groups, count, part), "col")
        return pieces if aligned else pieces.transpose(1, 0, 2).reshape(1, count, width)

    def to_features(pieces):
        if not aligned:
            pieces = pieces[0].reshape(count, groups, part).transpose(1, 0, 2)
        return swap(pieces, "col").reshape(groups * count, part)

    tok_in = to_tokens(tokens)
    grad_in = to_tokens(out_grad)
    scale_rows = lax.dynamic_slice(scale_ids, (place * images, 0), (images, length))
    query_lanes, key_lanes = mask_lanes(scale_rows)

    ln_one, qkv = qkv_forward(tok_in, modulation, bias_qkv, qkv_parts, blocks, length)
    qkv = qkv.reshape(3, images, length, width)
    attended, log_sums = attention_forward(qkv, gain_row, query_lanes, key_lanes)
    attn_rows = attended.reshape(count, width)
    (
        layer_pieces,
        ln_two,
        hidden,
        d_two,
        d_pre,
        d_one,
        d_res,
        d_attended,
        mod_sums,
        sum_bproj,
        sum_b1,
        sum_b2,
    ) = ffn(
        tok_in,
        attn_rows,
        grad_in,
        modulation,
        bias_proj,
        bias_one,
        bias_two,
        rest_parts,
        blocks,
        length,
    )
    layer_out = to_features(layer_pieces)
    wide_ffn = ffn_grads(ln_two, d_pre, d_two, hidden, blocks)
    if aligned:
        wide_ffn = wide_ffn.reshape(everyone, block, 2 * ff_part)
    else:
        wide_ffn = wide_ffn[0, 0]
        wide_ffn = jnp.concatenate(
            [spread(wide_ffn[:, :hidden_width]), spread(wide_ffn[:, hidden_width:])], axis=2
        )
    d_attended, wide_ffn = lax.optimization_barrier((d_attended, wide_ffn))
    wide_ffn = row_major(lax.psum_scatter(wide_ffn, BOTH, scatter_dimension=0, tiled=False))
    wide_ffn = wide_ffn.astype(f32)
    grad_fc1 = wide_ffn[:, :ff_part]
    grad_fc2 = wide_ffn[:, ff_part:].T

    d_qkv, head_totals = attention_backward(
        qkv,
        gain_row,
        query_lanes,
        key_lanes,
        attended,
        log_sums,
        d_attended.reshape(images, length, width),
    )
    d_qkv, layer_out = lax.optimization_barrier((d_qkv, layer_out))
    d_qkv = d_qkv.reshape(3, count, width)
    token_pieces, first_sums = input_backward(
        d_qkv, tok_in, d_res, modulation, qkv_parts, blocks, length
    )
    grad_tokens = to_features(token_pieces)

    head_totals = head_totals.sum(axis=0)
    totals = jnp.concatenate(
        [
            head_totals[:3].reshape(3, groups, part).transpose(1, 0, 2).reshape(groups, 3 * part),
            sum_bproj.reshape(groups, part),
            sum_b1.reshape(groups, ff_part),
            sum_b2.reshape(groups, part),
            head_totals[3].reshape(-1, HEAD_DIM).sum(axis=1).reshape(groups, -1),
        ],
        axis=1,
    )
    d_mod = jnp.concatenate([first_sums, mod_sums], axis=1).astype(bf16)
    d_mod = d_mod.reshape(images, 6, groups, part).transpose(2, 0, 1, 3)
    if aligned:
        held = totals.shape[1]
        totals = jnp.pad(totals, ((0, 0), (0, -held % 1024)))
        totals = totals.reshape(2, 2, -1, 128).transpose(1, 0, 2, 3)
        d_mod = d_mod.reshape(2, 2, images * 6, part).transpose(1, 0, 2, 3)
        wide_attn, totals, d_mod = attn_grads_everywhere(
            attn_rows, d_one, ln_one, d_qkv, totals, d_mod
        )
        d_mod, grad_tokens = lax.optimization_barrier((d_mod, grad_tokens))
        totals = totals.reshape(-1)[:held]
        d_mod = d_mod.reshape(everyone * images, 6, part)
        grad_proj = wide_attn[0]
        grad_qkv = wide_attn[1:].transpose(1, 0, 2)
    else:
        wide_attn = [
            jnp.einsum("td,tf->df", one, two, preferred_element_type=f32).astype(bf16)
            for one, two in [(attn_rows, d_one)] + [(ln_one, d_qkv[index]) for index in range(3)]
        ]
        wide_attn = jnp.concatenate([spread(wide) for wide in wide_attn], axis=2)
        wide_attn = row_major(lax.psum_scatter(wide_attn, BOTH, scatter_dimension=0, tiled=False))
        wide_attn = wide_attn.astype(f32)
        grad_proj = wide_attn[:, :part]
        grad_qkv = wide_attn[:, part:].reshape(block, 3, part)
        totals = jnp.broadcast_to(totals[None], (rows,) + totals.shape)
        totals = swap(totals.reshape(everyone, -1), BOTH).sum(axis=0)
        d_mod = jnp.broadcast_to(d_mod[None], (rows,) + d_mod.shape)
        d_mod = swap(d_mod.reshape((everyone,) + d_mod.shape[2:]), BOTH)
        d_mod = d_mod.reshape(everyone * images, 6, part)
    grad_ada = jnp.einsum("ic,isd->scd", soft_mine, d_mod, preferred_element_type=f32)
    grad_bada = jnp.sum(d_mod.astype(f32), axis=0)
    d_soft = jnp.einsum("isd,scd->ic", d_mod, w_ada, preferred_element_type=f32)
    d_soft = d_soft.reshape(rows, 1, images_row, ada_block)
    d_soft = jnp.broadcast_to(d_soft, (rows, groups, images_row, ada_block))
    d_soft = swap(d_soft.reshape(everyone, images_row, ada_block), BOTH)
    d_soft = d_soft.reshape(rows, groups, images_row, ada_block).sum(axis=1)
    d_soft = d_soft.transpose(1, 0, 2).reshape(images_row, width)
    d_soft = lax.dynamic_slice(d_soft, (0, place * part), (images_row, part))
    _, silu_pull = jax.vjp(jax.nn.silu, cond_float)
    grad_condition = silu_pull(d_soft)[0].astype(bf16)
    return (
        layer_out.T,
        grad_tokens.T,
        grad_condition,
        grad_qkv,
        totals[: cuts[0]].reshape(3, part),
        totals[cuts[3] :],
        grad_proj,
        totals[cuts[0] : cuts[1]],
        grad_fc1,
        totals[cuts[1] : cuts[2]],
        grad_fc2,
        totals[cuts[2] : cuts[3]],
        grad_ada,
        grad_bada,
    )


def solution(mesh):
    placed = (
        P("col", "row"),
        P("row", "col"),
        P("row", None),
        P("row", None, "col"),
        P(None, "col"),
        P("col"),
        P("row", "col"),
        P("col"),
        P("row", "col"),
        P("col"),
        P("col", "row"),
        P("col"),
        P(None, "row", "col"),
        P(None, "col"),
        P("col", "row"),
    )
    return jax.shard_map(
        shards,
        mesh=mesh,
        in_specs=placed,
        out_specs=(
            P("col", "row"),
            P("col", "row"),
            P("row", "col"),
            P("row", None, "col"),
            P(None, "col"),
            P("col"),
            P("row", "col"),
            P("col"),
            P("row", "col"),
            P("col"),
            P("col", "row"),
            P("col"),
            P(None, "row", "col"),
            P(None, "col"),
        ),
        check_vma=False,
    )
```

```python
import functools
import jax
import jax.numpy as jnp
from jax import lax
from jax.sharding import PartitionSpec as P
from jax.experimental import pallas as pl
from jax.experimental.layout import Layout, with_layout_constraint
from jax.experimental.pallas import tpu as pltpu

HEAD_DIM = 64
PAIR = 2 * HEAD_DIM
NEG = -1024.0
FIRST_EXTRA = 16


def head_sums(values, left):
    first = jnp.sum(jnp.where(left, values, 0.0), axis=-1, keepdims=True)
    second = jnp.sum(jnp.where(left, 0.0, values), axis=-1, keepdims=True)
    return first, second


def unit_of(raw, left):
    first, second = head_sums(raw * raw, left)
    inverse = jnp.where(left, lax.rsqrt(first + 1e-06), lax.rsqrt(second + 1e-06))
    return raw * inverse, inverse


def nt(left_rows, right_rows):
    return lax.dot_general(
        left_rows, right_rows, (((1,), (1,)), ((), ())), preferred_element_type=jnp.float32
    )


def nn(left_rows, right_rows):
    return jnp.dot(left_rows, right_rows, preferred_element_type=jnp.float32)


def split_three(value):
    high = value.astype(jnp.bfloat16)
    rest = value - high.astype(jnp.float32)
    middle = rest.astype(jnp.bfloat16)
    lowest = (rest - middle.astype(jnp.float32)).astype(jnp.bfloat16)
    return high, middle, lowest


def forward_kernel(q_ref, k_ref, v_ref, gain_ref, qm_ref, km_ref, o_ref, lse_ref):
    lane = lax.broadcasted_iota(jnp.int32, q_ref.shape[-2:], 1)
    left = lane < HEAD_DIM
    q_unit, _ = unit_of(q_ref[0, 0], left)
    k_unit, _ = unit_of(k_ref[0, 0], left)
    q_low = (q_unit * gain_ref[...]).astype(jnp.bfloat16)
    k_low = k_unit.astype(jnp.bfloat16)
    v_low = v_ref[0, 0].astype(jnp.bfloat16)
    qm = qm_ref[0]
    km = km_ref[0]
    one = jnp.ones_like(v_low)
    results = []
    for head in range(2):
        mine = left if head == 0 else ~left
        scores = nt(jnp.where(mine, q_low, qm), jnp.where(mine, k_low, km))
        weights = jnp.exp(scores).astype(jnp.bfloat16)
        results.append(nn(weights, jnp.where(mine, v_low, one)))
    totals = jnp.where(left, results[1], results[0])
    lse_ref[0] = jnp.log(totals)
    swapped = pltpu.roll(totals, HEAD_DIM, 1)
    o_ref[0] = (jnp.where(left, results[0], results[1]) / swapped).astype(jnp.bfloat16)


def backward_kernel(
    q_ref, k_ref, v_ref, gain_ref, qm_ref, km_ref, o_ref, lse_ref, do_ref, d_ref, sums_ref
):
    shape = q_ref.shape[-2:]
    lane = lax.broadcasted_iota(jnp.int32, shape, 1)
    left = lane < HEAD_DIM
    spot = lane % HEAD_DIM
    gain = gain_ref[...]
    q_unit, q_inv = unit_of(q_ref[0, 0], left)
    k_unit, k_inv = unit_of(k_ref[0, 0], left)
    q_low = (q_unit * gain).astype(jnp.bfloat16)
    k_low = k_unit.astype(jnp.bfloat16)
    v_low = v_ref[0, 0].astype(jnp.bfloat16)
    d_out = do_ref[0]
    km = km_ref[0]

    def place(base, value):
        high, middle, lowest = split_three(value)
        base = jnp.where(spot == FIRST_EXTRA, high, base)
        base = jnp.where(spot == FIRST_EXTRA + 1, middle, base)
        return jnp.where(spot == FIRST_EXTRA + 2, lowest, base)

    qm = place(qm_ref[0], -lse_ref[0])
    product = d_out.astype(jnp.float32) * o_ref[0].astype(jnp.float32)
    first, second = head_sums(product, left)
    dm = place(jnp.zeros_like(d_out), -jnp.where(left, second, first))
    k_turned = k_low.astype(jnp.float32).T.astype(jnp.bfloat16)
    d_v, d_k, d_q = [], [], []
    for head in range(2):
        mine = left if head == 0 else ~left
        probs = jnp.exp(nt(jnp.where(mine, k_low, km), jnp.where(mine, q_low, qm)))
        d_v.append(nn(probs.astype(jnp.bfloat16), d_out))
        shifted = nt(jnp.where(mine, v_low, km), jnp.where(mine, d_out, dm))
        d_scores = (probs * shifted).astype(jnp.bfloat16)
        d_k.append(nn(d_scores, q_low))
        d_q.append(nn(k_turned[head * HEAD_DIM : (head + 1) * HEAD_DIM], d_scores))
    d_q_low = jnp.concatenate(d_q, axis=0).T
    d_k_low = jnp.where(left, d_k[0], d_k[1])
    d_values = jnp.where(left, d_v[0], d_v[1])
    turned = d_q_low * gain
    first, second = head_sums(turned * q_unit, left)
    d_queries = q_inv * (turned - q_unit * jnp.where(left, first, second))
    first, second = head_sums(d_k_low * k_unit, left)
    d_keys = k_inv * (d_k_low - k_unit * jnp.where(left, first, second))
    parts = []
    for index, value in enumerate((d_queries, d_keys, d_values)):
        rounded = value.astype(jnp.bfloat16)
        d_ref[index, 0] = rounded
        parts.append(jnp.sum(rounded.astype(jnp.float32), axis=0, keepdims=True))
    parts.append(jnp.sum(d_q_low * q_unit, axis=0, keepdims=True))
    parts.append(jnp.zeros((4, PAIR), jnp.float32))
    sums_ref[0] = jnp.concatenate(parts, axis=0)


def mask_lanes(ids):
    spot = jnp.arange(PAIR, dtype=jnp.int32) % HEAD_DIM
    rows = ids[:, :, None]
    queries = (rows == spot).astype(jnp.bfloat16)
    keys = jnp.where((rows > spot) & (spot < FIRST_EXTRA), NEG, 0.0)
    extra = (spot >= FIRST_EXTRA) & (spot < FIRST_EXTRA + 3)
    return queries, jnp.where(extra, 1.0, keys).astype(jnp.bfloat16)


def specs(length):
    def raw(which):
        return pl.BlockSpec((1, 1, length, PAIR), lambda b, h: (which, b, 0, h))

    gain = pl.BlockSpec((1, PAIR), lambda b, h: (0, h))
    lanes = pl.BlockSpec((1, length, PAIR), lambda b, h: (b, 0, 0))
    tokens = pl.BlockSpec((1, length, PAIR), lambda b, h: (b, 0, h))
    return [raw(0), raw(1), raw(2), gain, lanes, lanes], tokens


def attention_forward(qkv, gain_row, qm, km):
    _, images, length, width = qkv.shape
    ins, tokens = specs(length)
    return pl.pallas_call(
        forward_kernel,
        grid=(images, width // PAIR),
        in_specs=ins,
        out_specs=[tokens, tokens],
        out_shape=[
            jax.ShapeDtypeStruct((images, length, width), jnp.bfloat16),
            jax.ShapeDtypeStruct((images, length, width), jnp.float32),
        ],
        compiler_params=pltpu.CompilerParams(vmem_limit_bytes=48 << 20),
        cost_estimate=pl.CostEstimate(
            flops=4 * images * length * length * width * 2, bytes_accessed=images * length * width * 18, transcendentals=images * length * length * 16
        ),
        name="attention_forward",
    )(qkv, qkv, qkv, gain_row, qm, km)


def attention_backward(qkv, gain_row, qm, km, out, lse, d_out):
    _, images, length, width = qkv.shape
    ins, tokens = specs(length)
    return pl.pallas_call(
        backward_kernel,
        grid=(images, width // PAIR),
        in_specs=ins + [tokens, tokens, tokens],
        out_specs=[
            pl.BlockSpec((3, 1, length, PAIR), lambda b, h: (0, b, 0, h)),
            pl.BlockSpec((1, 8, PAIR), lambda b, h: (b, 0, h)),
        ],
        out_shape=[
            jax.ShapeDtypeStruct((3, images, length, width), jnp.bfloat16),
            jax.ShapeDtypeStruct((images, 8, width), jnp.float32),
        ],
        compiler_params=pltpu.CompilerParams(vmem_limit_bytes=56 << 20),
        cost_estimate=pl.CostEstimate(
            flops=10 * images * length * length * width * 2, bytes_accessed=images * length * width * 30, transcendentals=images * length * length * 16
        ),
        name="attention_backward",
    )(qkv, qkv, qkv, gain_row, qm, km, out, lse, d_out)


GELU_RATE = 0.7978845608
GELU_CUBE = 0.7978845608 * 0.044715
FFN_CHUNK = 512


def tile_of(count, want):
    best = 8
    for size in range(8, want + 1, 8):
        if count % size == 0:
            best = size
    return best


def side_by_side(ref):
    return jnp.concatenate([ref[index] for index in range(ref.shape[0])], axis=1)


class Images:
    def __init__(self, rows, length, images):
        start = pl.program_id(0) * rows
        self.first = start // length
        self.second = jnp.minimum((start + rows - 1) // length, images - 1)
        index = lax.broadcasted_iota(jnp.int32, (rows, 1), 0) + start
        self.early = index < (self.first + 1) * length

    def pick(self, table, which):
        return jnp.where(
            self.early,
            table[self.first, which : which + 1],
            table[self.second, which : which + 1],
        )

    def add(self, sums, which, value):
        early = jnp.sum(jnp.where(self.early, value, 0.0), axis=0, keepdims=True)
        late = jnp.sum(jnp.where(self.early, 0.0, value), axis=0, keepdims=True)
        sums[self.first, which : which + 1] += early
        sums[self.second, which : which + 1] += late


def standard_rows(value):
    centered = value - jnp.mean(value, axis=-1, keepdims=True)
    inv_std = lax.rsqrt(jnp.mean(centered * centered, axis=-1, keepdims=True) + 1e-06)
    return centered * inv_std, inv_std


def norm_back(incoming, normed, inv_std):
    average = jnp.mean(incoming, axis=-1, keepdims=True)
    cross = jnp.mean(incoming * normed, axis=-1, keepdims=True)
    return inv_std * (incoming - average - normed * cross)


def block_copies(parts, start, target, sem, row_blocks, col_blocks):
    height = target.shape[0] // row_blocks
    span = target.shape[1] // col_blocks
    for r in range(row_blocks):
        for c in range(col_blocks):
            pltpu.make_async_copy(
                parts.at[r * col_blocks + c, :, pl.ds(start, span)],
                target.at[pl.ds(r * height, height), pl.ds(c * span, span)],
                sem,
            ).start()


def wait_all(target, sem):
    pltpu.make_async_copy(target, target, sem).wait()


def ffn_kernel(
    blocks, length, images,
    x_ref, att_ref, g_ref, mod_ref, bias_proj_ref, bias_one_ref, bias_two_ref, parts_ref,
    out_ref, ln_ref, hidden_ref, d_two_ref, d_pre_ref, d_one_ref, d_res_ref, d_att_ref,
    sums_ref, sum_proj_ref, sum_one_ref, sum_two_ref,
    w_proj, w_one, w_two, slope, sems,
):
    rows = att_ref.shape[0]
    ff = w_one.shape[1]
    first_step = pl.program_id(0) == 0

    @pl.when(first_step)
    def _():
        part = w_proj.shape[1] // blocks[1]
        ff_part = ff // blocks[1]
        block_copies(parts_ref, 0, w_proj, sems.at[0], *blocks)
        block_copies(parts_ref, part, w_one, sems.at[1], *blocks)
        block_copies(parts_ref, part + ff_part, w_two, sems.at[2], *blocks)
        sums_ref[...] = jnp.zeros_like(sums_ref)
        sum_proj_ref[...] = jnp.zeros_like(sum_proj_ref)
        sum_one_ref[...] = jnp.zeros_like(sum_one_ref)
        sum_two_ref[...] = jnp.zeros_like(sum_two_ref)
        wait_all(w_proj, sems.at[0])
        wait_all(w_one, sems.at[1])
        wait_all(w_two, sems.at[2])

    here = Images(rows, length, images)
    gate_attn = here.pick(mod_ref, 2)
    branch_one = nn(att_ref[...], w_proj[...]) + bias_proj_ref[...]
    residual = side_by_side(x_ref).astype(jnp.float32) + gate_attn * branch_one
    normed, inv_std = standard_rows(residual)
    scale = 1.0 + here.pick(mod_ref, 4)
    ln_two = (normed * scale + here.pick(mod_ref, 3)).astype(jnp.bfloat16)
    ln_ref[...] = ln_two
    branch_two = jnp.broadcast_to(bias_two_ref[...], residual.shape)
    for start in range(0, ff, FFN_CHUNK):
        span = slice(start, start + FFN_CHUNK)
        pre = nn(ln_two, w_one[:, span]) + bias_one_ref[:, span]
        square = pre * pre
        turn = jnp.tanh(pre * (GELU_RATE + GELU_CUBE * square))
        half = 0.5 + 0.5 * turn
        value = pre * half
        slope[:, span] = half + value * (1.0 - turn) * (GELU_RATE + 3.0 * GELU_CUBE * square)
        low = value.astype(jnp.bfloat16)
        hidden_ref[:, span] = low
        branch_two += nt(low, w_two[:, span])
    gate_ffn = here.pick(mod_ref, 5)
    result = (residual + gate_ffn * branch_two).astype(jnp.bfloat16)
    part = out_ref.shape[2]
    for index in range(out_ref.shape[0]):
        out_ref[index] = result[:, index * part : (index + 1) * part]
    incoming = side_by_side(g_ref).astype(jnp.float32)
    here.add(sums_ref, 3, incoming * branch_two)
    d_two = (gate_ffn * incoming).astype(jnp.bfloat16)
    d_two_ref[...] = d_two
    sum_two_ref[...] += jnp.sum(d_two.astype(jnp.float32), axis=0, keepdims=True)
    d_back = jnp.zeros_like(residual)
    for start in range(0, ff, FFN_CHUNK):
        span = slice(start, start + FFN_CHUNK)
        d_pre = (nn(d_two, w_two[:, span]) * slope[:, span]).astype(jnp.bfloat16)
        d_pre_ref[:, span] = d_pre
        sum_one_ref[:, span] += jnp.sum(d_pre.astype(jnp.float32), axis=0, keepdims=True)
        d_back += nt(d_pre, w_one[:, span])
    here.add(sums_ref, 1, d_back)
    here.add(sums_ref, 2, d_back * normed)
    d_res = incoming + norm_back(d_back * scale, normed, inv_std)
    d_res_ref[...] = d_res
    here.add(sums_ref, 0, d_res * branch_one)
    d_one = (gate_attn * d_res).astype(jnp.bfloat16)
    d_one_ref[...] = d_one
    sum_proj_ref[...] += jnp.sum(d_one.astype(jnp.float32), axis=0, keepdims=True)
    d_att_ref[...] = nt(d_one, w_proj[...]).astype(jnp.bfloat16)


def ffn(x, attended, g, modulation, bias_proj, bias_one, bias_two, parts, blocks, length):
    groups, count, part = x.shape
    width = groups * part
    ff = bias_one.shape[1]
    images = modulation.shape[0]
    rows = tile_of(count, 272)
    f32, bf16 = jnp.float32, jnp.bfloat16
    pieces = pl.BlockSpec((groups, rows, part), lambda i: (0, i, 0))
    wide = pl.BlockSpec((rows, width), lambda i: (i, 0))
    tall = pl.BlockSpec((rows, ff), lambda i: (i, 0))

    def fixed(*shape):
        return pl.BlockSpec(shape, lambda i: (0,) * len(shape))

    def made(shape, dtype):
        return jax.ShapeDtypeStruct(shape, dtype)

    return pl.pallas_call(
        functools.partial(ffn_kernel, blocks, length, images),
        grid=(count // rows,),
        in_specs=[
            pieces, wide, pieces, fixed(images, 6, width), fixed(1, width), fixed(1, ff),
            fixed(1, width), pl.BlockSpec(memory_space=pl.ANY),
        ],
        out_specs=[
            pieces, wide, tall, wide, tall, wide, wide, wide,
            fixed(images, 4, width), fixed(1, width), fixed(1, ff), fixed(1, width),
        ],
        out_shape=[
            made((groups, count, part), bf16), made((count, width), bf16),
            made((count, ff), bf16), made((count, width), bf16), made((count, ff), bf16),
            made((count, width), bf16), made((count, width), f32), made((count, width), bf16),
            made((images, 4, width), f32), made((1, width), f32), made((1, ff), f32),
            made((1, width), f32),
        ],
        scratch_shapes=[
            pltpu.VMEM((width, width), bf16), pltpu.VMEM((width, ff), bf16),
            pltpu.VMEM((width, ff), bf16), pltpu.VMEM((rows, ff), f32),
            pltpu.SemaphoreType.DMA((3,)),
        ],
        compiler_params=pltpu.CompilerParams(vmem_limit_bytes=62 << 20),
        cost_estimate=pl.CostEstimate(
            flops=4 * count * width * (2 * ff + width),
            bytes_accessed=count * width * 20 + count * ff * 4 + width * (2 * ff + width) * 2,
            transcendentals=count * ff,
        ),
        name="ffn_both",
    )(x, attended, g, modulation, bias_proj, bias_one, bias_two, parts)


def cube_copies(parts, target, sem, row_blocks, col_blocks):
    height = target.shape[1] // row_blocks
    span = target.shape[2] // col_blocks
    for r in range(row_blocks):
        for c in range(col_blocks):
            pltpu.make_async_copy(
                parts.at[r * col_blocks + c],
                target.at[:, pl.ds(r * height, height), pl.ds(c * span, span)],
                sem,
            ).start()


def qkv_kernel(blocks, length, images, x_ref, mod_ref, bias_ref, parts_ref, ln_ref, qkv_ref, weights, sem):
    @pl.when(pl.program_id(0) == 0)
    def _():
        cube_copies(parts_ref, weights, sem.at[0], *blocks)
        wait_all(weights, sem.at[0])

    here = Images(ln_ref.shape[0], length, images)
    normed, _ = standard_rows(side_by_side(x_ref).astype(jnp.float32))
    ln_one = (normed * (1.0 + here.pick(mod_ref, 1)) + here.pick(mod_ref, 0)).astype(jnp.bfloat16)
    ln_ref[...] = ln_one
    for index in range(3):
        qkv_ref[index] = nn(ln_one, weights[index]) + bias_ref[index]


def qkv_forward(x, modulation, bias, parts, blocks, length):
    groups, count, part = x.shape
    width = groups * part
    images = modulation.shape[0]
    rows = tile_of(count, 544)
    return pl.pallas_call(
        functools.partial(qkv_kernel, blocks, length, images),
        grid=(count // rows,),
        in_specs=[
            pl.BlockSpec((groups, rows, part), lambda i: (0, i, 0)),
            pl.BlockSpec((images, 6, width), lambda i: (0, 0, 0)),
            pl.BlockSpec((3, 1, width), lambda i: (0, 0, 0)),
            pl.BlockSpec(memory_space=pl.ANY),
        ],
        out_specs=[
            pl.BlockSpec((rows, width), lambda i: (i, 0)),
            pl.BlockSpec((3, rows, width), lambda i: (0, i, 0)),
        ],
        out_shape=[
            jax.ShapeDtypeStruct((count, width), jnp.bfloat16),
            jax.ShapeDtypeStruct((3, count, width), jnp.float32),
        ],
        scratch_shapes=[
            pltpu.VMEM((3, width, width), jnp.bfloat16),
            pltpu.SemaphoreType.DMA((1,)),
        ],
        compiler_params=pltpu.CompilerParams(vmem_limit_bytes=48 << 20),
        cost_estimate=pl.CostEstimate(
            flops=6 * count * width * width,
            bytes_accessed=count * width * 16 + 6 * width * width,
            transcendentals=count,
        ),
        name="qkv_forward",
    )(x, modulation, bias, parts)


def input_kernel(
    blocks, length, images, d_ref, x_ref, res_ref, mod_ref, parts_ref, out_ref, sums_ref, weights, sem
):
    @pl.when(pl.program_id(0) == 0)
    def _():
        cube_copies(parts_ref, weights, sem.at[0], *blocks)
        sums_ref[...] = jnp.zeros_like(sums_ref)
        wait_all(weights, sem.at[0])

    here = Images(res_ref.shape[0], length, images)
    normed, inv_std = standard_rows(side_by_side(x_ref).astype(jnp.float32))
    d_ln = nt(d_ref[0], weights[0]) + nt(d_ref[1], weights[1]) + nt(d_ref[2], weights[2])
    here.add(sums_ref, 0, d_ln)
    here.add(sums_ref, 1, d_ln * normed)
    scale = 1.0 + here.pick(mod_ref, 1)
    result = (res_ref[...] + norm_back(d_ln * scale, normed, inv_std)).astype(jnp.bfloat16)
    part = out_ref.shape[2]
    for index in range(out_ref.shape[0]):
        out_ref[index] = result[:, index * part : (index + 1) * part]


def input_backward(d_qkv, x, d_res, modulation, parts, blocks, length):
    groups, count, part = x.shape
    width = groups * part
    images = modulation.shape[0]
    rows = tile_of(count, 544)
    pieces = pl.BlockSpec((groups, rows, part), lambda i: (0, i, 0))
    return pl.pallas_call(
        functools.partial(input_kernel, blocks, length, images),
        grid=(count // rows,),
        in_specs=[
            pl.BlockSpec((3, rows, width), lambda i: (0, i, 0)),
            pieces,
            pl.BlockSpec((rows, width), lambda i: (i, 0)),
            pl.BlockSpec((images, 6, width), lambda i: (0, 0, 0)),
            pl.BlockSpec(memory_space=pl.ANY),
        ],
        out_specs=[pieces, pl.BlockSpec((images, 2, width), lambda i: (0, 0, 0))],
        out_shape=[
            jax.ShapeDtypeStruct((groups, count, part), jnp.bfloat16),
            jax.ShapeDtypeStruct((images, 2, width), jnp.float32),
        ],
        scratch_shapes=[
            pltpu.VMEM((3, width, width), jnp.bfloat16),
            pltpu.SemaphoreType.DMA((1,)),
        ],
        compiler_params=pltpu.CompilerParams(vmem_limit_bytes=48 << 20),
        cost_estimate=pl.CostEstimate(
            flops=6 * count * width * width,
            bytes_accessed=count * width * 14 + 6 * width * width,
            transcendentals=count,
        ),
        name="input_backward",
    )(d_qkv, x, d_res, modulation, parts)


def turn_rows(source, target):
    total = source.shape[0]
    step = 640
    for start in range(0, total, step):
        size = min(step, total - start)
        target[:, start : start + size] = source[start : start + size, :].T


def plain_grad_kernel(left, right, out_ref, turned):
    @pl.when(pl.program_id(0) == 0)
    def _():
        turn_rows(left, turned)

    value = nn(turned[...], right[...]).astype(jnp.bfloat16)
    out_ref[...] = value.reshape(out_ref.shape)


def plain_grads(left, right, blocks):
    row_blocks, col_blocks = blocks
    count, width = left.shape
    ff = right.shape[1]
    ff_part = ff // col_blocks
    span = min(512, ff_part)
    inner = ff_part // span
    height = width // row_blocks
    return pl.pallas_call(
        plain_grad_kernel,
        grid=(ff // span,),
        in_specs=[
            pl.BlockSpec((count, width), lambda j: (0, 0)),
            pl.BlockSpec((count, span), lambda j: (0, j)),
        ],
        out_specs=pl.BlockSpec(
            (row_blocks, 1, height, span), lambda j: (0, j // inner, 0, j % inner)
        ),
        out_shape=jax.ShapeDtypeStruct((row_blocks, col_blocks, height, ff_part), jnp.bfloat16),
        scratch_shapes=[pltpu.VMEM((width, count), jnp.bfloat16)],
        compiler_params=pltpu.CompilerParams(vmem_limit_bytes=56 << 20),
        cost_estimate=pl.CostEstimate(
            flops=2 * count * width * ff,
            bytes_accessed=count * width * 2 + count * ff * 2 + width * ff * 2,
            transcendentals=0,
        ),
        name="plain_grads",
    )(left, right)


MESH = pl.DeviceIdType.MESH


class Place:
    def __init__(self):
        row = lax.axis_index("row")
        col = lax.axis_index("col")
        self.z, self.x, self.y, self.k = row // 2, row % 2, col // 2, col % 2

    def other(self, z=None, x=None, y=None, k=None):
        z = self.z if z is None else z
        x = self.x if x is None else x
        y = self.y if y is None else y
        k = self.k if k is None else k
        return (z * 2 + x, y * 2 + k)

    def partners(self):
        near = [self.other(k=1 - self.k), self.other(x=1 - self.x), self.other(y=1 - self.y)]
        return near + [self.other(z=(self.z + step) % 4) for step in (1, 2, 3)]

    def meet(self, *more):
        barrier = pltpu.get_barrier_semaphore()
        partners = self.partners() + list(more)
        for partner in partners:
            pl.semaphore_signal(barrier, inc=1, device_id=partner, device_id_type=MESH)
        pl.semaphore_wait(barrier, len(partners))


def add_into(target, first, second):
    for index in range(first.shape[0]):
        value = first[index].astype(jnp.float32) + second[index].astype(jnp.float32)
        target[index] = value.astype(target.dtype)


def grad_kernel(small, *refs):
    if small:
        att_ref, one_ref, ln_ref, d_ref, totals_ref, mod_ref = refs[:6]
        out_ref, totals_out, mod_out = refs[6:9]
        refs = refs[9:]
        t_core, t_x, t_z, t_y, t_sum, e_core, e_y, e_x = refs[:8]
        refs = refs[8:]
    else:
        two_ref, hidden_ref, out_ref = refs[:3]
        refs = refs[3:]
    left, turned, right, mine, core_in, after_core, x_in, after_x = refs[:8]
    z_in, summed, y_send, y_in, load_sems, send_sems, recv_sems = refs[8:]
    at = Place()

    def load(source, target, index):
        copy = pltpu.make_async_copy(source, target, load_sems.at[index])
        copy.start()
        return copy

    def load_right(p):
        if small:
            source = one_ref if p == 0 else d_ref.at[p - 1]
            return [load(source, right.at[p % 2], 4 * p)]
        part = hidden_ref.shape[1] // 4
        return [
            load(
                hidden_ref.at[:, pl.ds(c * part + p * 256, 256)],
                right.at[p % 2, :, pl.ds(c * 256, 256)],
                4 * p + c,
            )
            for c in range(4)
        ]

    left_first = load(att_ref if small else two_ref, left, 16)
    rights = [load_right(0), load_right(1)]
    at.meet()
    across = at.other(k=1 - at.k)
    beside = at.other(x=1 - at.x)
    over = at.other(y=1 - at.y)
    ahead = [(at.z + step) % 4 for step in (1, 2, 3)]
    sent = []

    def send(flow, which, source, target, device):
        copy = pltpu.make_async_remote_copy(
            src_ref=source,
            dst_ref=target,
            send_sem=send_sems.at[flow, which],
            recv_sem=recv_sems.at[flow, which],
            device_id=device,
            device_id_type=MESH,
        )
        copy.start()
        sent.append(copy)
        return copy

    flights = {}

    def small_zero():
        flights[4, 0] = send(4, 0, totals_ref.at[1 - at.k], t_core, across)
        flights[5, 0] = send(5, 0, mod_ref.at[1 - at.k], e_core.at[at.k], across)

    def small_one():
        flights[4, 0].wait_recv()
        for y in range(2):
            t_core[y] = t_core[y] + totals_ref[at.k, y]
        flights[4, 1] = send(4, 1, t_core, t_x, beside)
        flights[5, 0].wait_recv()
        for y in range(2):
            e_core[at.k, y] = mod_ref[at.k, y]
        flights[5, 1] = send(5, 1, e_core.at[:, 1 - at.y], e_y.at[at.y], over)

    def small_two():
        flights[4, 1].wait_recv()
        for y in range(2):
            t_z[at.z, y] = t_x[y] + t_core[y]
        flights[4, 2] = [
            send(4, 2 + index, t_z.at[at.z], t_z.at[at.z], at.other(z=z))
            for index, z in enumerate(ahead)
        ]
        flights[5, 1].wait_recv()
        for k in range(2):
            e_y[at.y, k] = e_core[k, at.y]
        flights[5, 2] = send(5, 2, e_y, e_x.at[at.x], beside)

    def small_three():
        for copy in flights[4, 2]:
            copy.wait_recv()
        for y in range(2):
            t_sum[y] = (t_z[0, y] + t_z[1, y]) + (t_z[2, y] + t_z[3, y])
        flights[4, 3] = send(4, 5, t_sum.at[1 - at.y], t_y, over)
        flights[5, 2].wait_recv()
        for y in range(2):
            for k in range(2):
                e_x[at.x, y, k] = e_y[y, k]
        mod_out[at.z] = e_x[...]
        flights[5, 3] = [
            send(5, 3 + index, e_x, mod_out.at[at.z], at.other(z=z))
            for index, z in enumerate(ahead)
        ]

    def small_four():
        flights[4, 3].wait_recv()
        totals_out[...] = t_sum[at.y] + t_y[...]
        for copy in flights[5, 3]:
            copy.wait_recv()

    def compute(p):
        for c in range(4):
            span = slice(c * 256, (c + 1) * 256)
            value = nn(turned[...], right[p % 2, :, span]).astype(jnp.bfloat16)
            for r in range(8):
                mine[p, c % 2, r % 2, r // 2, c // 2] = value[r * 128 : (r + 1) * 128]
        flights[p, 0] = send(p, 0, mine.at[p, 1 - at.k], core_in.at[p], across)

    def core_done(p):
        flights[p, 0].wait_recv()
        for x in range(2):
            for z in range(4):
                add_into(after_core.at[p, x, z], mine.at[p, at.k, x, z], core_in.at[p, x, z])

    def x_start(p):
        flights[p, 1] = send(p, 1, after_core.at[p, 1 - at.x], x_in.at[p], beside)

    def x_done(p):
        flights[p, 1].wait_recv()
        for z in range(4):
            add_into(after_x.at[p, z], after_core.at[p, at.x, z], x_in.at[p, z])
        flights[p, 2] = [
            send(p, 2 + index, after_x.at[p, z], z_in.at[p, index], at.other(z=z))
            for index, z in enumerate(ahead)
        ]

    def z_done(p):
        for copy in flights[p, 2]:
            copy.wait_recv()
        for y in range(2):
            value = after_x[p, at.z, y].astype(jnp.float32)
            for index in range(3):
                value = value + z_in[p, index, y].astype(jnp.float32)
            summed[p, y] = value
        y_send[p] = summed[p, 1 - at.y].astype(jnp.bfloat16)
        flights[p, 3] = send(p, 5, y_send.at[p], y_in.at[p], over)

    def y_done(p):
        flights[p, 3].wait_recv()
        out_ref[p] = summed[p, at.y] + y_in[p].astype(jnp.float32)

    def right_ready(p):
        for copy in rights[p]:
            copy.wait()

    hops = [small_zero, small_one, small_two, small_three, small_four]
    if not small:
        hops = [lambda: None] * 5
    hops[0]()
    left_first.wait()
    turn_rows(left, turned)
    if small:
        left_second = load(ln_ref, left, 17)
    right_ready(0)
    compute(0)
    rights.append(load_right(2))
    hops[1]()
    core_done(0)
    x_start(0)
    if small:
        left_second.wait()
        turn_rows(left, turned)
    right_ready(1)
    compute(1)
    rights.append(load_right(3))
    core_done(1)
    hops[2]()
    x_done(0)
    x_start(1)
    right_ready(2)
    compute(2)
    core_done(2)
    hops[3]()
    x_done(1)
    x_start(2)
    z_done(0)
    right_ready(3)
    compute(3)
    core_done(3)
    hops[4]()
    x_done(2)
    x_start(3)
    z_done(1)
    y_done(0)
    z_done(2)
    y_done(1)
    x_done(3)
    y_done(2)
    z_done(3)
    y_done(3)
    for copy in sent:
        copy.wait_send()


def grads_everywhere(count, width, tensors, totals=None, d_mod=None):
    f32, bf16 = jnp.float32, jnp.bfloat16
    small = totals is not None
    anywhere = pl.BlockSpec(memory_space=pl.ANY)
    inside = pl.BlockSpec(memory_space=pltpu.VMEM)
    tile = (128, 256)
    vmem = pltpu.VMEM
    outs = [jax.ShapeDtypeStruct((4,) + tile, f32)]
    flows = []
    if small:
        vec, mod = totals.shape[2:], d_mod.shape[2:]
        outs += [
            jax.ShapeDtypeStruct(vec, f32),
            jax.ShapeDtypeStruct((4, 2, 2, 2) + mod, bf16),
        ]
        flows = [
            vmem((2,) + vec, f32),
            vmem((2,) + vec, f32),
            vmem((4, 2) + vec, f32),
            vmem(vec, f32),
            vmem((2,) + vec, f32),
            vmem((2, 2) + mod, bf16),
            vmem((2, 2) + mod, bf16),
            vmem((2, 2, 2) + mod, bf16),
        ]
    return pl.pallas_call(
        functools.partial(grad_kernel, small),
        in_specs=[anywhere] * len(tensors) + [inside] * (2 if small else 0),
        out_specs=[inside] * len(outs),
        out_shape=outs,
        scratch_shapes=flows
        + [
            vmem((count, width), bf16),
            vmem((width, count), bf16),
            vmem((2, count, width), bf16),
            vmem((4, 2, 2, 4, 2) + tile, bf16),
            vmem((4, 2, 4, 2) + tile, bf16),
            vmem((4, 2, 4, 2) + tile, bf16),
            vmem((4, 4, 2) + tile, bf16),
            vmem((4, 4, 2) + tile, bf16),
            vmem((4, 3, 2) + tile, bf16),
            vmem((4, 2) + tile, f32),
            vmem((4,) + tile, bf16),
            vmem((4,) + tile, bf16),
            pltpu.SemaphoreType.DMA((18,)),
            pltpu.SemaphoreType.DMA((6, 6)),
            pltpu.SemaphoreType.DMA((6, 6)),
        ],
        compiler_params=pltpu.CompilerParams(
            vmem_limit_bytes=62 << 20, collective_id=1 if small else 3, has_side_effects=True
        ),
        cost_estimate=pl.CostEstimate(
            flops=16 * count * width * width,
            bytes_accessed=count * width * 12 + width * width * 8,
            transcendentals=0,
        ),
        name="attn_grads" if small else "second_grads",
    )(*tensors, *((totals, d_mod) if small else ()))


class Sender:
    def __init__(self, send_sems, recv_sems):
        self.send_sems, self.recv_sems, self.copies = send_sems, recv_sems, []

    def __call__(self, source, target, device):
        used = len(self.copies)
        copy = pltpu.make_async_remote_copy(
            src_ref=source,
            dst_ref=target,
            send_sem=self.send_sems.at[used],
            recv_sem=self.recv_sems.at[used],
            device_id=device,
            device_id_type=MESH,
        )
        copy.start()
        self.copies.append(copy)
        return copy

    def finish(self):
        for copy in self.copies:
            copy.wait_send()


START_COPIES = 41
TURN = 640


class Turner:
    def __init__(self, source, target, held_in, held_out, sems, back=False):
        self.source, self.target, self.back = source, target, back
        self.held_in, self.held_out, self.sems = held_in, held_out, sems
        self.total = source.shape[0 if back else 1] // TURN
        self.done, self.loads, self.stores = 0, [], []
        for _ in range(2):
            self.load()

    def slab(self, ref, index, by_rows):
        span = pl.ds(index * TURN, TURN)
        return ref.at[span] if by_rows else ref.at[:, span]

    def load(self):
        index = len(self.loads)
        if index < self.total:
            copy = pltpu.make_async_copy(
                self.slab(self.source, index, self.back),
                self.held_in.at[index % 2],
                self.sems.at[index % 2],
            )
            copy.start()
            self.loads.append(copy)

    def run(self, steps):
        for _ in range(min(steps, self.total - self.done)):
            index = self.done
            self.loads[index].wait()
            if index >= 2:
                self.stores[index - 2].wait()
            self.held_out[index % 2] = self.held_in[index % 2].T
            copy = pltpu.make_async_copy(
                self.held_out.at[index % 2],
                self.slab(self.target, index, not self.back),
                self.sems.at[2 + index % 2],
            )
            copy.start()
            self.stores.append(copy)
            self.done += 1
            self.load()

    def finish(self):
        self.run(self.total)
        for copy in self.stores[-2:]:
            copy.wait()


def start_kernel(
    tok_ref, shard_ref, grad_ref, soft_ref, vec_ref, ada_ref, bias_ref,
    tok_out, parts_out, grad_out, mod_out, vec_out, soft_out,
    s_col, x_send, x_rows, rows_in, partial, p_in, q_sum, z_in, y_send, n_y, k_send,
    g_in, g_out, held,
    send_sems, recv_sems, local_sems, g_sems,
):
    at = Place()
    mine = at.y * 2 + at.k
    turning = Turner(grad_ref, grad_out, g_in, g_out, g_sems)
    own_load = pltpu.make_async_copy(tok_ref.at[mine], held.at[0], local_sems.at[0])
    own_tokens = pltpu.make_async_copy(held.at[0], tok_out.at[mine], local_sems.at[2])
    side_load = pltpu.make_async_copy(
        tok_ref.at[at.y * 2 + 1 - at.k], held.at[1], local_sems.at[3]
    )
    own_shard = pltpu.make_async_copy(
        shard_ref, parts_out.at[at.z, at.x, at.y, at.k], local_sems.at[1]
    )
    own_shard.start()
    own_load.start()
    side_load.start()
    at.meet(at.other(y=1 - at.y, k=1 - at.k))
    across = at.other(k=1 - at.k)
    beside = at.other(x=1 - at.x)
    over = at.other(y=1 - at.y)
    ahead = [(at.z + step) % 4 for step in (1, 2, 3)]
    send = Sender(send_sems, recv_sems)
    length = tok_ref.shape[1] // 4
    arrivals = []

    def tokens_over(index):
        span = pl.ds(index * length, length)
        for k in (at.k, 1 - at.k):
            source = tok_ref.at[(1 - at.y) * 2 + k, span]
            arrivals.append(send(source, tok_out.at[mine, span], at.other(y=1 - at.y, k=k)))

    zs, xs, ys = pl.ds(0, 4), pl.ds(0, 2), pl.ds(0, 2)

    def forward(block, device):
        return send(parts_out.at[block], parts_out.at[block], device)

    def to_ahead(s):
        return [forward((at.z, at.x, ys, at.k, s), at.other(z=z)) for z in ahead]

    def all_in(copies):
        for copy in copies:
            copy.wait_recv()

    shard_y = [
        send(shard_ref.at[s], parts_out.at[at.z, at.x, at.y, at.k, s], over) for s in range(3)
    ]
    s_col[at.y, at.k] = soft_ref[...]
    vec_out[at.y, at.k] = vec_ref[...]
    soft_k = send(soft_ref, s_col.at[at.y, at.k], across)
    vec_k = send(vec_ref, vec_out.at[at.y, at.k], across)
    tokens_over(0)
    soft_k.wait_recv()
    vec_k.wait_recv()
    soft_y = send(s_col.at[at.y], s_col.at[at.y], over)
    vec_y = send(vec_out.at[at.y], vec_out.at[at.y], over)
    own_shard.wait()
    all_in(shard_y)
    shard_z, shard_x, shard_k = [to_ahead(0)], [], []

    def next_x(s):
        all_in(shard_z[s])
        shard_x.append(forward((zs, at.x, ys, at.k, s), beside))
        if s < 2:
            shard_z.append(to_ahead(s + 1))

    def next_k(s):
        shard_x[s].wait_recv()
        shard_k.append(forward((zs, xs, ys, at.k, s), across))

    own_load.wait()
    own_tokens.start()
    side_load.wait()
    arrivals.append(send(held.at[1], tok_out.at[mine], across))
    soft_y.wait_recv()
    vec_y.wait_recv()
    for z in range(4):
        x_send[z] = s_col[z // 2, z % 2, 1 - at.x]
        x_rows[at.x, z] = s_col[z // 2, z % 2, at.x]
    soft_x = send(x_send, x_rows.at[at.x], beside)
    tokens_over(1)
    turning.run(1)
    soft_x.wait_recv()
    for x in range(2):
        rows_in[at.z, x] = x_rows[x, at.z]
    soft_z = [send(x_rows.at[xs, z], rows_in.at[at.z], at.other(z=z)) for z in ahead]
    turning.run(2)
    all_in(soft_z)
    soft = jnp.concatenate([rows_in[r // 2, r % 2] for r in range(8)], axis=0)
    soft_out[...] = soft
    for part in range(6):
        value = nn(soft, ada_ref[part])
        for r in range(8):
            partial[r % 2, r // 2, part] = value[r * 16 : (r + 1) * 16]
    mod_x = send(partial.at[1 - at.x], p_in, beside)
    tokens_over(2)
    next_x(0)
    turning.run(2)
    mod_x.wait_recv()
    for z in range(4):
        for part in range(6):
            q_sum[z, part] = partial[at.x, z, part] + p_in[z, part]
    mod_z = [send(q_sum.at[z], z_in.at[at.z], at.other(z=z)) for z in ahead]
    for part in range(6):
        z_in[at.z, part] = q_sum[at.z, part]
    turning.run(3)
    next_x(1)
    all_in(mod_z)
    for part in range(6):
        value = (z_in[0, part] + z_in[1, part]) + (z_in[2, part] + z_in[3, part])
        value = value + bias_ref[part : part + 1]
        for y in range(2):
            y_send[y, part] = value[y * 8 : (y + 1) * 8]
    mod_y = send(y_send.at[1 - at.y], n_y.at[at.y], over)
    tokens_over(3)
    for part in range(6):
        n_y[at.y, part] = y_send[at.y, part]
    next_k(0)
    turning.run(2)
    next_x(2)
    mod_y.wait_recv()
    for y in range(2):
        for part in range(6):
            for k in range(2):
                k_send[k, y, part] = n_y[y, part, k * 4 : (k + 1) * 4]
    mod_k = send(k_send.at[1 - at.k], mod_out.at[at.k], across)
    for y in range(2):
        for part in range(6):
            mod_out[at.k, y, part] = k_send[at.k, y, part]
    next_k(1)
    turning.run(3)
    next_k(2)
    turning.finish()
    mod_k.wait_recv()
    all_in(arrivals)
    all_in(shard_k)
    own_tokens.wait()
    send.finish()


def start_everything(tok_pieces, shard, grad, soft, vec, w_ada, b_ada):
    f32, bf16 = jnp.float32, jnp.bfloat16
    anywhere = pl.BlockSpec(memory_space=pl.ANY)
    inside = pl.BlockSpec(memory_space=pltpu.VMEM)
    six = (6, 16, 256)
    vmem = pltpu.VMEM
    return pl.pallas_call(
        start_kernel,
        in_specs=[anywhere, inside, anywhere] + [inside] * 4,
        out_specs=[anywhere, inside, anywhere] + [inside] * 3,
        out_shape=[
            jax.ShapeDtypeStruct(tok_pieces.shape, bf16),
            jax.ShapeDtypeStruct((4, 2, 2, 2) + shard.shape, bf16),
            jax.ShapeDtypeStruct(grad.shape[::-1], bf16),
            jax.ShapeDtypeStruct((2, 2, 6, 4, 256), f32),
            jax.ShapeDtypeStruct((2, 2) + vec.shape, f32),
            jax.ShapeDtypeStruct((128, 128), bf16),
        ],
        scratch_shapes=[
            vmem((2, 2) + soft.shape, bf16),
            vmem((4, 16, 128), bf16),
            vmem((2, 4, 16, 128), bf16),
            vmem((4, 2, 16, 128), bf16),
            vmem((2, 4) + six, f32),
            vmem((4,) + six, f32),
            vmem((4,) + six, f32),
            vmem((4,) + six, f32),
            vmem((2, 6, 8, 256), f32),
            vmem((2, 6, 8, 256), f32),
            vmem((2, 2, 6, 4, 256), f32),
            vmem((2, grad.shape[0], TURN), bf16),
            vmem((2, TURN, grad.shape[0]), bf16),
            vmem((2,) + tok_pieces.shape[1:], bf16),
            pltpu.SemaphoreType.DMA((START_COPIES,)),
            pltpu.SemaphoreType.DMA((START_COPIES,)),
            pltpu.SemaphoreType.DMA((4,)),
            pltpu.SemaphoreType.DMA((4,)),
        ],
        compiler_params=pltpu.CompilerParams(
            vmem_limit_bytes=60 << 20, collective_id=2, has_side_effects=True
        ),
        cost_estimate=pl.CostEstimate(
            flops=100_000_000_000, bytes_accessed=30_000_000, transcendentals=0
        ),
        name="start_exchange",
    )(tok_pieces, shard, grad, soft, vec, w_ada, b_ada)


def swap(pieces, axes):
    return lax.all_to_all(pieces, axes, split_axis=0, concat_axis=0, tiled=False)


def share(value, axes, count):
    return swap(jnp.broadcast_to(value[None], (count,) + value.shape), axes)


BOTH = ("row", "col")


def row_major(value):
    return with_layout_constraint(value, Layout(tuple(range(value.ndim))))


def after(value, *others):
    return lax.optimization_barrier((value,) + others)[0]


def shards(
    tokens,
    condition,
    scale_ids,
    attention_triple_matrix,
    attention_triple_offset,
    qk_gain,
    w_proj,
    b_proj,
    w_fc1,
    b_fc1,
    w_fc2,
    b_fc2,
    w_ada,
    b_ada,
    out_grad,
):
    rows = lax.axis_size("row")
    groups = lax.axis_size("col")
    row = lax.axis_index("row")
    place = lax.axis_index("col")
    everyone = rows * groups
    part = tokens.shape[0]
    width = part * groups
    images_row, length = scale_ids.shape
    images = images_row // groups
    count = images * length
    block = w_proj.shape[0]
    ff_part = b_fc1.shape[0]
    hidden_width = ff_part * groups
    aligned = part == 256 and (rows, groups) == (8, 4)
    blocks = (rows, groups) if aligned else (1, 1)
    f32, bf16 = jnp.float32, jnp.bfloat16

    rest_parts = lax.all_gather(
        row_major(jnp.concatenate([w_proj, w_fc1, w_fc2.T], axis=1)), BOTH
    )

    def whole(parts):
        parts = parts.reshape((rows, groups) + parts.shape[1:])
        return parts.transpose(0, 2, 1, 3).reshape(width, groups * parts.shape[-1])

    def spread(wide):
        cols = wide.shape[1] // groups
        pieces = wide.reshape(rows, block, groups, cols).transpose(0, 2, 1, 3)
        return pieces.reshape(everyone, block, cols)

    offsets = attention_triple_offset.astype(f32).reshape(-1)
    vector = jnp.concatenate(
        [offsets, b_proj.astype(f32), b_fc1.astype(f32), b_fc2.astype(f32), qk_gain]
    )
    ada_block = w_ada.shape[1]
    cond_float = condition.astype(f32)
    soft = jax.nn.silu(cond_float).astype(bf16)
    def to_tokens(features):
        pieces = swap(features.T.reshape(groups, count, part), "col")
        return pieces if aligned else pieces.transpose(1, 0, 2).reshape(1, count, width)

    def to_features(pieces):
        if not aligned:
            pieces = pieces[0].reshape(count, groups, part).transpose(1, 0, 2)
        return swap(pieces, "col").reshape(groups * count, part)

    if aligned:
        held = vector.shape[0]
        tok_in, qkv_parts, grad_in, modulation, small, soft_mine = start_everything(
            tokens.T.reshape(groups, count, part),
            attention_triple_matrix.transpose(1, 0, 2),
            out_grad,
            soft.reshape(images_row, 2, ada_block).transpose(1, 0, 2),
            jnp.pad(vector, (0, -held % 1024)).reshape(-1, 128),
            w_ada,
            b_ada.astype(f32),
        )
        qkv_parts = qkv_parts.reshape(everyone, 3, block, part)
        modulation = modulation.transpose(3, 2, 1, 0, 4).reshape(images, 6, width)
        small = small.reshape(groups, -1)[:, :held]
        grad_in = swap(grad_in.reshape(groups, count, part), "col")
    else:
        qkv_parts = lax.all_gather(attention_triple_matrix.transpose(1, 0, 2), BOTH)
        qkv_parts = jnp.stack([whole(qkv_parts[:, index]) for index in range(3)])[None]
        cut = part + ff_part
        rest_parts = jnp.concatenate(
            [
                whole(rest_parts[:, :, :part]),
                whole(rest_parts[:, :, part:cut]),
                whole(rest_parts[:, :, cut:]),
            ],
            axis=1,
        )[None]

        small = share(vector, "col", groups)
        soft_all = (
            share(soft, BOTH, everyone)
            .reshape(rows, groups, images_row, part)
            .transpose(0, 2, 1, 3)
            .reshape(rows * images_row, width)
        )
        soft_mine = lax.dynamic_slice(
            soft_all, (0, row * ada_block), (rows * images_row, ada_block)
        )
        mod_part = jnp.einsum("ic,scd->isd", soft_mine, w_ada, preferred_element_type=f32)
        mod_part = mod_part + jnp.where(row == 0, b_ada.astype(f32), 0.0)[None]
        modulation = swap(mod_part.reshape(everyone, images, 6, part), BOTH)
        modulation = (
            modulation.reshape(rows, groups, images, 6, part)
            .sum(axis=0)
            .transpose(1, 2, 0, 3)
            .reshape(images, 6, width)
        )

        tok_in = to_tokens(tokens)
        grad_in = to_tokens(out_grad)
    cuts = [3 * part, 4 * part, 4 * part + ff_part, 5 * part + ff_part]
    bias_qkv = small[:, : cuts[0]].reshape(groups, 3, part).transpose(1, 0, 2).reshape(3, 1, width)
    bias_proj = small[:, cuts[0] : cuts[1]].reshape(1, width)
    bias_one = small[:, cuts[1] : cuts[2]].reshape(1, hidden_width)
    bias_two = small[:, cuts[2] : cuts[3]].reshape(1, width)
    gain_row = jnp.repeat(small[:, cuts[3] :].reshape(-1), HEAD_DIM)[None]

    scale_rows = lax.dynamic_slice(scale_ids, (place * images, 0), (images, length))
    query_lanes, key_lanes = mask_lanes(scale_rows)

    ln_one, qkv = qkv_forward(tok_in, modulation, bias_qkv, qkv_parts, blocks, length)
    qkv = qkv.reshape(3, images, length, width)
    attended, log_sums = attention_forward(qkv, gain_row, query_lanes, key_lanes)
    attn_rows = attended.reshape(count, width)
    (
        layer_pieces,
        ln_two,
        hidden,
        d_two,
        d_pre,
        d_one,
        d_res,
        d_attended,
        mod_sums,
        sum_bproj,
        sum_b1,
        sum_b2,
    ) = ffn(
        tok_in,
        attn_rows,
        grad_in,
        modulation,
        bias_proj,
        bias_one,
        bias_two,
        rest_parts,
        blocks,
        length,
    )
    layer_out = to_features(layer_pieces)
    if aligned:
        wide_one = plain_grads(ln_two, d_pre, blocks).reshape(everyone, block, ff_part)
        wide_one, d_two = lax.optimization_barrier((wide_one, d_two))
    else:
        wide_one = spread(plain_grads(ln_two, d_pre, blocks)[0, 0])
    wide_one = row_major(lax.psum_scatter(wide_one, BOTH, scatter_dimension=0, tiled=False))
    grad_fc1 = wide_one.astype(f32)
    if aligned:
        (grad_fc2,) = grads_everywhere(count, width, (d_two, hidden))
        grad_fc2 = grad_fc2.transpose(0, 2, 1).reshape(ff_part, block)
        d_attended, grad_fc2 = lax.optimization_barrier((d_attended, grad_fc2))
    else:
        wide_two = spread(plain_grads(d_two, hidden, blocks)[0, 0])
        wide_two = row_major(lax.psum_scatter(wide_two, BOTH, scatter_dimension=0, tiled=False))
        grad_fc2 = wide_two.astype(f32).T
    d_qkv, head_totals = attention_backward(
        qkv,
        gain_row,
        query_lanes,
        key_lanes,
        attended,
        log_sums,
        d_attended.reshape(images, length, width),
    )
    d_qkv, layer_out = lax.optimization_barrier((d_qkv, layer_out))
    d_qkv = d_qkv.reshape(3, count, width)
    token_pieces, first_sums = input_backward(
        d_qkv, tok_in, d_res, modulation, qkv_parts, blocks, length
    )
    grad_tokens = to_features(token_pieces)

    head_totals = head_totals.sum(axis=0)
    totals = jnp.concatenate(
        [
            head_totals[:3].reshape(3, groups, part).transpose(1, 0, 2).reshape(groups, 3 * part),
            sum_bproj.reshape(groups, part),
            sum_b1.reshape(groups, ff_part),
            sum_b2.reshape(groups, part),
            head_totals[3].reshape(-1, HEAD_DIM).sum(axis=1).reshape(groups, -1),
        ],
        axis=1,
    )
    d_mod = jnp.concatenate([first_sums, mod_sums], axis=1).astype(bf16)
    d_mod = d_mod.reshape(images, 6, groups, part).transpose(2, 0, 1, 3)
    if aligned:
        held = totals.shape[1]
        totals = jnp.pad(totals, ((0, 0), (0, -held % 1024)))
        totals = totals.reshape(2, 2, -1, 128).transpose(1, 0, 2, 3)
        d_mod = d_mod.reshape(2, 2, images * 6, part).transpose(1, 0, 2, 3)
        wide_attn, totals, d_mod = grads_everywhere(
            count, width, (attn_rows, d_one, ln_one, d_qkv), totals, d_mod
        )
        d_mod, grad_tokens = lax.optimization_barrier((d_mod, grad_tokens))
        totals = totals.reshape(-1)[:held]
        d_mod = d_mod.reshape(everyone * images, 6, part)
        grad_proj = wide_attn[0]
        grad_qkv = wide_attn[1:].transpose(1, 0, 2)
    else:
        wide_attn = [
            jnp.einsum("td,tf->df", one, two, preferred_element_type=f32).astype(bf16)
            for one, two in [(attn_rows, d_one)] + [(ln_one, d_qkv[index]) for index in range(3)]
        ]
        wide_attn = jnp.concatenate([spread(wide) for wide in wide_attn], axis=2)
        wide_attn = row_major(lax.psum_scatter(wide_attn, BOTH, scatter_dimension=0, tiled=False))
        wide_attn = wide_attn.astype(f32)
        grad_proj = wide_attn[:, :part]
        grad_qkv = wide_attn[:, part:].reshape(block, 3, part)
        totals = jnp.broadcast_to(totals[None], (rows,) + totals.shape)
        totals = swap(totals.reshape(everyone, -1), BOTH).sum(axis=0)
        d_mod = jnp.broadcast_to(d_mod[None], (rows,) + d_mod.shape)
        d_mod = swap(d_mod.reshape((everyone,) + d_mod.shape[2:]), BOTH)
        d_mod = d_mod.reshape(everyone * images, 6, part)
    grad_ada = jnp.einsum("ic,isd->scd", soft_mine, d_mod, preferred_element_type=f32)
    grad_bada = jnp.sum(d_mod.astype(f32), axis=0)
    d_soft = jnp.einsum("isd,scd->ic", d_mod, w_ada, preferred_element_type=f32)
    d_soft = d_soft.reshape(rows, 1, images_row, ada_block)
    d_soft = jnp.broadcast_to(d_soft, (rows, groups, images_row, ada_block))
    d_soft = swap(d_soft.reshape(everyone, images_row, ada_block), BOTH)
    d_soft = d_soft.reshape(rows, groups, images_row, ada_block).sum(axis=1)
    d_soft = d_soft.transpose(1, 0, 2).reshape(images_row, width)
    d_soft = lax.dynamic_slice(d_soft, (0, place * part), (images_row, part))
    _, silu_pull = jax.vjp(jax.nn.silu, cond_float)
    grad_condition = silu_pull(d_soft)[0].astype(bf16)
    return (
        layer_out.T,
        grad_tokens.T,
        grad_condition,
        grad_qkv,
        totals[: cuts[0]].reshape(3, part),
        totals[cuts[3] :],
        grad_proj,
        totals[cuts[0] : cuts[1]],
        grad_fc1,
        totals[cuts[1] : cuts[2]],
        grad_fc2,
        totals[cuts[2] : cuts[3]],
        grad_ada,
        grad_bada,
    )


def solution(mesh):
    placed = (
        P("col", "row"),
        P("row", "col"),
        P("row", None),
        P("row", None, "col"),
        P(None, "col"),
        P("col"),
        P("row", "col"),
        P("col"),
        P("row", "col"),
        P("col"),
        P("col", "row"),
        P("col"),
        P(None, "row", "col"),
        P(None, "col"),
        P("col", "row"),
    )
    return jax.shard_map(
        shards,
        mesh=mesh,
        in_specs=placed,
        out_specs=(
            P("col", "row"),
            P("col", "row"),
            P("row", "col"),
            P("row", None, "col"),
            P(None, "col"),
            P("col"),
            P("row", "col"),
            P("col"),
            P("row", "col"),
            P("col"),
            P("col", "row"),
            P("col"),
            P(None, "row", "col"),
            P(None, "col"),
        ),
        check_vma=False,
    )
```

```python
import functools
import jax
import jax.numpy as jnp
from jax import lax
from jax.sharding import PartitionSpec as P
from jax.experimental import pallas as pl
from jax.experimental.layout import Layout, with_layout_constraint
from jax.experimental.pallas import tpu as pltpu

HEAD_DIM = 64
PAIR = 2 * HEAD_DIM
NEG = -1024.0
FIRST_EXTRA = 16


def head_sums(values, left):
    first = jnp.sum(jnp.where(left, values, 0.0), axis=-1, keepdims=True)
    second = jnp.sum(jnp.where(left, 0.0, values), axis=-1, keepdims=True)
    return first, second


def unit_of(raw, left):
    first, second = head_sums(raw * raw, left)
    inverse = jnp.where(left, lax.rsqrt(first + 1e-06), lax.rsqrt(second + 1e-06))
    return raw * inverse, inverse


def nt(left_rows, right_rows):
    return lax.dot_general(
        left_rows, right_rows, (((1,), (1,)), ((), ())), preferred_element_type=jnp.float32
    )


def nn(left_rows, right_rows):
    return jnp.dot(left_rows, right_rows, preferred_element_type=jnp.float32)


def split_three(value):
    high = value.astype(jnp.bfloat16)
    rest = value - high.astype(jnp.float32)
    middle = rest.astype(jnp.bfloat16)
    lowest = (rest - middle.astype(jnp.float32)).astype(jnp.bfloat16)
    return high, middle, lowest


def forward_kernel(q_ref, k_ref, v_ref, gain_ref, qm_ref, km_ref, o_ref, lse_ref):
    lane = lax.broadcasted_iota(jnp.int32, q_ref.shape[-2:], 1)
    left = lane < HEAD_DIM
    q_unit, _ = unit_of(q_ref[0, 0], left)
    k_unit, _ = unit_of(k_ref[0, 0], left)
    q_low = (q_unit * gain_ref[...]).astype(jnp.bfloat16)
    k_low = k_unit.astype(jnp.bfloat16)
    v_low = v_ref[0, 0].astype(jnp.bfloat16)
    qm = qm_ref[0]
    km = km_ref[0]
    one = jnp.ones_like(v_low)
    results = []
    for head in range(2):
        mine = left if head == 0 else ~left
        scores = nt(jnp.where(mine, q_low, qm), jnp.where(mine, k_low, km))
        weights = jnp.exp(scores).astype(jnp.bfloat16)
        results.append(nn(weights, jnp.where(mine, v_low, one)))
    totals = jnp.where(left, results[1], results[0])
    lse_ref[0] = jnp.log(totals)
    swapped = pltpu.roll(totals, HEAD_DIM, 1)
    o_ref[0] = (jnp.where(left, results[0], results[1]) / swapped).astype(jnp.bfloat16)


def backward_kernel(
    q_ref, k_ref, v_ref, gain_ref, qm_ref, km_ref, o_ref, lse_ref, do_ref, d_ref, sums_ref
):
    shape = q_ref.shape[-2:]
    lane = lax.broadcasted_iota(jnp.int32, shape, 1)
    left = lane < HEAD_DIM
    spot = lane % HEAD_DIM
    gain = gain_ref[...]
    q_unit, q_inv = unit_of(q_ref[0, 0], left)
    k_unit, k_inv = unit_of(k_ref[0, 0], left)
    q_low = (q_unit * gain).astype(jnp.bfloat16)
    k_low = k_unit.astype(jnp.bfloat16)
    v_low = v_ref[0, 0].astype(jnp.bfloat16)
    d_out = do_ref[0]
    km = km_ref[0]

    def place(base, value):
        high, middle, lowest = split_three(value)
        base = jnp.where(spot == FIRST_EXTRA, high, base)
        base = jnp.where(spot == FIRST_EXTRA + 1, middle, base)
        return jnp.where(spot == FIRST_EXTRA + 2, lowest, base)

    qm = place(qm_ref[0], -lse_ref[0])
    zero = jnp.zeros_like(d_out)
    k_turned = k_low.astype(jnp.float32).T.astype(jnp.bfloat16)
    d_v, d_k, d_q = [], [], []
    for head in range(2):
        mine = left if head == 0 else ~left
        probs = jnp.exp(nt(jnp.where(mine, k_low, km), jnp.where(mine, q_low, qm)))
        d_v.append(nn(probs.astype(jnp.bfloat16), d_out))
        product = probs * nt(v_low, jnp.where(mine, d_out, zero))
        expected = jnp.sum(product, axis=0, keepdims=True)
        d_scores = (product - probs * expected).astype(jnp.bfloat16)
        d_k.append(nn(d_scores, q_low))
        d_q.append(nn(k_turned[head * HEAD_DIM : (head + 1) * HEAD_DIM], d_scores))
    d_q_low = jnp.concatenate(d_q, axis=0).T
    d_k_low = jnp.where(left, d_k[0], d_k[1])
    d_values = jnp.where(left, d_v[0], d_v[1])
    turned = d_q_low * gain
    first, second = head_sums(turned * q_unit, left)
    d_queries = q_inv * (turned - q_unit * jnp.where(left, first, second))
    first, second = head_sums(d_k_low * k_unit, left)
    d_keys = k_inv * (d_k_low - k_unit * jnp.where(left, first, second))
    parts = []
    for index, value in enumerate((d_queries, d_keys, d_values)):
        rounded = value.astype(jnp.bfloat16)
        d_ref[index, 0] = rounded
        parts.append(jnp.sum(rounded.astype(jnp.float32), axis=0, keepdims=True))
    parts.append(jnp.sum(d_q_low * q_unit, axis=0, keepdims=True))
    parts.append(jnp.zeros((4, PAIR), jnp.float32))
    sums_ref[0] = jnp.concatenate(parts, axis=0)


def mask_lanes(ids):
    spot = jnp.arange(PAIR, dtype=jnp.int32) % HEAD_DIM
    rows = ids[:, :, None]
    queries = (rows == spot).astype(jnp.bfloat16)
    keys = jnp.where((rows > spot) & (spot < FIRST_EXTRA), NEG, 0.0)
    extra = (spot >= FIRST_EXTRA) & (spot < FIRST_EXTRA + 3)
    return queries, jnp.where(extra, 1.0, keys).astype(jnp.bfloat16)


def specs(length):
    def raw(which):
        return pl.BlockSpec((1, 1, length, PAIR), lambda b, h: (which, b, 0, h))

    gain = pl.BlockSpec((1, PAIR), lambda b, h: (0, h))
    lanes = pl.BlockSpec((1, length, PAIR), lambda b, h: (b, 0, 0))
    tokens = pl.BlockSpec((1, length, PAIR), lambda b, h: (b, 0, h))
    return [raw(0), raw(1), raw(2), gain, lanes, lanes], tokens


def attention_forward(qkv, gain_row, qm, km):
    _, images, length, width = qkv.shape
    ins, tokens = specs(length)
    return pl.pallas_call(
        forward_kernel,
        grid=(images, width // PAIR),
        in_specs=ins,
        out_specs=[tokens, tokens],
        out_shape=[
            jax.ShapeDtypeStruct((images, length, width), jnp.bfloat16),
            jax.ShapeDtypeStruct((images, length, width), jnp.float32),
        ],
        compiler_params=pltpu.CompilerParams(vmem_limit_bytes=48 << 20),
        cost_estimate=pl.CostEstimate(
            flops=4 * images * length * length * width * 2, bytes_accessed=images * length * width * 18, transcendentals=images * length * length * 16
        ),
        name="attention_forward",
    )(qkv, qkv, qkv, gain_row, qm, km)


def attention_backward(qkv, gain_row, qm, km, out, lse, d_out):
    _, images, length, width = qkv.shape
    ins, tokens = specs(length)
    return pl.pallas_call(
        backward_kernel,
        grid=(images, width // PAIR),
        in_specs=ins + [tokens, tokens, tokens],
        out_specs=[
            pl.BlockSpec((3, 1, length, PAIR), lambda b, h: (0, b, 0, h)),
            pl.BlockSpec((1, 8, PAIR), lambda b, h: (b, 0, h)),
        ],
        out_shape=[
            jax.ShapeDtypeStruct((3, images, length, width), jnp.bfloat16),
            jax.ShapeDtypeStruct((images, 8, width), jnp.float32),
        ],
        compiler_params=pltpu.CompilerParams(vmem_limit_bytes=56 << 20),
        cost_estimate=pl.CostEstimate(
            flops=10 * images * length * length * width * 2, bytes_accessed=images * length * width * 30, transcendentals=images * length * length * 16
        ),
        name="attention_backward",
    )(qkv, qkv, qkv, gain_row, qm, km, out, lse, d_out)


GELU_RATE = 0.7978845608
GELU_CUBE = 0.7978845608 * 0.044715
FFN_CHUNK = 1024


def tile_of(count, length, want):
    best = 8
    for size in range(8, want + 1, 8):
        halves = size % 16 == 0 and length % (size // 2) == 0
        if count % size == 0 and (length % size == 0 or halves):
            best = size
    return best


def side_by_side(ref):
    return jnp.concatenate([ref[index] for index in range(ref.shape[0])], axis=1)


class Images:
    def __init__(self, rows, length, images):
        self.unit = rows if length % rows == 0 else rows // 2
        start = pl.program_id(0) * rows
        self.spans = [(first, first + self.unit) for first in range(0, rows, self.unit)]
        self.which = [(start + first) // length for first, _ in self.spans]

    def pick(self, table, column):
        parts = [table[image, column : column + 1] for image in self.which]
        shape = (self.unit, parts[0].shape[1])
        return jnp.concatenate([jnp.broadcast_to(part, shape) for part in parts], axis=0)

    def add(self, sums, column, value):
        for image, (first, last) in zip(self.which, self.spans):
            sums[image, column : column + 1] += jnp.sum(value[first:last], axis=0, keepdims=True)


def standard_rows(value):
    centered = value - jnp.mean(value, axis=-1, keepdims=True)
    inv_std = lax.rsqrt(jnp.mean(centered * centered, axis=-1, keepdims=True) + 1e-06)
    return centered * inv_std, inv_std


def norm_back(incoming, normed, inv_std):
    average = jnp.mean(incoming, axis=-1, keepdims=True)
    cross = jnp.mean(incoming * normed, axis=-1, keepdims=True)
    return inv_std * (incoming - average - normed * cross)


def block_copies(parts, start, target, sem, row_blocks, col_blocks):
    height = target.shape[0] // row_blocks
    span = target.shape[1] // col_blocks
    for r in range(row_blocks):
        for c in range(col_blocks):
            pltpu.make_async_copy(
                parts.at[r * col_blocks + c, :, pl.ds(start, span)],
                target.at[pl.ds(r * height, height), pl.ds(c * span, span)],
                sem,
            ).start()


def wait_all(target, sem):
    pltpu.make_async_copy(target, target, sem).wait()


def ffn_kernel(
    blocks, length, images,
    x_ref, att_ref, g_ref, mod_ref, bias_proj_ref, bias_one_ref, bias_two_ref, parts_ref,
    out_ref, ln_ref, hidden_ref, d_two_ref, d_pre_ref, d_one_ref, d_res_ref, d_att_ref,
    sums_ref, sum_proj_ref, sum_one_ref, sum_two_ref,
    w_proj, w_one, w_two, slope, sems,
):
    rows = att_ref.shape[0]
    ff = w_one.shape[1]
    first_step = pl.program_id(0) == 0

    @pl.when(first_step)
    def _():
        part = w_proj.shape[1] // blocks[1]
        ff_part = ff // blocks[1]
        block_copies(parts_ref, 0, w_proj, sems.at[0], *blocks)
        block_copies(parts_ref, part, w_one, sems.at[1], *blocks)
        block_copies(parts_ref, part + ff_part, w_two, sems.at[2], *blocks)
        sums_ref[...] = jnp.zeros_like(sums_ref)
        sum_proj_ref[...] = jnp.zeros_like(sum_proj_ref)
        sum_one_ref[...] = jnp.zeros_like(sum_one_ref)
        sum_two_ref[...] = jnp.zeros_like(sum_two_ref)
        wait_all(w_proj, sems.at[0])

    here = Images(rows, length, images)
    gate_attn = here.pick(mod_ref, 2)
    branch_one = nn(att_ref[...], w_proj[...]) + bias_proj_ref[...]
    residual = side_by_side(x_ref).astype(jnp.float32) + gate_attn * branch_one
    normed, inv_std = standard_rows(residual)
    scale = 1.0 + here.pick(mod_ref, 4)
    ln_two = (normed * scale + here.pick(mod_ref, 3)).astype(jnp.bfloat16)
    ln_ref[...] = ln_two

    @pl.when(first_step)
    def _():
        wait_all(w_one, sems.at[1])
        wait_all(w_two, sems.at[2])

    branch_two = jnp.broadcast_to(bias_two_ref[...], residual.shape)
    for start in range(0, ff, FFN_CHUNK):
        span = slice(start, start + FFN_CHUNK)
        pre = nn(ln_two, w_one[:, span]) + bias_one_ref[:, span]
        square = pre * pre
        turn = jnp.tanh(pre * (GELU_RATE + GELU_CUBE * square))
        half = 0.5 + 0.5 * turn
        value = pre * half
        slope[:, span] = half + value * (1.0 - turn) * (GELU_RATE + 3.0 * GELU_CUBE * square)
        low = value.astype(jnp.bfloat16)
        hidden_ref[:, span] = low
        branch_two += nt(low, w_two[:, span])
    gate_ffn = here.pick(mod_ref, 5)
    result = (residual + gate_ffn * branch_two).astype(jnp.bfloat16)
    part = out_ref.shape[2]
    for index in range(out_ref.shape[0]):
        out_ref[index] = result[:, index * part : (index + 1) * part]
    incoming = side_by_side(g_ref).astype(jnp.float32)
    here.add(sums_ref, 3, incoming * branch_two)
    d_two = (gate_ffn * incoming).astype(jnp.bfloat16)
    d_two_ref[...] = d_two
    sum_two_ref[...] += jnp.sum(d_two.astype(jnp.float32), axis=0, keepdims=True)
    d_back = jnp.zeros_like(residual)
    for start in range(0, ff, FFN_CHUNK):
        span = slice(start, start + FFN_CHUNK)
        d_pre = (nn(d_two, w_two[:, span]) * slope[:, span]).astype(jnp.bfloat16)
        d_pre_ref[:, span] = d_pre
        sum_one_ref[:, span] += jnp.sum(d_pre.astype(jnp.float32), axis=0, keepdims=True)
        d_back += nt(d_pre, w_one[:, span])
    here.add(sums_ref, 1, d_back)
    here.add(sums_ref, 2, d_back * normed)
    d_res = incoming + norm_back(d_back * scale, normed, inv_std)
    d_res_ref[...] = d_res
    here.add(sums_ref, 0, d_res * branch_one)
    d_one = (gate_attn * d_res).astype(jnp.bfloat16)
    d_one_ref[...] = d_one
    sum_proj_ref[...] += jnp.sum(d_one.astype(jnp.float32), axis=0, keepdims=True)
    d_att_ref[...] = nt(d_one, w_proj[...]).astype(jnp.bfloat16)


def ffn(x, attended, g, modulation, bias_proj, bias_one, bias_two, parts, blocks, length):
    groups, count, part = x.shape
    width = groups * part
    ff = bias_one.shape[1]
    images = modulation.shape[0]
    rows = tile_of(count, length, 272)
    f32, bf16 = jnp.float32, jnp.bfloat16
    pieces = pl.BlockSpec((groups, rows, part), lambda i: (0, i, 0))
    wide = pl.BlockSpec((rows, width), lambda i: (i, 0))
    tall = pl.BlockSpec((rows, ff), lambda i: (i, 0))

    def fixed(*shape):
        return pl.BlockSpec(shape, lambda i: (0,) * len(shape))

    def made(shape, dtype):
        return jax.ShapeDtypeStruct(shape, dtype)

    return pl.pallas_call(
        functools.partial(ffn_kernel, blocks, length, images),
        grid=(count // rows,),
        in_specs=[
            pieces, wide, pieces, fixed(images, 6, width), fixed(1, width), fixed(1, ff),
            fixed(1, width), pl.BlockSpec(memory_space=pl.ANY),
        ],
        out_specs=[
            pieces, wide, tall, wide, tall, wide, wide, wide,
            fixed(images, 4, width), fixed(1, width), fixed(1, ff), fixed(1, width),
        ],
        out_shape=[
            made((groups, count, part), bf16), made((count, width), bf16),
            made((count, ff), bf16), made((count, width), bf16), made((count, ff), bf16),
            made((count, width), bf16), made((count, width), f32), made((count, width), bf16),
            made((images, 4, width), f32), made((1, width), f32), made((1, ff), f32),
            made((1, width), f32),
        ],
        scratch_shapes=[
            pltpu.VMEM((width, width), bf16), pltpu.VMEM((width, ff), bf16),
            pltpu.VMEM((width, ff), bf16), pltpu.VMEM((rows, ff), f32),
            pltpu.SemaphoreType.DMA((3,)),
        ],
        compiler_params=pltpu.CompilerParams(vmem_limit_bytes=62 << 20),
        cost_estimate=pl.CostEstimate(
            flops=4 * count * width * (2 * ff + width),
            bytes_accessed=count * width * 20 + count * ff * 4 + width * (2 * ff + width) * 2,
            transcendentals=count * ff,
        ),
        name="ffn_both",
    )(x, attended, g, modulation, bias_proj, bias_one, bias_two, parts)


def cube_copies(parts, target, sem, row_blocks, col_blocks):
    height = target.shape[1] // row_blocks
    span = target.shape[2] // col_blocks
    for r in range(row_blocks):
        for c in range(col_blocks):
            pltpu.make_async_copy(
                parts.at[r * col_blocks + c],
                target.at[:, pl.ds(r * height, height), pl.ds(c * span, span)],
                sem,
            ).start()


def qkv_kernel(blocks, length, images, x_ref, mod_ref, bias_ref, parts_ref, ln_ref, qkv_ref, weights, sem):
    @pl.when(pl.program_id(0) == 0)
    def _():
        cube_copies(parts_ref, weights, sem.at[0], *blocks)
        wait_all(weights, sem.at[0])

    here = Images(ln_ref.shape[0], length, images)
    normed, _ = standard_rows(side_by_side(x_ref).astype(jnp.float32))
    ln_one = (normed * (1.0 + here.pick(mod_ref, 1)) + here.pick(mod_ref, 0)).astype(jnp.bfloat16)
    ln_ref[...] = ln_one
    for index in range(3):
        qkv_ref[index] = nn(ln_one, weights[index]) + bias_ref[index]


def qkv_forward(x, modulation, bias, parts, blocks, length):
    groups, count, part = x.shape
    width = groups * part
    images = modulation.shape[0]
    rows = tile_of(count, length, 272)
    return pl.pallas_call(
        functools.partial(qkv_kernel, blocks, length, images),
        grid=(count // rows,),
        in_specs=[
            pl.BlockSpec((groups, rows, part), lambda i: (0, i, 0)),
            pl.BlockSpec((images, 6, width), lambda i: (0, 0, 0)),
            pl.BlockSpec((3, 1, width), lambda i: (0, 0, 0)),
            pl.BlockSpec(memory_space=pl.ANY),
        ],
        out_specs=[
            pl.BlockSpec((rows, width), lambda i: (i, 0)),
            pl.BlockSpec((3, rows, width), lambda i: (0, i, 0)),
        ],
        out_shape=[
            jax.ShapeDtypeStruct((count, width), jnp.bfloat16),
            jax.ShapeDtypeStruct((3, count, width), jnp.float32),
        ],
        scratch_shapes=[
            pltpu.VMEM((3, width, width), jnp.bfloat16),
            pltpu.SemaphoreType.DMA((1,)),
        ],
        compiler_params=pltpu.CompilerParams(vmem_limit_bytes=48 << 20),
        cost_estimate=pl.CostEstimate(
            flops=6 * count * width * width,
            bytes_accessed=count * width * 16 + 6 * width * width,
            transcendentals=count,
        ),
        name="qkv_forward",
    )(x, modulation, bias, parts)


def input_kernel(
    blocks, length, images, d_ref, x_ref, res_ref, mod_ref, parts_ref, out_ref, sums_ref, weights, sem
):
    @pl.when(pl.program_id(0) == 0)
    def _():
        cube_copies(parts_ref, weights, sem.at[0], *blocks)
        sums_ref[...] = jnp.zeros_like(sums_ref)
        wait_all(weights, sem.at[0])

    here = Images(res_ref.shape[0], length, images)
    normed, inv_std = standard_rows(side_by_side(x_ref).astype(jnp.float32))
    d_ln = nt(d_ref[0], weights[0]) + nt(d_ref[1], weights[1]) + nt(d_ref[2], weights[2])
    here.add(sums_ref, 0, d_ln)
    here.add(sums_ref, 1, d_ln * normed)
    scale = 1.0 + here.pick(mod_ref, 1)
    result = (res_ref[...] + norm_back(d_ln * scale, normed, inv_std)).astype(jnp.bfloat16)
    part = out_ref.shape[2]
    for index in range(out_ref.shape[0]):
        out_ref[index] = result[:, index * part : (index + 1) * part]


def input_backward(d_qkv, x, d_res, modulation, parts, blocks, length):
    groups, count, part = x.shape
    width = groups * part
    images = modulation.shape[0]
    rows = tile_of(count, length, 272)
    pieces = pl.BlockSpec((groups, rows, part), lambda i: (0, i, 0))
    return pl.pallas_call(
        functools.partial(input_kernel, blocks, length, images),
        grid=(count // rows,),
        in_specs=[
            pl.BlockSpec((3, rows, width), lambda i: (0, i, 0)),
            pieces,
            pl.BlockSpec((rows, width), lambda i: (i, 0)),
            pl.BlockSpec((images, 6, width), lambda i: (0, 0, 0)),
            pl.BlockSpec(memory_space=pl.ANY),
        ],
        out_specs=[pieces, pl.BlockSpec((images, 2, width), lambda i: (0, 0, 0))],
        out_shape=[
            jax.ShapeDtypeStruct((groups, count, part), jnp.bfloat16),
            jax.ShapeDtypeStruct((images, 2, width), jnp.float32),
        ],
        scratch_shapes=[
            pltpu.VMEM((3, width, width), jnp.bfloat16),
            pltpu.SemaphoreType.DMA((1,)),
        ],
        compiler_params=pltpu.CompilerParams(vmem_limit_bytes=48 << 20),
        cost_estimate=pl.CostEstimate(
            flops=6 * count * width * width,
            bytes_accessed=count * width * 14 + 6 * width * width,
            transcendentals=count,
        ),
        name="input_backward",
    )(d_qkv, x, d_res, modulation, parts)


def turn_rows(source, target):
    total = source.shape[0]
    step = 640
    for start in range(0, total, step):
        size = min(step, total - start)
        target[:, start : start + size] = source[start : start + size, :].T


def plain_grad_kernel(left, right, out_ref, turned):
    @pl.when(pl.program_id(0) == 0)
    def _():
        turn_rows(left, turned)

    value = nn(turned[...], right[...]).astype(jnp.bfloat16)
    out_ref[...] = value.reshape(out_ref.shape)


def plain_grads(left, right, blocks):
    row_blocks, col_blocks = blocks
    count, width = left.shape
    ff = right.shape[1]
    ff_part = ff // col_blocks
    span = min(512, ff_part)
    inner = ff_part // span
    height = width // row_blocks
    return pl.pallas_call(
        plain_grad_kernel,
        grid=(ff // span,),
        in_specs=[
            pl.BlockSpec((count, width), lambda j: (0, 0)),
            pl.BlockSpec((count, span), lambda j: (0, j)),
        ],
        out_specs=pl.BlockSpec(
            (row_blocks, 1, height, span), lambda j: (0, j // inner, 0, j % inner)
        ),
        out_shape=jax.ShapeDtypeStruct((row_blocks, col_blocks, height, ff_part), jnp.bfloat16),
        scratch_shapes=[pltpu.VMEM((width, count), jnp.bfloat16)],
        compiler_params=pltpu.CompilerParams(vmem_limit_bytes=56 << 20),
        cost_estimate=pl.CostEstimate(
            flops=2 * count * width * ff,
            bytes_accessed=count * width * 2 + count * ff * 2 + width * ff * 2,
            transcendentals=0,
        ),
        name="plain_grads",
    )(left, right)


MESH = pl.DeviceIdType.MESH


TURN = 640


class Turner:
    def __init__(self, source, target, held_in, held_out, sems, back=False, shift=0, ahead=None):
        self.source, self.target, self.back = source, target, back
        self.held_in, self.held_out, self.sems = held_in, held_out, sems
        self.total = source.shape[0 if back else 1] // TURN
        self.done, self.settled, self.loads, self.stores, self.shift = 0, 0, [], [], shift
        self.limit = self.total if ahead is None else ahead
        for _ in range(2):
            self.load()

    def slab(self, ref, index, by_rows):
        span = pl.ds(pl.multiple_of((index + self.shift) % self.total * TURN, TURN), TURN)
        return ref.at[span] if by_rows else ref.at[:, span]

    def load(self):
        index = len(self.loads)
        if index < min(self.limit, self.total):
            copy = pltpu.make_async_copy(
                self.slab(self.source, index, self.back),
                self.held_in.at[index % 2],
                self.sems.at[index % 2],
            )
            copy.start()
            self.loads.append(copy)

    def run(self, steps):
        for _ in range(min(steps, self.total - self.done)):
            index = self.done
            self.loads[index].wait()
            if index - 2 >= self.settled:
                self.stores[index - 2].wait()
                self.settled = index - 1
            self.held_out[index % 2] = self.held_in[index % 2].T
            copy = pltpu.make_async_copy(
                self.held_out.at[index % 2],
                self.slab(self.target, index, not self.back),
                self.sems.at[2 + index % 2],
            )
            copy.start()
            self.stores.append(copy)
            self.done += 1
            self.load()

    def release(self):
        self.limit = self.total
        while len(self.loads) < min(self.done + 2, self.total):
            self.load()

    def settle(self):
        for copy in self.stores[self.settled :]:
            copy.wait()
        self.settled = len(self.stores)

    def finish(self):
        self.run(self.total)
        self.settle()


class Place:
    def __init__(self):
        row = lax.axis_index("row")
        col = lax.axis_index("col")
        self.z, self.x, self.y, self.k = row // 2, row % 2, col // 2, col % 2

    def other(self, z=None, x=None, y=None, k=None):
        z = self.z if z is None else z
        x = self.x if x is None else x
        y = self.y if y is None else y
        k = self.k if k is None else k
        return (z * 2 + x, y * 2 + k)

    def partners(self):
        near = [self.other(k=1 - self.k), self.other(x=1 - self.x), self.other(y=1 - self.y)]
        return near + [self.other(z=(self.z + step) % 4) for step in (1, 2, 3)]

    def meet(self, *more):
        barrier = pltpu.get_barrier_semaphore()
        partners = self.partners() + list(more)
        for partner in partners:
            pl.semaphore_signal(barrier, inc=1, device_id=partner, device_id_type=MESH)
        pl.semaphore_wait(barrier, len(partners))


class Sender:
    def __init__(self, send_sems, recv_sems):
        self.send_sems, self.recv_sems, self.copies = send_sems, recv_sems, []

    def __call__(self, source, target, device):
        used = len(self.copies)
        copy = pltpu.make_async_remote_copy(
            src_ref=source,
            dst_ref=target,
            send_sem=self.send_sems.at[used],
            recv_sem=self.recv_sems.at[used],
            device_id=device,
            device_id_type=MESH,
        )
        copy.start()
        self.copies.append(copy)
        return copy

    def finish(self):
        for copy in self.copies:
            copy.wait_send()


def add_into(target, first, second):
    for index in range(first.shape[0]):
        value = first[index].astype(jnp.float32) + second[index].astype(jnp.float32)
        target[index] = value.astype(target.dtype)


def grad_kernel(small, *refs):
    if small:
        att_ref, one_ref, ln_ref, d_ref, tok_ref, layer_ref, totals_ref, mod_ref, ada_ref = refs[:9]
        out_ref, totals_out, mod_out, soft_out, tok_in, tok_out, layer_out = refs[9:16]
        refs = refs[16:]
        g_own, g_z, g_x, g_turn, g_y, g_sum, g_k, soft_sems = refs[:8]
        refs = refs[8:]
        t_core, t_x, t_z, t_y, t_sum, e_core, e_y, e_x = refs[:8]
        turn_in, turn_out, turn_sems, more_sems = refs[8:12]
        refs = refs[12:]
    else:
        two_ref, hidden_ref, two_left_ref, pre_ref, out_ref, wide_ref, stage, stage_sems = refs[:8]
        refs = refs[8:]
    left, turned, right, mine, core_in, after_core, x_in, after_x = refs[:8]
    z_in, summed, y_send, y_in, load_sems, send_sems, recv_sems = refs[8:]
    at = Place()

    def load(source, target, index):
        copy = pltpu.make_async_copy(source, target, load_sems.at[index])
        copy.start()
        return copy

    def load_right(p):
        if small:
            source = one_ref if p == 0 else d_ref.at[p - 1]
            return [load(source, right.at[p % 2], 4 * p)]
        if p >= 4:
            width = right.shape[2]
            source = pre_ref.at[:, pl.ds((p - 4) * width, width)]
            return [load(source, right.at[p % 2], 16 + p)]
        part = hidden_ref.shape[1] // 4
        return [
            load(
                hidden_ref.at[:, pl.ds(c * part + p * 256, 256)],
                right.at[p % 2, :, pl.ds(c * 256, 256)],
                4 * p + c,
            )
            for c in range(4)
        ]

    if small:
        layer = Turner(layer_ref, layer_out, turn_in.at[0], turn_out.at[0], turn_sems.at[0], back=True)
    left_first = load(att_ref if small else two_ref, left, 16)
    rights = [load_right(0), load_right(1)]
    at.meet(at.other(y=1 - at.y, k=1 - at.k))
    across = at.other(k=1 - at.k)
    beside = at.other(x=1 - at.x)
    over = at.other(y=1 - at.y)
    ahead = [(at.z + step) % 4 for step in (1, 2, 3)]
    sent = []

    def send(flow, which, source, target, device):
        copy = pltpu.make_async_remote_copy(
            src_ref=source,
            dst_ref=target,
            send_sem=send_sems.at[flow, which],
            recv_sem=recv_sems.at[flow, which],
            device_id=device,
            device_id_type=MESH,
        )
        copy.start()
        sent.append(copy)
        return copy

    flights = {}

    def small_zero():
        flights[4, 0] = send(4, 0, totals_ref.at[1 - at.k], t_core, across)
        flights[5, 0] = send(5, 0, mod_ref.at[1 - at.k], e_core.at[at.k], across)

    def small_one():
        flights[4, 0].wait_recv()
        for y in range(2):
            t_core[y] = t_core[y] + totals_ref[at.k, y]
        flights[4, 1] = send(4, 1, t_core, t_x, beside)
        flights[5, 0].wait_recv()
        for y in range(2):
            e_core[at.k, y] = mod_ref[at.k, y]
        flights[5, 1] = send(5, 1, e_core.at[:, 1 - at.y], e_y.at[at.y], over)

    def small_two():
        flights[4, 1].wait_recv()
        for y in range(2):
            t_z[at.z, y] = t_x[y] + t_core[y]
        flights[4, 2] = [
            send(4, 2 + index, t_z.at[at.z], t_z.at[at.z], at.other(z=z))
            for index, z in enumerate(ahead)
        ]
        flights[5, 1].wait_recv()
        for k in range(2):
            e_y[at.y, k] = e_core[k, at.y]
        flights[5, 2] = send(5, 2, e_y, e_x.at[at.x], beside)

    def small_three():
        for copy in flights[4, 2]:
            copy.wait_recv()
        for y in range(2):
            t_sum[y] = (t_z[0, y] + t_z[1, y]) + (t_z[2, y] + t_z[3, y])
        flights[4, 3] = send(4, 5, t_sum.at[1 - at.y], t_y, over)
        flights[5, 2].wait_recv()
        for y in range(2):
            for k in range(2):
                e_x[at.x, y, k] = e_y[y, k]
        mod_out[at.z] = e_x[...]
        flights[5, 3] = [
            send(5, 3 + index, e_x, mod_out.at[at.z], at.other(z=z))
            for index, z in enumerate(ahead)
        ]

    def small_four():
        flights[4, 3].wait_recv()
        totals_out[...] = t_sum[at.y] + t_y[...]
        for copy in flights[5, 3]:
            copy.wait_recv()

    soft_flights = []

    def soft_send(source, target, device):
        used = len(soft_flights)
        copy = pltpu.make_async_remote_copy(
            src_ref=source,
            dst_ref=target,
            send_sem=soft_sems.at[0, used],
            recv_sem=soft_sems.at[1, used],
            device_id=device,
            device_id_type=MESH,
        )
        copy.start()
        sent.append(copy)
        soft_flights.append(copy)

    def soft_one():
        share = jnp.zeros((128, 128), jnp.float32)
        for part in range(6):
            rows = []
            for r in range(8):
                for c in range(4):
                    rows.append(mod_out[r // 2, r % 2, c // 2, c % 2, part * 4 : part * 4 + 4])
            share = share + nt(jnp.concatenate(rows, axis=0), ada_ref[part])
        for r in range(8):
            g_own[r // 2, r % 2] = share[r * 16 : (r + 1) * 16]
        for z in ahead:
            soft_send(g_own.at[z], g_z.at[at.z], at.other(z=z))
        for x in range(2):
            g_z[at.z, x] = g_own[at.z, x]

    def soft_two():
        for copy in soft_flights[:3]:
            copy.wait_recv()
        for z in range(4):
            g_x[at.x, z] = g_z[z, at.x]
        soft_send(g_z.at[pl.ds(0, 4), 1 - at.x], g_x.at[at.x], beside)

    def soft_three():
        soft_flights[3].wait_recv()
        for z in range(4):
            for x in range(2):
                g_turn[z // 2, z % 2, x] = g_x[x, z]
        soft_send(g_turn.at[1 - at.y], g_y, over)

    def soft_four():
        soft_flights[4].wait_recv()
        for k in range(2):
            for x in range(2):
                g_sum[k, x] = g_turn[at.y, k, x] + g_y[k, x]
        soft_send(g_sum.at[1 - at.k], g_k, across)

    def soft_five():
        soft_flights[5].wait_recv()
        for x in range(2):
            soft_out[x] = g_sum[at.k, x] + g_k[x]

    def compute(p):
        for c in range(4):
            span = slice(c * 256, (c + 1) * 256)
            value = nn(turned[...], right[p % 2, :, span]).astype(jnp.bfloat16)
            for r in range(8):
                z, x, y = r // 2, r % 2, c // 2
                where = (x, z, y) if small else ((x, y, z), (y, x, z))[p % 2]
                mine[(p, c % 2) + where] = value[r * 128 : (r + 1) * 128]
        flights[p, 0] = send(p, 0, mine.at[p, 1 - at.k], core_in.at[p], across)

    def core_done(p):
        flights[p, 0].wait_recv()
        for one in range(mine.shape[2]):
            for two in range(mine.shape[3]):
                add_into(
                    after_core.at[p, one, two],
                    mine.at[p, at.k, one, two],
                    core_in.at[p, one, two],
                )

    def x_start(p):
        flights[p, 1] = send(p, 1, after_core.at[p, 1 - at.x], x_in.at[p], beside)

    def x_done(p):
        flights[p, 1].wait_recv()
        for z in range(4):
            add_into(after_x.at[p, z], after_core.at[p, at.x, z], x_in.at[p, z])
        flights[p, 2] = [
            send(p, 2 + index, after_x.at[p, z], z_in.at[p, index], at.other(z=z))
            for index, z in enumerate(ahead)
        ]

    def z_done(p):
        for copy in flights[p, 2]:
            copy.wait_recv()
        for y in range(2):
            value = after_x[p, at.z, y].astype(jnp.float32)
            for index in range(3):
                value = value + z_in[p, index, y].astype(jnp.float32)
            summed[p, y] = value
        y_send[p] = summed[p, 1 - at.y].astype(jnp.bfloat16)
        flights[p, 3] = send(p, 5, y_send.at[p], y_in.at[p], over)

    def y_done(p):
        flights[p, 3].wait_recv()
        out_ref[p] = summed[p, at.y] + y_in[p].astype(jnp.float32)

    def axes(p):
        return ((at.x, beside), (at.y, over))[:: 1 if p % 2 == 0 else -1]

    def first_start(p):
        place, partner = axes(p)[0]
        flights[p, 1] = send(p, 1, after_core.at[p, 1 - place], x_in.at[p], partner)

    def first_done(p):
        flights[p, 1].wait_recv()
        for index in range(2):
            add_into(after_x.at[p, index], after_core.at[p, axes(p)[0][0], index], x_in.at[p, index])
        place, partner = axes(p)[1]
        flights[p, 2] = send(p, 2, after_x.at[p, 1 - place], y_in.at[p], partner)

    def second_done(p):
        flights[p, 2].wait_recv()
        add_into(y_send.at[p], after_x.at[p, axes(p)[1][0]], y_in.at[p])
        flights[p, 3] = [
            send(p, 3 + index, y_send.at[p, z], z_in.at[p, index], at.other(z=z))
            for index, z in enumerate(ahead)
        ]

    def third_done(p):
        for copy in flights[p, 3]:
            copy.wait_recv()
        value = y_send[p, at.z].astype(jnp.float32)
        for index in range(3):
            value = value + z_in[p, index].astype(jnp.float32)
        out_ref[p] = value

    arrivals = []

    def tokens_from(c, index):
        length = tok_ref.shape[1] // 4
        here = pl.ds(index * length, length)
        there = pl.ds(pl.multiple_of((at.y * 2 + at.k) * tok_ref.shape[1] + index * length, 8), length)
        return tok_ref.at[c, here], tok_in.at[there]

    def tokens_over(index):
        for step, k in enumerate((at.k, 1 - at.k)):
            source, target = tokens_from((1 - at.y) * 2 + k, index)
            copy = pltpu.make_async_remote_copy(
                src_ref=source,
                dst_ref=target,
                send_sem=more_sems.at[0, 2 * index + step],
                recv_sem=more_sems.at[1, 2 * index + step],
                device_id=at.other(y=1 - at.y, k=k),
                device_id_type=MESH,
            )
            copy.start()
            arrivals.append(copy)
            sent.append(copy)

    def tokens_across():
        count = tok_ref.shape[1]
        copy = pltpu.make_async_remote_copy(
            src_ref=tok_ref.at[at.y * 2 + 1 - at.k],
            dst_ref=tok_in.at[pl.ds(pl.multiple_of((at.y * 2 + at.k) * count, 8), count)],
            send_sem=more_sems.at[0, 8],
            recv_sem=more_sems.at[1, 8],
            device_id=across,
            device_id_type=MESH,
        )
        copy.start()
        sent.append(copy)
        return copy

    def own_tokens():
        count = tok_ref.shape[1]
        held = left.at[:, pl.ds(0, tok_ref.shape[2])]
        load(tok_ref.at[at.y * 2 + at.k], held, 18).wait()
        place = pl.ds(pl.multiple_of((at.y * 2 + at.k) * count, 8), count)
        load(held, tok_in.at[place], 19).wait()

    def right_ready(p):
        for copy in rights[p]:
            copy.wait()

    writes = []

    def plain(c):
        right_ready(4 + c)
        if c >= 2:
            writes[c - 2].wait()
        for part in range(4):
            span = slice(part * 256, (part + 1) * 256)
            value = nn(turned[...], right[c % 2, :, span]).astype(jnp.bfloat16)
            for r in range(8):
                stage[c % 2, r, :, span] = value[r * 128 : (r + 1) * 128]
        copy = pltpu.make_async_copy(stage.at[c % 2], wide_ref.at[:, c], stage_sems.at[c % 2])
        copy.start()
        writes.append(copy)
        if c < 2:
            rights.append(load_right(6 + c))

    left_first.wait()
    if small:
        small_zero()
        from_across = tokens_across()
        tokens_over(0)
        turn_rows(left, turned)
        left_second = load(ln_ref, left, 17)
        right_ready(0)
        compute(0)
        rights.append(load_right(2))
        small_one()
        tokens_over(1)
        core_done(0)
        x_start(0)
        layer.run(4)
        left_second.wait()
        turn_rows(left, turned)
        right_ready(1)
        compute(1)
        rights.append(load_right(3))
        core_done(1)
        small_two()
        x_done(0)
        x_start(1)
        tokens_over(2)
        layer.run(4)
        own_tokens()
        from_across.wait_recv()
        right_ready(2)
        compute(2)
        core_done(2)
        small_three()
        x_done(1)
        x_start(2)
        tokens_over(3)
        z_done(0)
        right_ready(3)
        compute(3)
        core_done(3)
        small_four()
        soft_one()
        x_done(2)
        x_start(3)
        layer.run(5)
        soft_two()
        layer.run(4)
        soft_three()
        half = layer.total // 2
        turned_tokens = Turner(
            tok_in, tok_out, turn_in.at[1], turn_out.at[1], turn_sems.at[1],
            back=True, shift=at.y * (half + 1), ahead=half,
        )
        z_done(1)
        y_done(0)
        turned_tokens.run(half)
        soft_four()
        z_done(2)
        y_done(1)
        for copy in arrivals:
            copy.wait_recv()
        turned_tokens.release()
        soft_five()
        x_done(3)
        turned_tokens.finish()
        layer.finish()
        y_done(2)
        z_done(3)
        y_done(3)
    else:
        turn_rows(left, turned)
        left_second = load(two_left_ref, left, 17)
        right_ready(0)
        compute(0)
        rights.append(load_right(2))
        core_done(0)
        first_start(0)
        right_ready(1)
        compute(1)
        rights.append(load_right(3))
        core_done(1)
        first_start(1)
        right_ready(2)
        compute(2)
        rights.append(load_right(4))
        core_done(2)
        first_done(0)
        first_start(2)
        first_done(1)
        right_ready(3)
        compute(3)
        rights.append(load_right(5))
        core_done(3)
        first_start(3)
        left_second.wait()
        turn_rows(left, turned)
        second_done(0)
        second_done(1)
        plain(0)
        first_done(2)
        third_done(0)
        plain(1)
        third_done(1)
        first_done(3)
        second_done(2)
        plain(2)
        second_done(3)
        third_done(2)
        plain(3)
        third_done(3)
        writes[2].wait()
        writes[3].wait()
    for copy in sent:
        copy.wait_send()


def grads_everywhere(count, width, tensors, pieces=None, layer=None, totals=None, d_mod=None, w_ada=None):
    f32, bf16 = jnp.float32, jnp.bfloat16
    small = totals is not None
    anywhere = pl.BlockSpec(memory_space=pl.ANY)
    inside = pl.BlockSpec(memory_space=pltpu.VMEM)
    tile = (128, 256)
    cube = (2, 4, 2) if small else (2, 2, 4)
    vmem = pltpu.VMEM
    outs = [jax.ShapeDtypeStruct((4,) + tile, f32)]
    flows = [vmem((2, 8, 128, width), bf16), pltpu.SemaphoreType.DMA((2,))]
    if not small:
        outs += [jax.ShapeDtypeStruct((8, 4, 128, width), bf16)]
    else:
        vec, mod = totals.shape[2:], d_mod.shape[2:]
        outs += [
            jax.ShapeDtypeStruct(vec, f32),
            jax.ShapeDtypeStruct((4, 2, 2, 2) + mod, bf16),
            jax.ShapeDtypeStruct((2, 16, 128), f32),
            jax.ShapeDtypeStruct(layer.shape, bf16),
            jax.ShapeDtypeStruct(layer.shape[::-1], bf16),
            jax.ShapeDtypeStruct(layer.shape[::-1], bf16),
        ]
        flows = [
            vmem((4, 2, 16, 128), f32),
            vmem((4, 2, 16, 128), f32),
            vmem((2, 4, 16, 128), f32),
            vmem((2, 2, 2, 16, 128), f32),
            vmem((2, 2, 16, 128), f32),
            vmem((2, 2, 16, 128), f32),
            vmem((2, 16, 128), f32),
            pltpu.SemaphoreType.DMA((2, 6)),
            vmem((2,) + vec, f32),
            vmem((2,) + vec, f32),
            vmem((4, 2) + vec, f32),
            vmem(vec, f32),
            vmem((2,) + vec, f32),
            vmem((2, 2) + mod, bf16),
            vmem((2, 2) + mod, bf16),
            vmem((2, 2, 2) + mod, bf16),
            vmem((2, 2, TURN, layer.shape[1]), bf16),
            vmem((2, 2, layer.shape[1], TURN), bf16),
            pltpu.SemaphoreType.DMA((2, 4)),
            pltpu.SemaphoreType.DMA((2, 9)),
        ]
    return pl.pallas_call(
        functools.partial(grad_kernel, small),
        in_specs=[anywhere] * (len(tensors) + 2 * small) + [inside] * (3 * small),
        out_specs=[inside] * (4 if small else 1) + [anywhere] * (3 if small else 1),
        out_shape=outs,
        scratch_shapes=flows
        + [
            vmem((count, width), bf16),
            vmem((width, count), bf16),
            vmem((2, count, width), bf16),
            vmem((4, 2) + cube + tile, bf16),
            vmem((4,) + cube + tile, bf16),
            vmem((4,) + cube + tile, bf16),
            vmem((4,) + cube[1:] + tile, bf16),
            vmem((4,) + cube[1:] + tile, bf16),
            vmem((4, 3) + ((2,) if small else ()) + tile, bf16),
            vmem((4, 2 if small else 1) + tile, f32),
            vmem((4,) + (() if small else (4,)) + tile, bf16),
            vmem((4,) + (() if small else (4,)) + tile, bf16),
            pltpu.SemaphoreType.DMA((24,)),
            pltpu.SemaphoreType.DMA((6, 6)),
            pltpu.SemaphoreType.DMA((6, 6)),
        ],
        compiler_params=pltpu.CompilerParams(
            vmem_limit_bytes=62 << 20, collective_id=1 if small else 3, has_side_effects=True
        ),
        cost_estimate=pl.CostEstimate(
            flops=16 * count * width * width,
            bytes_accessed=count * width * 12 + width * width * 8,
            transcendentals=0,
        ),
        name="attn_grads" if small else "second_grads",
    )(*tensors, *((pieces, layer, totals, d_mod, w_ada) if small else ()))


START_COPIES = 41


def start_kernel(
    tok_ref, shard_ref, grad_ref, soft_ref, vec_ref, ada_ref, bias_ref,
    tok_out, parts_out, grad_out, tok_turned, mod_out, vec_out, soft_out,
    s_col, x_send, x_rows, rows_in, partial, p_in, q_sum, z_in, y_send, n_y, k_send,
    t_in, t_out, g_in, g_out, held,
    send_sems, recv_sems, local_sems, t_sems, g_sems,
):
    at = Place()
    mine = at.y * 2 + at.k
    turning = Turner(grad_ref, grad_out, g_in, g_out, g_sems)
    count = tok_turned.shape[0] // 4

    def piece(c, start, size):
        return tok_turned.at[pl.ds(pl.multiple_of(c * count + start, 8), size)]

    own_load = pltpu.make_async_copy(piece(mine, 0, count), held.at[0], local_sems.at[0])
    own_tokens = pltpu.make_async_copy(held.at[0], tok_out.at[mine], local_sems.at[2])
    side_load = pltpu.make_async_copy(
        piece(at.y * 2 + 1 - at.k, 0, count), held.at[1], local_sems.at[3]
    )
    own_shard = pltpu.make_async_copy(
        shard_ref, parts_out.at[at.z, at.x, at.y, at.k], local_sems.at[1]
    )
    own_shard.start()
    first = Turner(
        tok_ref, tok_turned, t_in, t_out, t_sems, shift=(1 - at.y) * (tok_ref.shape[1] // TURN // 2)
    )
    at.meet(at.other(y=1 - at.y, k=1 - at.k))
    across = at.other(k=1 - at.k)
    beside = at.other(x=1 - at.x)
    over = at.other(y=1 - at.y)
    ahead = [(at.z + step) % 4 for step in (1, 2, 3)]
    send = Sender(send_sems, recv_sems)
    length = count // 4
    arrivals = []

    def tokens_over(index):
        span = pl.ds(index * length, length)
        for k in (at.k, 1 - at.k):
            source = piece((1 - at.y) * 2 + k, index * length, length)
            arrivals.append(send(source, tok_out.at[mine, span], at.other(y=1 - at.y, k=k)))

    zs, xs, ys = pl.ds(0, 4), pl.ds(0, 2), pl.ds(0, 2)

    def forward(block, device):
        return send(parts_out.at[block], parts_out.at[block], device)

    def to_ahead(s):
        return [forward((at.z, at.x, ys, at.k, s), at.other(z=z)) for z in ahead]

    def all_in(copies):
        for copy in copies:
            copy.wait_recv()

    shard_y = [
        send(shard_ref.at[s], parts_out.at[at.z, at.x, at.y, at.k, s], over) for s in range(3)
    ]
    s_col[at.y, at.k] = soft_ref[...]
    vec_out[at.y, at.k] = vec_ref[...]
    soft_k = send(soft_ref, s_col.at[at.y, at.k], across)
    vec_k = send(vec_ref, vec_out.at[at.y, at.k], across)
    first.run(9)
    first.settle()
    tokens_over(0)
    soft_k.wait_recv()
    vec_k.wait_recv()
    soft_y = send(s_col.at[at.y], s_col.at[at.y], over)
    vec_y = send(vec_out.at[at.y], vec_out.at[at.y], over)
    own_shard.wait()
    all_in(shard_y)
    shard_z, shard_x, shard_k = [to_ahead(0)], [], []

    def next_x(s):
        all_in(shard_z[s])
        shard_x.append(forward((zs, at.x, ys, at.k, s), beside))
        if s < 2:
            shard_z.append(to_ahead(s + 1))

    def next_k(s):
        shard_x[s].wait_recv()
        shard_k.append(forward((zs, xs, ys, at.k, s), across))

    first.finish()
    own_load.start()
    side_load.start()
    own_load.wait()
    own_tokens.start()
    side_load.wait()
    arrivals.append(send(held.at[1], tok_out.at[mine], across))
    soft_y.wait_recv()
    vec_y.wait_recv()
    for z in range(4):
        x_send[z] = s_col[z // 2, z % 2, 1 - at.x]
        x_rows[at.x, z] = s_col[z // 2, z % 2, at.x]
    soft_x = send(x_send, x_rows.at[at.x], beside)
    tokens_over(1)
    turning.run(1)
    soft_x.wait_recv()
    for x in range(2):
        rows_in[at.z, x] = x_rows[x, at.z]
    soft_z = [send(x_rows.at[xs, z], rows_in.at[at.z], at.other(z=z)) for z in ahead]
    turning.run(2)
    all_in(soft_z)
    soft = jnp.concatenate([rows_in[r // 2, r % 2] for r in range(8)], axis=0)
    soft_out[...] = soft
    for part in range(6):
        value = nn(soft, ada_ref[part])
        for r in range(8):
            partial[r % 2, r // 2, part] = value[r * 16 : (r + 1) * 16]
    mod_x = send(partial.at[1 - at.x], p_in, beside)
    tokens_over(2)
    next_x(0)
    turning.run(2)
    mod_x.wait_recv()
    for z in range(4):
        for part in range(6):
            q_sum[z, part] = partial[at.x, z, part] + p_in[z, part]
    mod_z = [send(q_sum.at[z], z_in.at[at.z], at.other(z=z)) for z in ahead]
    for part in range(6):
        z_in[at.z, part] = q_sum[at.z, part]
    turning.run(3)
    next_x(1)
    all_in(mod_z)
    for part in range(6):
        value = (z_in[0, part] + z_in[1, part]) + (z_in[2, part] + z_in[3, part])
        value = value + bias_ref[part : part + 1]
        for y in range(2):
            y_send[y, part] = value[y * 8 : (y + 1) * 8]
    mod_y = send(y_send.at[1 - at.y], n_y.at[at.y], over)
    tokens_over(3)
    for part in range(6):
        n_y[at.y, part] = y_send[at.y, part]
    next_k(0)
    turning.run(2)
    next_x(2)
    mod_y.wait_recv()
    for y in range(2):
        for part in range(6):
            for k in range(2):
                k_send[k, y, part] = n_y[y, part, k * 4 : (k + 1) * 4]
    mod_k = send(k_send.at[1 - at.k], mod_out.at[at.k], across)
    for y in range(2):
        for part in range(6):
            mod_out[at.k, y, part] = k_send[at.k, y, part]
    next_k(1)
    turning.run(3)
    next_k(2)
    turning.finish()
    mod_k.wait_recv()
    all_in(arrivals)
    all_in(shard_k)
    own_tokens.wait()
    send.finish()


def start_everything(tokens, shard, grad, soft, vec, w_ada, b_ada):
    f32, bf16 = jnp.float32, jnp.bfloat16
    anywhere = pl.BlockSpec(memory_space=pl.ANY)
    inside = pl.BlockSpec(memory_space=pltpu.VMEM)
    six = (6, 16, 256)
    vmem = pltpu.VMEM
    return pl.pallas_call(
        start_kernel,
        in_specs=[anywhere, inside, anywhere] + [inside] * 4,
        out_specs=[anywhere, inside, anywhere, anywhere] + [inside] * 3,
        out_shape=[
            jax.ShapeDtypeStruct((4, tokens.shape[1] // 4, tokens.shape[0]), bf16),
            jax.ShapeDtypeStruct((4, 2, 2, 2) + shard.shape, bf16),
            jax.ShapeDtypeStruct(grad.shape[::-1], bf16),
            jax.ShapeDtypeStruct(tokens.shape[::-1], bf16),
            jax.ShapeDtypeStruct((2, 2, 6, 4, 256), f32),
            jax.ShapeDtypeStruct((2, 2) + vec.shape, f32),
            jax.ShapeDtypeStruct((128, 128), bf16),
        ],
        scratch_shapes=[
            vmem((2, 2) + soft.shape, bf16),
            vmem((4, 16, 128), bf16),
            vmem((2, 4, 16, 128), bf16),
            vmem((4, 2, 16, 128), bf16),
            vmem((2, 4) + six, f32),
            vmem((4,) + six, f32),
            vmem((4,) + six, f32),
            vmem((4,) + six, f32),
            vmem((2, 6, 8, 256), f32),
            vmem((2, 6, 8, 256), f32),
            vmem((2, 2, 6, 4, 256), f32),
            vmem((2, tokens.shape[0], TURN), bf16),
            vmem((2, TURN, tokens.shape[0]), bf16),
            vmem((2, grad.shape[0], TURN), bf16),
            vmem((2, TURN, grad.shape[0]), bf16),
            vmem((2, tokens.shape[1] // 4, tokens.shape[0]), bf16),
            pltpu.SemaphoreType.DMA((START_COPIES,)),
            pltpu.SemaphoreType.DMA((START_COPIES,)),
            pltpu.SemaphoreType.DMA((4,)),
            pltpu.SemaphoreType.DMA((4,)),
            pltpu.SemaphoreType.DMA((4,)),
        ],
        compiler_params=pltpu.CompilerParams(
            vmem_limit_bytes=60 << 20, collective_id=2, has_side_effects=True
        ),
        cost_estimate=pl.CostEstimate(
            flops=100_000_000_000, bytes_accessed=30_000_000, transcendentals=0
        ),
        name="start_exchange",
    )(tokens, shard, grad, soft, vec, w_ada, b_ada)


def swap(pieces, axes):
    return lax.all_to_all(pieces, axes, split_axis=0, concat_axis=0, tiled=False)


def share(value, axes, count):
    return swap(jnp.broadcast_to(value[None], (count,) + value.shape), axes)


BOTH = ("row", "col")


def row_major(value):
    return with_layout_constraint(value, Layout(tuple(range(value.ndim))))


def after(value, *others):
    return lax.optimization_barrier((value,) + others)[0]


def shards(
    tokens,
    condition,
    scale_ids,
    attention_triple_matrix,
    attention_triple_offset,
    qk_gain,
    w_proj,
    b_proj,
    w_fc1,
    b_fc1,
    w_fc2,
    b_fc2,
    w_ada,
    b_ada,
    out_grad,
):
    rows = lax.axis_size("row")
    groups = lax.axis_size("col")
    row = lax.axis_index("row")
    place = lax.axis_index("col")
    everyone = rows * groups
    part = tokens.shape[0]
    width = part * groups
    images_row, length = scale_ids.shape
    images = images_row // groups
    count = images * length
    block = w_proj.shape[0]
    ff_part = b_fc1.shape[0]
    hidden_width = ff_part * groups
    aligned = part == 256 and (rows, groups) == (8, 4)
    blocks = (rows, groups) if aligned else (1, 1)
    f32, bf16 = jnp.float32, jnp.bfloat16

    rest_parts = lax.all_gather(
        row_major(jnp.concatenate([w_proj, w_fc1, w_fc2.T], axis=1)), BOTH
    )

    def whole(parts):
        parts = parts.reshape((rows, groups) + parts.shape[1:])
        return parts.transpose(0, 2, 1, 3).reshape(width, groups * parts.shape[-1])

    def spread(wide):
        cols = wide.shape[1] // groups
        pieces = wide.reshape(rows, block, groups, cols).transpose(0, 2, 1, 3)
        return pieces.reshape(everyone, block, cols)

    offsets = attention_triple_offset.astype(f32).reshape(-1)
    vector = jnp.concatenate(
        [offsets, b_proj.astype(f32), b_fc1.astype(f32), b_fc2.astype(f32), qk_gain]
    )
    ada_block = w_ada.shape[1]
    cond_float = condition.astype(f32)
    soft = jax.nn.silu(cond_float).astype(bf16)
    def to_tokens(features):
        pieces = swap(features.T.reshape(groups, count, part), "col")
        return pieces if aligned else pieces.transpose(1, 0, 2).reshape(1, count, width)

    def to_features(pieces):
        if not aligned:
            pieces = pieces[0].reshape(count, groups, part).transpose(1, 0, 2)
        return swap(pieces, "col").reshape(groups * count, part)

    if aligned:
        held = vector.shape[0]
        tok_in, qkv_parts, grad_in, _, modulation, small, soft_mine = start_everything(
            tokens,
            attention_triple_matrix.transpose(1, 0, 2),
            out_grad,
            soft.reshape(images_row, 2, ada_block).transpose(1, 0, 2),
            jnp.pad(vector, (0, -held % 1024)).reshape(-1, 128),
            w_ada,
            b_ada.astype(f32),
        )
        qkv_parts = qkv_parts.reshape(everyone, 3, block, part)
        modulation = modulation.transpose(3, 2, 1, 0, 4).reshape(images, 6, width)
        small = small.reshape(groups, -1)[:, :held]
        grad_in = swap(grad_in.reshape(groups, count, part), "col")
    else:
        qkv_parts = lax.all_gather(attention_triple_matrix.transpose(1, 0, 2), BOTH)
        qkv_parts = jnp.stack([whole(qkv_parts[:, index]) for index in range(3)])[None]
        cut = part + ff_part
        rest_parts = jnp.concatenate(
            [
                whole(rest_parts[:, :, :part]),
                whole(rest_parts[:, :, part:cut]),
                whole(rest_parts[:, :, cut:]),
            ],
            axis=1,
        )[None]

        small = share(vector, "col", groups)
        soft_all = (
            share(soft, BOTH, everyone)
            .reshape(rows, groups, images_row, part)
            .transpose(0, 2, 1, 3)
            .reshape(rows * images_row, width)
        )
        soft_mine = lax.dynamic_slice(
            soft_all, (0, row * ada_block), (rows * images_row, ada_block)
        )
        mod_part = jnp.einsum("ic,scd->isd", soft_mine, w_ada, preferred_element_type=f32)
        mod_part = mod_part + jnp.where(row == 0, b_ada.astype(f32), 0.0)[None]
        modulation = swap(mod_part.reshape(everyone, images, 6, part), BOTH)
        modulation = (
            modulation.reshape(rows, groups, images, 6, part)
            .sum(axis=0)
            .transpose(1, 2, 0, 3)
            .reshape(images, 6, width)
        )

        tok_in = to_tokens(tokens)
        grad_in = to_tokens(out_grad)
    cuts = [3 * part, 4 * part, 4 * part + ff_part, 5 * part + ff_part]
    bias_qkv = small[:, : cuts[0]].reshape(groups, 3, part).transpose(1, 0, 2).reshape(3, 1, width)
    bias_proj = small[:, cuts[0] : cuts[1]].reshape(1, width)
    bias_one = small[:, cuts[1] : cuts[2]].reshape(1, hidden_width)
    bias_two = small[:, cuts[2] : cuts[3]].reshape(1, width)
    gain_row = jnp.repeat(small[:, cuts[3] :].reshape(-1), HEAD_DIM)[None]

    scale_rows = lax.dynamic_slice(scale_ids, (place * images, 0), (images, length))
    query_lanes, key_lanes = mask_lanes(scale_rows)

    ln_one, qkv = qkv_forward(tok_in, modulation, bias_qkv, qkv_parts, blocks, length)
    qkv = qkv.reshape(3, images, length, width)
    attended, log_sums = attention_forward(qkv, gain_row, query_lanes, key_lanes)
    attn_rows = attended.reshape(count, width)
    (
        layer_pieces,
        ln_two,
        hidden,
        d_two,
        d_pre,
        d_one,
        d_res,
        d_attended,
        mod_sums,
        sum_bproj,
        sum_b1,
        sum_b2,
    ) = ffn(
        tok_in,
        attn_rows,
        grad_in,
        modulation,
        bias_proj,
        bias_one,
        bias_two,
        rest_parts,
        blocks,
        length,
    )
    if aligned:
        grad_fc2, wide_one = grads_everywhere(count, width, (d_two, hidden, ln_two, d_pre))
        grad_fc2 = grad_fc2.transpose(0, 2, 1).reshape(ff_part, block)
        wide_one = wide_one.reshape(everyone, block, ff_part)
        wide_one, d_attended, layer_pieces = lax.optimization_barrier(
            (wide_one, d_attended, layer_pieces)
        )
    else:
        wide_one = spread(plain_grads(ln_two, d_pre, blocks)[0, 0])
        wide_two = spread(plain_grads(d_two, hidden, blocks)[0, 0])
        wide_two = row_major(lax.psum_scatter(wide_two, BOTH, scatter_dimension=0, tiled=False))
        grad_fc2 = wide_two.astype(f32).T
    wide_one = row_major(lax.psum_scatter(wide_one, BOTH, scatter_dimension=0, tiled=False))
    grad_fc1 = wide_one.astype(f32)
    layer_out = to_features(layer_pieces)
    d_qkv, head_totals = attention_backward(
        qkv,
        gain_row,
        query_lanes,
        key_lanes,
        attended,
        log_sums,
        d_attended.reshape(images, length, width),
    )
    d_qkv, layer_out = lax.optimization_barrier((d_qkv, layer_out))
    d_qkv = d_qkv.reshape(3, count, width)
    token_pieces, first_sums = input_backward(
        d_qkv, tok_in, d_res, modulation, qkv_parts, blocks, length
    )

    head_totals = head_totals.sum(axis=0)
    totals = jnp.concatenate(
        [
            head_totals[:3].reshape(3, groups, part).transpose(1, 0, 2).reshape(groups, 3 * part),
            sum_bproj.reshape(groups, part),
            sum_b1.reshape(groups, ff_part),
            sum_b2.reshape(groups, part),
            head_totals[3].reshape(-1, HEAD_DIM).sum(axis=1).reshape(groups, -1),
        ],
        axis=1,
    )
    d_mod = jnp.concatenate([first_sums, mod_sums], axis=1).astype(bf16)
    d_mod = d_mod.reshape(images, 6, groups, part).transpose(2, 0, 1, 3)
    if aligned:
        held = totals.shape[1]
        totals = jnp.pad(totals, ((0, 0), (0, -held % 1024)))
        totals = totals.reshape(2, 2, -1, 128).transpose(1, 0, 2, 3)
        d_mod = d_mod.reshape(2, 2, images, 6, part).transpose(1, 0, 3, 2, 4)
        d_mod = d_mod.reshape(2, 2, 6 * images, part)
        wide_attn, totals, d_mod, d_soft, _, grad_tokens, layer_out = grads_everywhere(
            count,
            width,
            (attn_rows, d_one, ln_one, d_qkv),
            token_pieces,
            layer_out,
            totals,
            d_mod,
            w_ada,
        )
        totals = totals.reshape(-1)[:held]
        d_mod = d_mod.reshape(everyone, 6, images, part).transpose(0, 2, 1, 3)
        d_mod = d_mod.reshape(everyone * images, 6, part)
        grad_proj = wide_attn[0]
        grad_qkv = wide_attn[1:].transpose(1, 0, 2)
    else:
        grad_tokens = to_features(token_pieces).T
        layer_out = layer_out.T
        wide_attn = [
            jnp.einsum("td,tf->df", one, two, preferred_element_type=f32).astype(bf16)
            for one, two in [(attn_rows, d_one)] + [(ln_one, d_qkv[index]) for index in range(3)]
        ]
        wide_attn = jnp.concatenate([spread(wide) for wide in wide_attn], axis=2)
        wide_attn = row_major(lax.psum_scatter(wide_attn, BOTH, scatter_dimension=0, tiled=False))
        wide_attn = wide_attn.astype(f32)
        grad_proj = wide_attn[:, :part]
        grad_qkv = wide_attn[:, part:].reshape(block, 3, part)
        totals = jnp.broadcast_to(totals[None], (rows,) + totals.shape)
        totals = swap(totals.reshape(everyone, -1), BOTH).sum(axis=0)
        d_mod = jnp.broadcast_to(d_mod[None], (rows,) + d_mod.shape)
        d_mod = swap(d_mod.reshape((everyone,) + d_mod.shape[2:]), BOTH)
        d_mod = d_mod.reshape(everyone * images, 6, part)
    grad_ada = jnp.einsum("ic,isd->scd", soft_mine, d_mod, preferred_element_type=f32)
    grad_bada = jnp.sum(d_mod.astype(f32), axis=0)
    if aligned:
        d_soft = d_soft.transpose(1, 0, 2).reshape(images_row, part)
    else:
        d_soft = jnp.einsum("isd,scd->ic", d_mod, w_ada, preferred_element_type=f32)
        d_soft = d_soft.reshape(rows, 1, images_row, ada_block)
        d_soft = jnp.broadcast_to(d_soft, (rows, groups, images_row, ada_block))
        d_soft = swap(d_soft.reshape(everyone, images_row, ada_block), BOTH)
        d_soft = d_soft.reshape(rows, groups, images_row, ada_block).sum(axis=1)
        d_soft = d_soft.transpose(1, 0, 2).reshape(images_row, width)
        d_soft = lax.dynamic_slice(d_soft, (0, place * part), (images_row, part))
    _, silu_pull = jax.vjp(jax.nn.silu, cond_float)
    grad_condition = silu_pull(d_soft)[0].astype(bf16)
    return (
        layer_out,
        grad_tokens,
        grad_condition,
        grad_qkv,
        totals[: cuts[0]].reshape(3, part),
        totals[cuts[3] :],
        grad_proj,
        totals[cuts[0] : cuts[1]],
        grad_fc1,
        totals[cuts[1] : cuts[2]],
        grad_fc2,
        totals[cuts[2] : cuts[3]],
        grad_ada,
        grad_bada,
    )


def solution(mesh):
    placed = (
        P("col", "row"),
        P("row", "col"),
        P("row", None),
        P("row", None, "col"),
        P(None, "col"),
        P("col"),
        P("row", "col"),
        P("col"),
        P("row", "col"),
        P("col"),
        P("col", "row"),
        P("col"),
        P(None, "row", "col"),
        P(None, "col"),
        P("col", "row"),
    )
    return jax.shard_map(
        shards,
        mesh=mesh,
        in_specs=placed,
        out_specs=(
            P("col", "row"),
            P("col", "row"),
            P("row", "col"),
            P("row", None, "col"),
            P(None, "col"),
            P("col"),
            P("row", "col"),
            P("col"),
            P("row", "col"),
            P("col"),
            P("col", "row"),
            P("col"),
            P(None, "row", "col"),
            P(None, "col"),
        ),
        check_vma=False,
    )
```
